32 devices in a mesh: row: 8 (over y, x, core), col: 4 (over z).
Axes of the slice: x: 2, y: 2, z: 4, core: 2. Of those that a mesh axis runs over, the one named last changes fastest.
Arguments:
- hidden_in: bfloat16 [16384, 1024], P('row', 'col'), may hold values from -6 to 6
- query_weight: bfloat16 [1024, 1024], P('row', 'col'), may hold values from -0.1875 to 0.1875
- key_weight: bfloat16 [1024, 1024], P('row', 'col'), may hold values from -0.1875 to 0.1875
- value_weight: bfloat16 [1024, 1024], P('row', 'col'), may hold values from -0.1875 to 0.1875
- query_bias: float32 [1024], P('col'), may hold values from -3 to 3
- value_bias: float32 [1024], P('col'), may hold values from -3 to 3
- proj_weight: bfloat16 [1024, 1024], P('col', 'row'), may hold values from -1 to 1
- proj_bias: float32 [1024], P('col'), may hold values from -3 to 3
- attn_gain: float32 [1024], P('col'), may hold values from 0.25 to 1.75
- attn_shift: float32 [1024], P('col'), may hold values from -3 to 3
- inner_weight: bfloat16 [1024, 4096], P('row', 'col'), may hold values from -0.1875 to 0.1875
- inner_bias: float32 [4096], P('col'), may hold values from -3 to 3
- outer_weight: bfloat16 [4096, 1024], P('col', 'row'), may hold values from -0.09375 to 0.09375
- outer_bias: float32 [1024], P('col'), may hold values from -3 to 3
- ffn_gain: float32 [1024], P('col'), may hold values from 0.25 to 1.75
- ffn_shift: float32 [1024], P('col'), may hold values from -3 to 3
- segment_ids: int32 [8, 2048], P('row'), may hold values from 0 to 15, never falling along the last dimension, each value on 1 to 1024 neighbouring positions
- grad_out: bfloat16 [16384, 1024], P('row', 'col'), may hold values from -6 to 6
Outputs:
- hidden_out: float32 [16384, 1024], P('row', 'col')
- grad_in: float32 [16384, 1024], P('row', 'col')
- grad_query_weight: float32 [1024, 1024], P('row', 'col')
- grad_key_weight: float32 [1024, 1024], P('row', 'col')
- grad_value_weight: float32 [1024, 1024], P('row', 'col')
- grad_query_bias: float32 [1024], P('col')
- grad_value_bias: float32 [1024], P('col')
- grad_proj_weight: float32 [1024, 1024], P('col', 'row')
- grad_proj_bias: float32 [1024], P('col')
- grad_attn_gain: float32 [1024], P('col')
- grad_attn_shift: float32 [1024], P('col')
- grad_inner_weight: float32 [1024, 4096], P('row', 'col')
- grad_inner_bias: float32 [4096], P('col')
- grad_outer_weight: float32 [4096, 1024], P('col', 'row')
- grad_outer_bias: float32 [1024], P('col')
- grad_ffn_gain: float32 [1024], P('col')
- grad_ffn_shift: float32 [1024], P('col')
The draws below stay inside these ranges and needn't reach their ends.
Inputs may be any that keep to these rules, and one draw needn't show every extreme that they name: `segment_ids`: each row is one packed sequence of 2048 tokens: the numbers never fall along it, every number from 0 to 15 appears, each document has 1 to 1024 tokens and one has exactly 1024.
All inputs are finite; a program needn't handle non-finite values.
Results may differ from the reference program's by a relative error of at most 0.035.
Values may be sent and summed in bfloat16 or wider, within the bound.
A program may use at most 256 MiB of HBM per device.

```python
import math
import jax
import jax.numpy as jnp
import numpy as np
from jax import lax

D = 1024
HEADS = 16
HEAD_DIM = 64
FF = 4096
LEN = 2048
DOCS = 16
DOC_MOST = 1024
NSEQ = 8
TOKENS = 16384


def levels(stream_key, shape, shards, smallest, top_value):
    loudness = 1.0
    for position, parts in shards:
        steps = jax.random.uniform(jax.random.fold_in(jax.random.fold_in(stream_key, 6), position), (parts,), jnp.float32, smallest / len(shards), top_value / len(shards))
        loudness = loudness * jnp.repeat(jnp.exp(steps), shape[position] // parts).reshape((-1,) + (1,) * (len(shape) - 1 - position))
    return loudness


def length_profile(number_of, total, limit, skew):
    portions = [(1 << 20) // math.isqrt(grade ** skew) + 1 for grade in range(2, number_of + 1)]
    spare, counts = total - limit - (number_of - 1), [1] * (number_of - 1)
    while spare > 0:
        candidates = [i for i in range(number_of - 1) if counts[i] < limit]
        whole, budget = sum([portions[i] for i in candidates]), spare
        for i in candidates:
            addition = min(limit - counts[i], max(1, budget * portions[i] // whole), spare)
            counts[i] = counts[i] + addition
            spare = spare - addition
    return np.array([limit] + counts)


def uneven(rng, count, total, limit, lean):
    if count == 2:
        one = jax.random.randint(rng, (), max(1, total - limit), min(limit, total - 1) + 1)
        return jnp.stack([one, total - one])
    tallies = jnp.asarray(length_profile(count, total, limit, lean), jnp.int32)
    couples = (count - 1) // 2
    giver, sink = tallies[1:1 + 2 * couples:2], tallies[2:2 + 2 * couples:2]
    slack = jnp.minimum(giver - 1, limit - sink)
    passed = jax.random.randint(jax.random.fold_in(rng, 1), (couples,), 0, 1 << 20) % (slack + 1)
    tallies = tallies.at[1:1 + 2 * couples:2].set(giver - passed).at[2:2 + 2 * couples:2].set(sink + passed)
    return tallies[jax.random.permutation(jax.random.fold_in(rng, 2), count)]


def noise(stream_key, shape, scale, reach, cuts=(), dtype=jnp.bfloat16):
    result = jax.random.normal(stream_key, shape, jnp.float32) * scale
    if len(cuts) > 0:
        result = levels(stream_key, shape, cuts, -0.22, 0.18) * result
    return jnp.clip(result, min=-reach, max=reach).astype(dtype)


def setup_inputs(seed: int = 0) -> dict:
    streams_of = jax.random.split(jax.random.key(seed), 19)
    return {
        "hidden_in": noise(streams_of[0], (TOKENS, D), 1.0, 6.0, ((0, 8), (1, 4))),
        "query_weight": noise(streams_of[1], (D, D), D ** -0.5, 0.1875, ((0, 8), (1, 4))),
        "key_weight": noise(streams_of[2], (D, D), D ** -0.5, 0.1875, ((0, 8), (1, 4))),
        "value_weight": noise(streams_of[3], (D, D), D ** -0.5, 0.1875, ((0, 8), (1, 4))),
        "query_bias": noise(streams_of[4], (D,), 0.5, 3.0, ((0, 4),), jnp.float32),
        "value_bias": noise(streams_of[5], (D,), 0.5, 3.0, ((0, 4),), jnp.float32),
        "proj_weight": noise(streams_of[6], (D, D), (D // 32) ** -0.5, 1.0, ((0, 4), (1, 8))),
        "proj_bias": noise(streams_of[7], (D,), 0.5, 3.0, ((0, 4),), jnp.float32),
        "attn_gain": jnp.clip(1.0 + 0.15 * jax.random.normal(streams_of[8], (D,), jnp.float32), 0.25, 1.75),
        "attn_shift": noise(streams_of[9], (D,), 0.5, 3.0, ((0, 4),), jnp.float32),
        "inner_weight": noise(streams_of[10], (D, FF), D ** -0.5, 0.1875, ((0, 8), (1, 4))),
        "inner_bias": noise(streams_of[11], (FF,), 0.5, 3.0, ((0, 4),), jnp.float32),
        "outer_weight": noise(streams_of[12], (FF, D), FF ** -0.5, 0.09375, ((0, 4), (1, 8))),
        "outer_bias": noise(streams_of[13], (D,), 0.5, 3.0, ((0, 4),), jnp.float32),
        "ffn_gain": jnp.clip(1.0 + 0.15 * jax.random.normal(streams_of[14], (D,), jnp.float32), 0.25, 1.75),
        "ffn_shift": noise(streams_of[15], (D,), 0.5, 3.0, ((0, 4),), jnp.float32),
        "segment_ids": jax.vmap(lambda own: jnp.searchsorted(jnp.cumsum(uneven(own, DOCS, LEN, DOC_MOST, 2)), jnp.arange(LEN), side="right"))(jax.random.split(streams_of[16], NSEQ)).reshape((NSEQ, LEN)).astype(jnp.int32),
        "grad_out": noise(streams_of[17], (TOKENS, D), 1.0, 6.0, ((0, 8), (1, 4))),
    }


EPSILON = 1e-06
NEG_FILL = -1e+30
HIGHEST = lax.Precision.HIGHEST

@jax.custom_vjp
def low(v):
    return lax.optimization_barrier(v.astype(jnp.bfloat16)).astype(jnp.float32)

@jax.custom_vjp
def low_back(v):
    return v

def low_keep(v):
    return (low(v), None)

def low_pass(kept, grad):
    return (grad,)

def back_keep(v):
    return (v, None)

def back_low(kept, grad):
    return (low(grad),)
low.defvjp(low_keep, low_pass)
low_back.defvjp(back_keep, back_low)

def matmul(left, right):
    return jnp.dot(left, right, precision=HIGHEST, preferred_element_type=jnp.float32)

def layer_norm(summed, norm_gain, norm_shift):
    center = lax.optimization_barrier(jnp.mean(summed, axis=-1, keepdims=True))
    spread = lax.optimization_barrier(jnp.mean(summed * summed, axis=-1, keepdims=True)) - center * center
    return (summed - center) * lax.rsqrt(spread + EPSILON) * norm_gain + norm_shift

def attend_one(pieces):
    queries, key_rows, value_rows, segments = pieces
    product = jnp.einsum('qhd,khd->hqk', queries, key_rows, precision=HIGHEST)
    scores = low_back(product * HEAD_DIM ** (-0.5))
    same_doc = segments[:, None] == segments[None, :]
    scores = jnp.where(same_doc[None], scores, NEG_FILL)
    highest = lax.optimization_barrier(jnp.max(scores, axis=-1, keepdims=True))
    weights = jnp.exp(scores - highest)
    probs = low(weights / lax.optimization_barrier(jnp.sum(weights, axis=-1, keepdims=True)))
    return jnp.einsum('hqk,khd->qhd', probs, value_rows, precision=HIGHEST)

def encoder_layer(hidden, params, segments):
    query_weight, key_weight, value_weight, query_bias, value_bias, proj_weight, proj_bias, attn_gain, attn_shift, inner_weight, inner_bias, outer_weight, outer_bias, ffn_gain, ffn_shift = params
    group_count = hidden.shape[0] // LEN
    whole_in = low(hidden)
    queries = low(low_back(matmul(whole_in, query_weight) + query_bias))
    key_rows = low(low_back(matmul(whole_in, key_weight)))
    value_rows = low(low_back(matmul(whole_in, value_weight) + value_bias))
    head_shape = (group_count, LEN, HEADS, HEAD_DIM)
    attended = lax.map(jax.checkpoint(attend_one), (queries.reshape(head_shape), key_rows.reshape(head_shape), value_rows.reshape(head_shape), segments))
    attended = low(low_back(attended.reshape(hidden.shape)))
    attn_branch = low_back(matmul(attended, proj_weight) + proj_bias)
    first_norm = layer_norm(hidden + attn_branch, attn_gain, attn_shift)
    inner_act = low_back(matmul(low(first_norm), inner_weight) + inner_bias)
    active = low(jax.nn.gelu(inner_act, approximate=False))
    ffn_branch = low_back(matmul(active, outer_weight) + outer_bias)
    return layer_norm(first_norm + ffn_branch, ffn_gain, ffn_shift)

def reference(hidden_in, query_weight, key_weight, value_weight, query_bias, value_bias, proj_weight, proj_bias, attn_gain, attn_shift, inner_weight, inner_bias, outer_weight, outer_bias, ffn_gain, ffn_shift, segment_ids, grad_out):
    params = (query_weight.astype(jnp.float32), key_weight.astype(jnp.float32), value_weight.astype(jnp.float32), query_bias.astype(jnp.float32), value_bias.astype(jnp.float32), proj_weight.astype(jnp.float32), proj_bias.astype(jnp.float32), attn_gain.astype(jnp.float32), attn_shift.astype(jnp.float32), inner_weight.astype(jnp.float32), inner_bias.astype(jnp.float32), outer_weight.astype(jnp.float32), outer_bias.astype(jnp.float32), ffn_gain.astype(jnp.float32), ffn_shift.astype(jnp.float32))
    group_size = math.gcd(NSEQ, max(1, 4096 // LEN))
    group_total = NSEQ // group_size
    inputs = hidden_in.astype(jnp.float32).reshape(group_total, group_size * LEN, D)
    cotangents = grad_out.astype(jnp.float32).reshape(group_total, group_size * LEN, D)
    segments = segment_ids.reshape(group_total, group_size, LEN)

    def one_group(totals, pieces):
        block_in, block_segments, block_cotangent = pieces

        def forward(start_in, weights):
            return encoder_layer(encoder_layer(start_in, weights, block_segments), weights, block_segments)
        output, pullback = jax.vjp(forward, block_in, params)
        grad_start, grad_weights = pullback(block_cotangent)
        return (jax.tree.map(jnp.add, totals, grad_weights), (output, grad_start))
    zeros_init = jax.tree.map(jnp.zeros_like, params)
    totals, (outputs, grad_inputs) = lax.scan(one_group, zeros_init, (inputs, segments, cotangents))
    return (outputs.reshape(TOKENS, D), grad_inputs.reshape(TOKENS, D), totals[0], totals[1], totals[2], totals[3], totals[4], totals[5], totals[6], totals[7], totals[8], totals[9], totals[10], totals[11], totals[12], totals[13], totals[14])
```

```python
import functools

import jax
import jax.numpy as jnp
from jax import lax
from jax.experimental import pallas as pl
from jax.experimental.pallas import tpu as pltpu
from jax.sharding import PartitionSpec as P

NEG_FILL = -1e30
HEAD_DIM = 64
D = 1024
LEN = 2048
QBLOCK = 512
SEQS = 1


EPSILON = 1e-06


def rounded(values):
    return values.astype(jnp.bfloat16)


def matmul(left, right):
    return jnp.dot(left, right, preferred_element_type=jnp.float32)


def over_tokens(left, right):
    return lax.dot_general(
        left, right, (((0,), (0,)), ((), ())), preferred_element_type=jnp.float32
    )


def against(left, right):
    return lax.dot_general(
        left, right, (((1,), (1,)), ((), ())), preferred_element_type=jnp.float32
    )


def token_sum(values):
    return jnp.sum(values, axis=0, dtype=jnp.float32)


def exact_gelu(inputs):
    return jax.nn.gelu(inputs, approximate=False)


def gather_weights(shards):
    front_set = (
        lax.all_gather(shards[0], "row", axis=0, tiled=True),
        lax.all_gather(shards[1], "row", axis=0, tiled=True),
        lax.all_gather(shards[2], "row", axis=0, tiled=True),
        lax.all_gather(shards[3], "row", axis=0, tiled=True),
    )
    back_set = (
        lax.all_gather(shards[4], "row", axis=1, tiled=True),
        lax.all_gather(shards[5], "row", axis=1, tiled=True),
    )
    proj_cols = back_set[0]
    return (
        front_set[0],
        front_set[1],
        front_set[2],
        front_set[3],
        back_set[0],
        back_set[1],
        proj_cols,
    )


def spread_features(values):
    return lax.all_gather(rounded(values), "col", axis=1, tiled=True)


def sum_partials(partial_terms):
    return lax.psum_scatter(
        partial_terms.astype(jnp.bfloat16), "col", scatter_dimension=1, tiled=True
    ).astype(jnp.float32)


def spread_grads(values):
    return lax.all_gather(values, "col", axis=1, tiled=True)


def sum_grad_partials(partial_terms):
    return lax.psum_scatter(
        partial_terms.astype(jnp.bfloat16), "col", scatter_dimension=1, tiled=True
    ).astype(jnp.float32)


def norm_forward(summed, norm_gain, norm_shift):
    totals = lax.psum((jnp.sum(summed, axis=1), jnp.sum(summed * summed, axis=1)), "col")
    center = totals[0][:, None] / D
    spread = totals[1][:, None] / D - center * center
    inverse = lax.rsqrt(spread + EPSILON)
    normed = (summed - center) * inverse
    return (normed * norm_gain + norm_shift, normed, inverse)


def norm_backward(grad_output, normed, inverse, norm_gain):
    scaled = grad_output * norm_gain
    totals = lax.psum((jnp.sum(scaled, axis=1), jnp.sum(scaled * normed, axis=1)), "col")
    grad_input = inverse * (scaled - totals[0][:, None] / D - normed * (totals[1][:, None] / D))
    return (grad_input, jnp.sum(grad_output * normed, axis=0), jnp.sum(grad_output, axis=0))


def split_heads(values):
    return values.reshape(SEQS, LEN, values.shape[1] // HEAD_DIM, HEAD_DIM)


def attend_forward(queries, key_rows, value_rows, segments):
    score_scale = HEAD_DIM ** (-0.5)
    blocks = LEN // QBLOCK
    query_heads = split_heads(queries)
    key_heads = split_heads(key_rows)
    value_heads = split_heads(value_rows)

    def attend_one_block(block_index):
        sequence = block_index // blocks
        offset = block_index % blocks * QBLOCK
        seq_queries = lax.dynamic_index_in_dim(query_heads, sequence, 0, keepdims=False)
        seq_keys = lax.dynamic_index_in_dim(key_heads, sequence, 0, keepdims=False)
        seq_values = lax.dynamic_index_in_dim(value_heads, sequence, 0, keepdims=False)
        seq_segments = lax.dynamic_index_in_dim(segments, sequence, 0, keepdims=False)
        block_queries = lax.dynamic_slice_in_dim(seq_queries, offset, QBLOCK, 0)
        block_segments = lax.dynamic_slice_in_dim(seq_segments, offset, QBLOCK, 0)
        scores = (
            jnp.einsum("qhd,khd->hqk", block_queries, seq_keys, preferred_element_type=jnp.float32)
            * score_scale
        )
        same_doc = block_segments[:, None] == seq_segments[None, :]
        scores = jnp.where(same_doc[None], scores, NEG_FILL)
        highest = jnp.max(scores, axis=2, keepdims=True)
        weights = jnp.exp(scores - highest)
        totals = jnp.sum(weights, axis=2, keepdims=True)
        mixture = jnp.einsum(
            "hqk,khd->qhd",
            rounded(weights / totals),
            seq_values,
            preferred_element_type=jnp.float32,
        )
        return (mixture, (highest + jnp.log(totals))[:, :, 0])

    mixture, log_total = lax.map(attend_one_block, jnp.arange(SEQS * blocks))
    return (mixture.reshape(queries.shape), log_total)


def attend_backward(queries, key_rows, value_rows, segments, log_total, grad_mixed):
    score_scale = HEAD_DIM ** (-0.5)
    blocks = LEN // QBLOCK
    heads_here = queries.shape[1] // HEAD_DIM
    query_heads = split_heads(queries)
    key_heads = split_heads(key_rows)
    value_heads = split_heads(value_rows)
    grad_heads = split_heads(grad_mixed)
    lse_rows = log_total.reshape(SEQS, blocks, heads_here, QBLOCK)

    def one_sequence(sequence):
        seq_queries = lax.dynamic_index_in_dim(query_heads, sequence, 0, keepdims=False)
        seq_keys = lax.dynamic_index_in_dim(key_heads, sequence, 0, keepdims=False)
        seq_values = lax.dynamic_index_in_dim(value_heads, sequence, 0, keepdims=False)
        seq_grads = lax.dynamic_index_in_dim(grad_heads, sequence, 0, keepdims=False)
        seq_segments = lax.dynamic_index_in_dim(segments, sequence, 0, keepdims=False)
        seq_lse = lax.dynamic_index_in_dim(lse_rows, sequence, 0, keepdims=False)

        def one_one_block(carry, block_index):
            offset = block_index * QBLOCK
            block_queries = lax.dynamic_slice_in_dim(seq_queries, offset, QBLOCK, 0)
            block_grads = lax.dynamic_slice_in_dim(seq_grads, offset, QBLOCK, 0)
            block_segments = lax.dynamic_slice_in_dim(seq_segments, offset, QBLOCK, 0)
            block_lse = lax.dynamic_index_in_dim(seq_lse, block_index, 0, keepdims=False)
            scores = (
                jnp.einsum(
                    "qhd,khd->hqk", block_queries, seq_keys, preferred_element_type=jnp.float32
                )
                * score_scale
            )
            same_doc = block_segments[:, None] == seq_segments[None, :]
            scores = jnp.where(same_doc[None], scores, NEG_FILL)
            probs = jnp.exp(scores - block_lse[:, :, None])
            grad_probs = jnp.einsum(
                "qhd,khd->hqk", block_grads, seq_values, preferred_element_type=jnp.float32
            )
            grad_scores = rounded(
                probs * (grad_probs - jnp.sum(probs * grad_probs, axis=2, keepdims=True))
            )
            grad_query = (
                jnp.einsum(
                    "hqk,khd->qhd", grad_scores, seq_keys, preferred_element_type=jnp.float32
                )
                * score_scale
            )
            key_sum = (
                carry[0]
                + jnp.einsum(
                    "hqk,qhd->khd", grad_scores, block_queries, preferred_element_type=jnp.float32
                )
                * score_scale
            )
            value_sum = carry[1] + jnp.einsum(
                "hqk,qhd->khd", rounded(probs), block_grads, preferred_element_type=jnp.float32
            )
            return ((key_sum, value_sum), rounded(grad_query))

        zeros_init = jnp.zeros((LEN, heads_here, HEAD_DIM), jnp.float32)
        (key_sum, value_sum), grad_query = lax.scan(
            one_one_block, (zeros_init, zeros_init), jnp.arange(blocks)
        )
        return (grad_query.reshape(LEN, heads_here, HEAD_DIM), rounded(key_sum), rounded(value_sum))

    grad_query, grad_key, grad_value = lax.map(one_sequence, jnp.arange(SEQS))
    return (
        grad_query.reshape(queries.shape),
        grad_key.reshape(queries.shape),
        grad_value.reshape(queries.shape),
    )


def layer_forward(hidden, params, gathered, segments):
    query_w, key_w, value_w, inner_w, proj_w, outer_w, proj_cols = gathered
    whole_in = spread_features(hidden)
    queries = rounded(matmul(whole_in, query_w) + params[0])
    key_rows = rounded(matmul(whole_in, key_w))
    value_rows = rounded(matmul(whole_in, value_w) + params[1])
    mixture, log_total = attend_forward(queries, key_rows, value_rows, segments)
    attended = rounded(mixture)
    attn_branch = sum_partials(matmul(attended, proj_w)) + params[2]
    first_norm, normed_one, inverse_one = norm_forward(hidden + attn_branch, params[3], params[4])
    whole_mid = spread_features(first_norm)
    inner_act = matmul(whole_mid, inner_w) + params[5]
    active = rounded(exact_gelu(inner_act))
    ffn_branch = sum_partials(matmul(active, outer_w)) + params[6]
    output, normed_two, inverse_two = norm_forward(first_norm + ffn_branch, params[7], params[8])
    kept_values = (
        whole_in,
        queries,
        key_rows,
        value_rows,
        log_total,
        attended,
        normed_one,
        inverse_one,
        whole_mid,
        inner_act,
        active,
        normed_two,
        inverse_two,
    )
    return (output, kept_values)


def layer_backward(grad_output, kept_values, gathered, params, segments):
    (
        whole_in,
        queries,
        key_rows,
        value_rows,
        log_total,
        attended,
        normed_one,
        inverse_one,
        whole_mid,
        inner_act,
        active,
        normed_two,
        inverse_two,
    ) = kept_values
    query_w, key_w, value_w, inner_w, proj_w, outer_w, proj_cols = gathered
    grad_second, ffn_gain_sum, ffn_shift_sum = norm_backward(
        grad_output, normed_two, inverse_two, params[7]
    )
    ffn_low = rounded(grad_second)
    whole_second = spread_grads(ffn_low)
    outer_term = over_tokens(active, whole_second)
    active_grad = against(whole_second, outer_w)
    unused, pullback = jax.vjp(exact_gelu, inner_act)
    inner_low = rounded(pullback(active_grad)[0])
    inner_term = over_tokens(whole_mid, inner_low)
    grad_first = grad_second + sum_grad_partials(against(inner_low, inner_w))
    grad_attn, attn_gain_sum, attn_shift_sum = norm_backward(
        grad_first, normed_one, inverse_one, params[3]
    )
    attn_low = rounded(grad_attn)
    whole_attn = spread_grads(attn_low)
    proj_term = over_tokens(attended, whole_attn)
    mixed_grad = rounded(against(whole_attn, proj_w))
    query_low, key_low, value_low = attend_backward(
        queries, key_rows, value_rows, segments, log_total, mixed_grad
    )
    input_terms = (
        against(query_low, query_w) + against(key_low, key_w) + against(value_low, value_w)
    )
    grad_input = grad_attn + sum_grad_partials(input_terms)
    row_terms = (
        over_tokens(whole_in, query_low),
        over_tokens(whole_in, key_low),
        over_tokens(whole_in, value_low),
        inner_term,
    )
    col_terms = (proj_term, outer_term)
    small_terms = (
        token_sum(query_low),
        token_sum(value_low),
        token_sum(attn_low),
        attn_gain_sum,
        attn_shift_sum,
        token_sum(inner_low),
        token_sum(ffn_low),
        ffn_gain_sum,
        ffn_shift_sum,
    )
    return (grad_input, row_terms, col_terms, small_terms)


def general_device(
    hidden_in,
    query_weight,
    key_weight,
    value_weight,
    query_bias,
    value_bias,
    proj_weight,
    proj_bias,
    attn_gain,
    attn_shift,
    inner_weight,
    inner_bias,
    outer_weight,
    outer_bias,
    ffn_gain,
    ffn_shift,
    segment_ids,
    grad_out,
):
    shards = (query_weight, key_weight, value_weight, inner_weight, proj_weight, outer_weight)
    params = (
        query_bias,
        value_bias,
        proj_bias,
        attn_gain,
        attn_shift,
        inner_bias,
        outer_bias,
        ffn_gain,
        ffn_shift,
    )
    gathered = gather_weights(shards)
    start_in = hidden_in.astype(jnp.float32)
    middle, kept_one = layer_forward(start_in, params, gathered, segment_ids)
    final_out, kept_two = layer_forward(middle, params, gathered, segment_ids)
    kept = (kept_one, kept_two)
    grad_flow = grad_out.astype(jnp.float32)
    row_parts = []
    col_parts = []
    small_parts = []
    for layer_index in (1, 0):
        grad_flow, row_terms, col_terms, small_terms = layer_backward(
            grad_flow, kept[layer_index], gathered, params, segment_ids
        )
        row_parts.append(row_terms)
        col_parts.append(col_terms)
        small_parts.append(small_terms)
    row_sum = jax.tree.map(jnp.add, tuple(row_parts[0]), tuple(row_parts[1]))
    col_sum = jax.tree.map(jnp.add, tuple(col_parts[0]), tuple(col_parts[1]))
    small_sum = jax.tree.map(jnp.add, small_parts[0], small_parts[1])
    row_sum = (
        lax.psum_scatter(
            row_sum[0].astype(jnp.bfloat16), "row", scatter_dimension=0, tiled=True
        ).astype(jnp.float32),
        lax.psum_scatter(
            row_sum[1].astype(jnp.bfloat16), "row", scatter_dimension=0, tiled=True
        ).astype(jnp.float32),
        lax.psum_scatter(
            row_sum[2].astype(jnp.bfloat16), "row", scatter_dimension=0, tiled=True
        ).astype(jnp.float32),
        lax.psum_scatter(
            row_sum[3].astype(jnp.bfloat16), "row", scatter_dimension=0, tiled=True
        ).astype(jnp.float32),
    )
    col_sum = (
        lax.psum_scatter(
            col_sum[0].astype(jnp.bfloat16), "row", scatter_dimension=1, tiled=True
        ).astype(jnp.float32),
        lax.psum_scatter(
            col_sum[1].astype(jnp.bfloat16), "row", scatter_dimension=1, tiled=True
        ).astype(jnp.float32),
    )
    small_sum = lax.psum(
        (
            small_sum[0],
            small_sum[1],
            small_sum[2],
            small_sum[3],
            small_sum[4],
            small_sum[5],
            small_sum[6],
            small_sum[7],
            small_sum[8],
        ),
        "row",
    )
    return (
        final_out,
        grad_flow,
        row_sum[0],
        row_sum[1],
        row_sum[2],
        small_sum[0],
        small_sum[1],
        col_sum[0],
        small_sum[2],
        small_sum[3],
        small_sum[4],
        row_sum[3],
        small_sum[5],
        col_sum[1],
        small_sum[6],
        small_sum[7],
        small_sum[8],
    )


ANY = pl.BlockSpec(memory_space=pl.ANY)
VMEM = pl.BlockSpec(memory_space=pltpu.VMEM)
MESH = pl.DeviceIdType.MESH
DMA = pltpu.SemaphoreType.DMA
BF16 = jnp.bfloat16
F32 = jnp.float32


def place():
    row = lax.axis_index("row")
    depth = lax.axis_index("col")
    core = row % 2
    chip = row // 2
    x = chip % 2
    y = chip // 2
    return row, depth, core, chip, x, y


def remote(src, dst, send_sem, recv_sem, row, depth):
    return pltpu.make_async_remote_copy(
        src_ref=src,
        dst_ref=dst,
        send_sem=send_sem,
        recv_sem=recv_sem,
        device_id={"row": row, "col": depth},
        device_id_type=MESH,
    )


def span(start, size):
    return pl.ds(pl.multiple_of(start, 128), size)


def greet(row, depth, core, chip, x, y):
    barrier = pltpu.get_barrier_semaphore()
    mate = chip * 2 + (1 - core)
    friends = [(mate, depth)]
    for step in (1, 2, 3):
        friends.append((row, (depth + step) % 4))
        friends.append((mate, (depth + step) % 4))
    friends.append(((y * 2 + 1 - x) * 2 + core, depth))
    friends.append((((1 - y) * 2 + x) * 2 + core, depth))
    for r, d in friends:
        pl.semaphore_signal(
            barrier, inc=1, device_id={"row": r, "col": d}, device_id_type=MESH
        )
    pl.semaphore_wait(barrier, len(friends))


def gather_kernel(
    q_ref, k_ref, v_ref, proj_ref, inner_ref, outer_ref, small_ref, x_ref, g_ref,
    wqkv, wproj, winner, wouter, smalls, u_out, g_out,
    swap_s, swap_r, local_s, z_s, z_r, sm_s, sm_r, p1_s, p1_r, p2_s, p2_r, t_s, t_r, t_l,
):
    row, depth, core, chip, x, y = place()
    mate = chip * 2 + (1 - core)
    x_chip = y * 2 + 1 - x
    y_chip = (1 - y) * 2 + x
    x_row = x_chip * 2 + core
    y_row = y_chip * 2 + core
    greet(row, depth, core, chip, x, y)

    def swap_src(piece, half):
        if piece < 3:
            return (q_ref, k_ref, v_ref)[piece].at[:, span(half * 128, 128)]
        if piece == 3:
            return proj_ref.at[span(half * 128, 128), :]
        if piece == 4:
            return inner_ref.at[:, span(half * 512, 512)]
        return outer_ref.at[span(half * 512, 512), :]

    def swap_dst(piece, owner):
        if piece < 3:
            return wqkv.at[span(owner * 128, 128), span(piece * 512 + depth * 128, 128)]
        if piece == 3:
            return wproj.at[span(depth * 128, 128), span(owner * 128, 128)]
        if piece == 4:
            return winner.at[span(owner * 128, 128), span(depth * 512, 512)]
        return wouter.at[span(depth * 512, 512), span(owner * 128, 128)]

    def unit(piece):
        if piece < 3:
            return wqkv.at[span(chip * 256, 256), span(piece * 512 + depth * 128, 128)]
        if piece == 3:
            return wproj.at[span(depth * 128, 128), span(chip * 256, 256)]
        if piece == 4:
            return winner.at[span(chip * 256, 256), span(depth * 512, 512)]
        return wouter.at[span(depth * 512, 512), span(chip * 256, 256)]

    def region(group, part, block):
        if group == 0:
            return wqkv.at[span(block * 256 + part * 128, 128), :]
        if group == 1:
            return wproj.at[pl.ds(part * 256, 256), span(block * 256, 256)]
        if group == 2:
            return winner.at[span(block * 256 + part * 128, 128), :]
        return wouter.at[pl.ds(part * 1024, 1024), span(block * 256, 256)]

    waits = []
    swaps, locals_ = [], []
    for piece in range(6):
        cp = remote(
            swap_src(piece, 1 - core), swap_dst(piece, row),
            swap_s.at[piece], swap_r.at[piece], mate, depth,
        )
        cp.start()
        swaps.append(cp)
        lc = pltpu.make_async_copy(swap_src(piece, core), swap_dst(piece, row), local_s.at[piece])
        lc.start()
        locals_.append(lc)
    small_local = pltpu.make_async_copy(small_ref, smalls.at[depth], local_s.at[6])
    small_local.start()

    zs = {}

    def start_z(pieces):
        for piece in pieces:
            swaps[piece].wait_recv()
            locals_[piece].wait()
            for k in (1, 2, 3):
                cp = remote(
                    unit(piece), unit(piece), z_s.at[piece, k - 1], z_r.at[piece, k - 1],
                    row, (depth + k) % 4,
                )
                cp.start()
                zs[piece, k] = cp

    def token_copies(index, src, dst):
        for j in range(4):
            to_core, to_depth = j % 2, core * 2 + j // 2
            mine = (to_core == core) & (to_depth == depth)
            source = src.at[pl.ds(j * 512, 512), :]
            target = dst.at[:, span(depth * 256, 256)]

            @pl.when(mine)
            def _():
                pltpu.make_async_copy(source, target, t_l.at[index]).start()

            @pl.when(jnp.logical_not(mine))
            def _():
                remote(
                    source, target, t_s.at[index, j], t_r.at[index, depth],
                    chip * 2 + to_core, to_depth,
                ).start()

    def token_waits(index, src, dst):
        from_core = depth // 2
        for s in range(4):
            mine = (from_core == core) & (s == depth)
            target = dst.at[:, pl.ds(s * 256, 256)]
            source = src.at[pl.ds(0, 512), :]

            @pl.when(mine)
            def _():
                pltpu.make_async_copy(source, target, t_l.at[index]).wait()

            @pl.when(jnp.logical_not(mine))
            def _():
                remote(
                    source, target, t_s.at[index, 0], t_r.at[index, s], mate, depth
                ).wait_recv()
        for j in range(4):
            to_core, to_depth = j % 2, core * 2 + j // 2
            mine = (to_core == core) & (to_depth == depth)

            @pl.when(jnp.logical_not(mine))
            def _():
                remote(
                    src.at[pl.ds(j * 512, 512), :], dst.at[:, pl.ds(0, 256)],
                    t_s.at[index, j], t_r.at[index, 0], mate, depth,
                ).wait_send()

    start_z((0, 1, 2))
    token_copies(0, x_ref, u_out)
    start_z((3, 4, 5))
    small_copies = []
    for k in (1, 2, 3):
        cp = remote(
            small_ref, smalls.at[depth], sm_s.at[k - 1], sm_r.at[k - 1], row, (depth + k) % 4
        )
        cp.start()
        small_copies.append(cp)
    token_copies(1, g_ref, g_out)

    first, second = {}, {}

    def start_first(group):
        for part, target in ((0, x_row), (1, y_row)):
            cp = remote(
                region(group, part, chip), region(group, part, chip),
                p1_s.at[group, part], p1_r.at[group, part], target, depth,
            )
            cp.start()
            first[group, part] = cp

    def start_second(group):
        for part, target, other in ((0, y_row, x_chip), (1, x_row, y_chip)):
            first[group, part].wait_recv()
            for i, block in enumerate((chip, other)):
                cp = remote(
                    region(group, part, block), region(group, part, block),
                    p2_s.at[group, part, i], p2_r.at[group, part, i], target, depth,
                )
                cp.start()
                second[group, part, i] = cp

    members = ((0, 1, 2), (3,), (4,), (5,))
    for group in range(4):
        for piece in members[group]:
            for k in (1, 2, 3):
                zs[piece, k].wait_recv()
        start_first(group)
        if group > 0:
            start_second(group - 1)
    start_second(3)
    token_waits(0, x_ref, u_out)
    token_waits(1, g_ref, g_out)
    for cp in small_copies:
        cp.wait()
    small_local.wait()
    for cp in second.values():
        cp.wait()
    for cp in first.values():
        cp.wait_send()
    for cp in zs.values():
        cp.wait_send()
    for cp in swaps:
        cp.wait_send()


def gather_all(q, k, v, proj, inner, outer, small, x_rolled, g_rolled):
    sd = jax.ShapeDtypeStruct
    return pl.pallas_call(
        gather_kernel,
        out_shape=(
            sd((1024, 1536), BF16),
            sd((512, 1024), BF16),
            sd((1024, 2048), BF16),
            sd((2048, 1024), BF16),
            sd((4,) + small.shape, F32),
            sd((512, 1024), BF16),
            sd((512, 1024), BF16),
        ),
        in_specs=[ANY] * 9,
        out_specs=[ANY] * 7,
        scratch_shapes=[
            DMA((6,)), DMA((6,)), DMA((7,)), DMA((6, 3)), DMA((6, 3)), DMA((3,)), DMA((3,)),
            DMA((4, 2)), DMA((4, 2)), DMA((4, 2, 2)), DMA((4, 2, 2)),
            DMA((2, 4)), DMA((2, 4)), DMA((2,)),
        ],
        compiler_params=pltpu.CompilerParams(collective_id=1, has_side_effects=True),
    )(q, k, v, proj, inner, outer, small, x_rolled, g_rolled)


SHAPES = ((1024, 256), (128, 2048), (256, 256), (128, 512), (128, 512), (128, 512))
UNITS = ((512, 256), (256, 512), (128, 256), (256, 128), (256, 128), (256, 128))
FULLS = ((2048, 256), (256, 2048), (512, 256), (256, 512), (256, 512), (256, 512))
OUTS = ((1024, 128), (128, 1024), (256, 128), (128, 256), (128, 256), (128, 256))
HALVES = ((512, 128), (128, 512), (128, 128), (128, 128), (128, 128), (128, 128))
BY_COLS = (True, False, True, False, False, False)


def add_rows(dst, terms):
    rows = dst.shape[0]
    step = 32

    def body(i, carry):
        sl = pl.ds(pl.multiple_of(i * step, step), step)
        total = terms[0][sl, :].astype(F32)
        for term in terms[1:]:
            total = total + term[sl, :].astype(F32)
        dst[sl, :] = total.astype(dst.dtype)
        return carry

    lax.fori_loop(0, rows // step, body, 0)


def scatter_kernel(*refs):
    grads = refs[0:6]
    small_ref, ho_ref, gi_ref = refs[6:9]
    outs = refs[9:15]
    small_out, ho_out, gi_out = refs[15:18]
    rest = list(refs[18:])
    own = [[rest.pop(0) for _ in range(2)] for _ in range(6)]
    got1 = [[rest.pop(0) for _ in range(2)] for _ in range(6)]
    got2 = [[rest.pop(0) for _ in range(2)] for _ in range(6)]
    full = [rest.pop(0) for _ in range(6)]
    zgot = [rest.pop(0) for _ in range(6)]
    fin = [rest.pop(0) for _ in range(6)]
    cgot = [rest.pop(0) for _ in range(6)]
    sb = rest.pop(0)
    sg = rest.pop(0)
    (o_s, p1_s, p1_r, p2_s, p2_r, z_s, z_r, c_s, c_r, sm_s, sm_r, t_s, t_r, t_l) = rest

    row, depth, core, chip, x, y = place()
    mate = chip * 2 + (1 - core)
    x_row = (y * 2 + 1 - x) * 2 + core
    y_row = ((1 - y) * 2 + x) * 2 + core
    greet(row, depth, core, chip, x, y)

    def region(group, part, block):
        rows = SHAPES[group][0]
        if BY_COLS[group]:
            return grads[group].at[pl.ds(part * rows, rows), span(block * 256, 256)]
        return grads[group].at[span(block * 256 + part * 128, 128), :]

    def unit(group, z):
        if BY_COLS[group]:
            return full[group].at[span(z * UNITS[group][0], UNITS[group][0]), :]
        return full[group].at[:, span(z * UNITS[group][1], UNITS[group][1])]

    def side(group, half):
        if BY_COLS[group]:
            return fin[group].at[:, span(half * 128, 128)]
        return fin[group].at[span(half * 128, 128), :]

    def out_side(group, half):
        size = HALVES[group]
        if BY_COLS[group]:
            return outs[group].at[span(half * size[0], size[0]), :]
        return outs[group].at[:, span(half * size[1], size[1])]

    copies = {}

    def start_first(group):
        for part in (0, 1):
            target = y_row if part == 0 else x_row
            for i in (0, 1):
                kept = y * 2 + i if part == 0 else i * 2 + x
                sent = (1 - y) * 2 + i if part == 0 else i * 2 + (1 - x)
                lc = pltpu.make_async_copy(
                    region(group, part, kept), own[group][part].at[i], o_s.at[group, part, i]
                )
                lc.start()
                cp = remote(
                    region(group, part, sent), got1[group][part].at[i],
                    p1_s.at[group, part, i], p1_r.at[group, part, i], target, depth,
                )
                cp.start()
                copies["o", group, part, i] = lc
                copies["p1", group, part, i] = cp

    def start_second(group):
        for part in (0, 1):
            target = x_row if part == 0 else y_row
            mine = x if part == 0 else y
            for i in (0, 1):
                copies["o", group, part, i].wait()
                copies["p1", group, part, i].wait_recv()
            other = own[group][part].at[1 - mine]
            add_rows(other, (other, got1[group][part].at[1 - mine]))
            cp = remote(
                other, got2[group][part], p2_s.at[group, part], p2_r.at[group, part], target, depth
            )
            cp.start()
            copies["p2", group, part] = cp

    def start_depth(group):
        rows = SHAPES[group][0]
        for part in (0, 1):
            mine = x if part == 0 else y
            copies["p2", group, part].wait_recv()
            add_rows(
                full[group].at[pl.ds(part * rows, rows), :],
                (own[group][part].at[mine], got1[group][part].at[mine], got2[group][part]),
            )
        for k in (1, 2, 3):
            cp = remote(
                unit(group, (depth + k) % 4), zgot[group].at[k - 1],
                z_s.at[group, k - 1], z_r.at[group, k - 1], row, (depth + k) % 4,
            )
            cp.start()
            copies["z", group, k] = cp

    def start_core(group):
        for k in (1, 2, 3):
            copies["z", group, k].wait_recv()
        add_rows(
            fin[group],
            (unit(group, depth), zgot[group].at[0], zgot[group].at[1], zgot[group].at[2]),
        )
        cp = remote(
            side(group, 1 - core), cgot[group], c_s.at[group], c_r.at[group], mate, depth
        )
        cp.start()
        copies["c", group] = cp

    def finish(group):
        add_rows(out_side(group, core), (side(group, core),))
        copies["c", group].wait_recv()
        add_rows(out_side(group, 1 - core), (cgot[group],))

    def token_copies(index, src, dst):
        j = (depth % 2) * 2 + core
        to_core = depth // 2
        for z in range(4):
            mine = (to_core == core) & (z == depth)
            source = src.at[:, pl.ds(z * 256, 256)]
            target = dst.at[span(j * 512, 512), :]

            @pl.when(mine)
            def _():
                pltpu.make_async_copy(source, target, t_l.at[index]).start()

            @pl.when(jnp.logical_not(mine))
            def _():
                remote(
                    source, target, t_s.at[index, z], t_r.at[index, j], chip * 2 + to_core, z
                ).start()

    def token_waits(index, src, dst):
        to_core = depth // 2
        j_own = (depth % 2) * 2 + core
        for j in range(4):
            from_core, from_depth = j % 2, core * 2 + j // 2
            mine = (from_core == core) & (from_depth == depth)
            target = dst.at[pl.ds(j * 512, 512), :]
            source = src.at[:, pl.ds(0, 256)]

            @pl.when(mine)
            def _():
                pltpu.make_async_copy(source, target, t_l.at[index]).wait()

            @pl.when(jnp.logical_not(mine))
            def _():
                remote(
                    source, target, t_s.at[index, 0], t_r.at[index, j], mate, depth
                ).wait_recv()
        for z in range(4):
            mine = (to_core == core) & (z == depth)

            @pl.when(jnp.logical_not(mine))
            def _():
                remote(
                    src.at[:, pl.ds(z * 256, 256)], dst.at[pl.ds(0, 512), :],
                    t_s.at[index, z], t_r.at[index, 0], mate, depth,
                ).wait_send()

    def small_send(step, slot, target_row, target_depth):
        cp = remote(
            sb.at[step], sg.at[slot], sm_s.at[slot], sm_r.at[slot], target_row, target_depth
        )
        cp.start()
        copies["s", slot] = cp

    def small_add(step, slot):
        copies["s", slot].wait_recv()
        sb[step + 1] = sb[step] + sg[slot]

    sb[0] = small_ref[...]
    small_send(0, 0, mate, depth)
    start_first(0)
    start_first(1)
    token_copies(0, ho_ref, ho_out)
    token_copies(1, gi_ref, gi_out)
    small_add(0, 0)
    small_send(1, 1, x_row, depth)
    for group in range(6):
        start_second(group)
        if group + 2 < 6:
            start_first(group + 2)
        if group == 0:
            small_add(1, 1)
            small_send(2, 2, y_row, depth)
        if group == 1:
            small_add(2, 2)
            for k in (1, 2, 3):
                small_send(3, 2 + k, row, (depth + k) % 4)
        if group > 0:
            start_depth(group - 1)
        if group > 1:
            start_core(group - 2)
    start_depth(5)
    start_core(4)
    for k in (1, 2, 3):
        copies["s", 2 + k].wait_recv()
    small_out[...] = ((sb[3] + sg[3]) + sg[4]) + sg[5]
    for group in range(5):
        finish(group)
    token_waits(0, ho_ref, ho_out)
    token_waits(1, gi_ref, gi_out)
    start_core(5)
    finish(5)
    for key, cp in copies.items():
        if key[0] != "o":
            cp.wait_send()


def scatter_all(outer, inner, proj, q, k, v, small, ho, gi):
    sd = jax.ShapeDtypeStruct
    scratch = []
    for size in SHAPES:
        scratch += [pltpu.VMEM((2,) + size, BF16)] * 2
    for size in SHAPES:
        scratch += [pltpu.VMEM((2,) + size, BF16)] * 2
    for size in SHAPES:
        scratch += [pltpu.VMEM(size, BF16)] * 2
    scratch += [pltpu.VMEM(size, BF16) for size in FULLS]
    scratch += [pltpu.VMEM((3,) + size, BF16) for size in UNITS]
    scratch += [pltpu.VMEM(size, BF16) for size in UNITS]
    scratch += [pltpu.VMEM(size, BF16) for size in HALVES]
    scratch += [pltpu.VMEM((4,) + small.shape, F32), pltpu.VMEM((6,) + small.shape, F32)]
    scratch += [
        DMA((6, 2, 2)), DMA((6, 2, 2)), DMA((6, 2, 2)), DMA((6, 2)), DMA((6, 2)),
        DMA((6, 3)), DMA((6, 3)), DMA((6,)), DMA((6,)), DMA((6,)), DMA((6,)),
        DMA((2, 4)), DMA((2, 4)), DMA((2,)),
    ]
    return pl.pallas_call(
        scatter_kernel,
        out_shape=tuple(sd(size, F32) for size in OUTS)
        + (sd(small.shape, F32), sd((2048, 256), BF16), sd((2048, 256), BF16)),
        in_specs=[ANY] * 6 + [VMEM] + [ANY] * 2,
        out_specs=[VMEM] * 7 + [ANY] * 2,
        scratch_shapes=scratch,
        compiler_params=pltpu.CompilerParams(
            collective_id=2, has_side_effects=True, vmem_limit_bytes=56 * 1024 * 1024
        ),
    )(outer, inner, proj, q, k, v, small, ho, gi)


def attend_kernel(flag_ref, q_ref, k_ref, v_ref, idq_ref, idk_ref, o_ref, lse_ref):
    rows = q_ref.shape[0]
    lane = lax.broadcasted_iota(jnp.int32, (1, 128), 1)
    low_half = lane < HEAD_DIM

    def compute(masked):
        scaled = q_ref[...] * jnp.asarray(HEAD_DIM**-0.5, BF16)
        keys = k_ref[...]
        values = v_ref[...]
        outs, logs = [], []
        for head in (0, 1):
            here = low_half if head == 0 else jnp.logical_not(low_half)
            queries = jnp.where(here, scaled, jnp.zeros_like(scaled))
            scores = against(queries, keys)
            if masked:
                scores = jnp.where(idq_ref[...] == idk_ref[...], scores, NEG_FILL)
            top = jnp.max(scores, axis=1, keepdims=True)
            weights = jnp.exp(scores - top)
            total = jnp.sum(weights, axis=1, keepdims=True)
            mixed = matmul(weights.astype(BF16), values)
            outs.append(mixed / total)
            logs.append(top + jnp.log(total))
        o_ref[...] = jnp.where(low_half, outs[0], outs[1]).astype(o_ref.dtype)
        lse_ref[...] = jnp.where(low_half, logs[0], logs[1])

    @pl.when(flag_ref[0] == 1)
    def _():
        compute(False)

    @pl.when(flag_ref[0] != 1)
    def _():
        compute(True)


def attend(flag, qkv, id_col, id_row):
    tokens, width = qkv.shape[0], qkv.shape[1] // 3
    pairs = width // 128
    block = 256
    return pl.pallas_call(
        attend_kernel,
        out_shape=(
            jax.ShapeDtypeStruct((tokens, width), BF16),
            jax.ShapeDtypeStruct((tokens, width), F32),
        ),
        grid_spec=pltpu.PrefetchScalarGridSpec(
            num_scalar_prefetch=1,
            grid=(width // 128, tokens // block),
            in_specs=[
                pl.BlockSpec((block, 128), lambda h, i, f: (i, h)),
                pl.BlockSpec((tokens, 128), lambda h, i, f: (0, h + pairs)),
                pl.BlockSpec((tokens, 128), lambda h, i, f: (0, h + 2 * pairs)),
                pl.BlockSpec((block, 1), lambda h, i, f: (i, 0)),
                pl.BlockSpec((1, tokens), lambda h, i, f: (0, 0)),
            ],
            out_specs=[
                pl.BlockSpec((block, 128), lambda h, i, f: (i, h)),
                pl.BlockSpec((block, 128), lambda h, i, f: (i, h)),
            ],
        ),
        compiler_params=pltpu.CompilerParams(
            dimension_semantics=("arbitrary", "arbitrary"), vmem_limit_bytes=48 * 1024 * 1024
        ),
        name="attend",
    )(flag, qkv, qkv, qkv, id_col, id_row)


def attend_back_kernel(
    flag_ref, q_ref, k_ref, v_ref, do_ref, lse_ref, idk_ref, idq_ref,
    dq_ref, dk_ref, dv_ref, dk_acc, dv_acc,
):
    step = pl.program_id(1)
    last = pl.num_programs(1) - 1
    scale = HEAD_DIM**-0.5
    lane = lax.broadcasted_iota(jnp.int32, (1, 128), 1)
    low_half = lane < HEAD_DIM

    @pl.when(step == 0)
    def _():
        dk_acc[...] = jnp.zeros_like(dk_acc)
        dv_acc[...] = jnp.zeros_like(dv_acc)

    def compute(masked):
        queries = q_ref[...]
        scaled = queries * jnp.asarray(scale, BF16)
        keys = k_ref[...]
        values = v_ref[...]
        grads = do_ref[...]
        lse_t = lse_ref[...].T
        dqs, dks, dvs = [], [], []
        for head in (0, 1):
            here = low_half if head == 0 else jnp.logical_not(low_half)
            zero = jnp.zeros_like(keys)
            scores = against(jnp.where(here, keys, zero), scaled)
            if masked:
                scores = jnp.where(idk_ref[...] == idq_ref[...], scores, NEG_FILL)
            log_row = lse_t[head * HEAD_DIM : head * HEAD_DIM + 1, :]
            probs = jnp.exp(scores - log_row)
            grad_probs = against(jnp.where(here, values, zero), grads)
            moved = probs * grad_probs
            delta = jnp.sum(moved, axis=0, keepdims=True)
            grad_scores = (moved - probs * delta).astype(BF16)
            dvs.append(matmul(probs.astype(BF16), grads))
            dks.append(matmul(grad_scores, queries))
            dqs.append(over_tokens(grad_scores, keys))
        dq_ref[...] = (jnp.where(low_half, dqs[0], dqs[1]) * scale).astype(BF16)
        dk_acc[...] += jnp.where(low_half, dks[0], dks[1]) * scale
        dv_acc[...] += jnp.where(low_half, dvs[0], dvs[1])

    @pl.when(flag_ref[0] == 1)
    def _():
        compute(False)

    @pl.when(flag_ref[0] != 1)
    def _():
        compute(True)

    @pl.when(step == last)
    def _():
        dk_ref[...] = dk_acc[...].astype(BF16)
        dv_ref[...] = dv_acc[...].astype(BF16)


def attend_back(flag, qkv, do, lse, id_col, id_row):
    tokens, width = qkv.shape[0], qkv.shape[1] // 3
    pairs = width // 128
    block = 256
    shape = jax.ShapeDtypeStruct((tokens, width), BF16)
    rows = pl.BlockSpec((block, 128), lambda h, i, f: (i, h))
    full = pl.BlockSpec((tokens, 128), lambda h, i, f: (0, h))
    return pl.pallas_call(
        attend_back_kernel,
        out_shape=(shape, shape, shape),
        grid_spec=pltpu.PrefetchScalarGridSpec(
            num_scalar_prefetch=1,
            grid=(width // 128, tokens // block),
            in_specs=[
                rows,
                pl.BlockSpec((tokens, 128), lambda h, i, f: (0, h + pairs)),
                pl.BlockSpec((tokens, 128), lambda h, i, f: (0, h + 2 * pairs)),
                rows, rows,
                pl.BlockSpec((tokens, 1), lambda h, i, f: (0, 0)),
                pl.BlockSpec((1, block), lambda h, i, f: (0, i)),
            ],
            out_specs=[rows, full, full],
            scratch_shapes=[pltpu.VMEM((tokens, 128), F32)] * 2,
        ),
        compiler_params=pltpu.CompilerParams(
            dimension_semantics=("arbitrary", "arbitrary"), vmem_limit_bytes=48 * 1024 * 1024
        ),
        name="attend_back",
    )(flag, qkv, qkv, qkv, do, lse, id_col, id_row)


def ffn_in_kernel(x_ref, w_ref, b_ref, active_ref, slope_ref):
    inner = matmul(x_ref[...], w_ref[...]) + b_ref[...]
    size = jnp.abs(inner) * (0.5**0.5)
    bell = jnp.exp(-0.5 * inner * inner)
    t = 1.0 / (1.0 + 0.3275911 * size)
    poly = 1.061405429 * t - 1.453152027
    poly = poly * t + 1.421413741
    poly = poly * t - 0.284496736
    poly = poly * t + 0.254829592
    tail = 0.5 * (poly * t) * bell
    below = jnp.where(inner >= 0.0, 1.0 - tail, tail)
    active_ref[...] = (inner * below).astype(BF16)
    slope_ref[...] = (below + inner * bell * 0.3989422804014327).astype(BF16)


def ffn_in(x, w, bias):
    tokens, depth = x.shape
    hidden = w.shape[1]
    rows, cols = 256, 512
    shape = jax.ShapeDtypeStruct((tokens, hidden), BF16)
    out = pl.BlockSpec((rows, cols), lambda n, m: (m, n))
    return pl.pallas_call(
        ffn_in_kernel,
        out_shape=(shape, shape),
        grid=(hidden // cols, tokens // rows),
        in_specs=[
            pl.BlockSpec((rows, depth), lambda n, m: (m, 0)),
            pl.BlockSpec((depth, cols), lambda n, m: (0, n)),
            pl.BlockSpec((1, cols), lambda n, m: (0, n)),
        ],
        out_specs=[out, out],
        compiler_params=pltpu.CompilerParams(
            dimension_semantics=("arbitrary", "arbitrary"), vmem_limit_bytes=48 * 1024 * 1024
        ),
        name="ffn_in",
    )(x, w, bias)


def exchange(values):
    pairs = [(r, r + 1 - 2 * (r % 2)) for r in range(8)]
    return lax.ppermute(values, "row", pairs)


def both(own):
    return jnp.concatenate([own, exchange(own)], axis=0)


def share_sum(left, weight, product):
    mate_part = rounded(product(left[512:], weight))
    other = exchange(mate_part)
    return product(left[:512], weight) + other.astype(F32)


def norm_rows(summed, gain, shift):
    center = jnp.mean(summed, axis=1, keepdims=True)
    spread = jnp.mean(summed * summed, axis=1, keepdims=True) - center * center
    inverse = lax.rsqrt(spread + EPSILON)
    normed = (summed - center) * inverse
    return normed * gain + shift, normed, inverse


def norm_rows_back(grad_output, normed, inverse, gain):
    scaled = grad_output * gain
    mean_one = jnp.mean(scaled, axis=1, keepdims=True)
    mean_two = jnp.mean(scaled * normed, axis=1, keepdims=True)
    grad_input = inverse * (scaled - mean_one - normed * mean_two)
    return grad_input, token_sum(grad_output * normed), token_sum(grad_output)


def fast_forward(hidden, weights, vectors, ids):
    wqkv, wproj, winner, wouter = weights
    flag, id_col, id_row = ids
    whole_in = both(rounded(hidden))
    qkv = rounded(matmul(whole_in, wqkv) + vectors["qkv"])
    attended, lse = attend(flag, qkv, id_col, id_row)
    branch = share_sum(attended, wproj, matmul) + vectors["proj"]
    first, normed_one, inverse_one = norm_rows(
        hidden + branch, vectors["attn_gain"], vectors["attn_shift"]
    )
    whole_mid = both(rounded(first))
    active, slope = ffn_in(whole_mid, winner, vectors["inner"])
    ffn = share_sum(active, wouter, matmul) + vectors["outer"]
    output, normed_two, inverse_two = norm_rows(
        first + ffn, vectors["ffn_gain"], vectors["ffn_shift"]
    )
    kept = (
        whole_in, qkv, lse, attended, normed_one, inverse_one,
        whole_mid, active, slope, normed_two, inverse_two,
    )
    return output, kept


def fast_backward(grad_output, kept, weights, vectors, ids):
    (
        whole_in, qkv, lse, attended, normed_one, inverse_one,
        whole_mid, active, slope, normed_two, inverse_two,
    ) = kept
    wqkv, wproj, winner, wouter = weights
    flag, id_col, id_row = ids
    grad_second, ffn_gain_sum, ffn_shift_sum = norm_rows_back(
        grad_output, normed_two, inverse_two, vectors["ffn_gain"]
    )
    ffn_low = rounded(grad_second)
    whole_second = both(ffn_low)
    inner_low = rounded(against(whole_second, wouter) * slope.astype(F32))
    outer_term = over_tokens(active, whole_second)
    grad_first = grad_second + share_sum(inner_low, winner, against)
    inner_term = over_tokens(whole_mid, inner_low)
    grad_attn, attn_gain_sum, attn_shift_sum = norm_rows_back(
        grad_first, normed_one, inverse_one, vectors["attn_gain"]
    )
    attn_low = rounded(grad_attn)
    whole_attn = both(attn_low)
    mixed_grad = rounded(against(whole_attn, wproj))
    proj_term = over_tokens(attended, whole_attn)
    grads = attend_back(flag, qkv, mixed_grad, lse, id_col, id_row)
    grad_qkv = jnp.concatenate(grads, axis=1)
    grad_input = grad_attn + share_sum(grad_qkv, wqkv, against)
    terms = (outer_term, inner_term, proj_term) + tuple(
        over_tokens(whole_in, part) for part in grads
    )
    small = (
        token_sum(grads[0]), token_sum(grads[2]), token_sum(attn_low),
        attn_gain_sum, attn_shift_sum, token_sum(inner_low), token_sum(ffn_low),
        ffn_gain_sum, ffn_shift_sum,
    )
    return grad_input, terms, small


VECTORS = (
    ("q", 256), ("v", 256), ("proj", 256), ("attn_gain", 256), ("attn_shift", 256),
    ("inner", 1024), ("outer", 256), ("ffn_gain", 256), ("ffn_shift", 256),
)
SPLIT = ("q", "v", "inner")


def fast_device(
    hidden_in,
    query_weight,
    key_weight,
    value_weight,
    query_bias,
    value_bias,
    proj_weight,
    proj_bias,
    attn_gain,
    attn_shift,
    inner_weight,
    inner_bias,
    outer_weight,
    outer_bias,
    ffn_gain,
    ffn_shift,
    segment_ids,
    grad_out,
):
    core = lax.axis_index("row") % 2
    depth = lax.axis_index("col")
    own_ids = segment_ids[0]
    mate_ids = exchange(own_ids)

    def big_start(ids):
        found = ids[:1025] == ids[1023:]
        return jnp.sum(jnp.where(found, jnp.arange(1025, dtype=jnp.int32), 0))

    own_start = big_start(own_ids)
    ids = jnp.where(depth // 2 == core, own_ids, mate_ids)
    ids = lax.dynamic_slice(
        jnp.concatenate([ids, ids[:1024]]), (big_start(ids),), (2048,)
    ).reshape(2, 2, 512)
    ids = lax.dynamic_index_in_dim(ids, depth % 2, 0, keepdims=False)
    ids = jnp.where(core == 0, ids, ids[::-1]).reshape(1024)
    flag = (1 - depth % 2).reshape(1).astype(jnp.int32)
    ids = (flag, ids[:, None], ids[None, :])

    def turned(values):
        longer = jnp.concatenate([values, values[:1024]], axis=0)
        return lax.dynamic_slice(longer, (own_start, 0), (2048, 256))

    def turned_back(values):
        longer = jnp.concatenate([values[1024:], values], axis=0)
        return lax.dynamic_slice(longer, (1024 - own_start, 0), (2048, 256)).astype(F32)

    small = jnp.concatenate(
        [
            query_bias, value_bias, proj_bias, attn_gain, attn_shift,
            inner_bias, outer_bias, ffn_gain, ffn_shift,
        ]
    ).reshape(24, 128)
    wqkv, wproj, winner, wouter, smalls, start_low, grad_low = gather_all(
        query_weight, key_weight, value_weight, proj_weight, inner_weight, outer_weight,
        small, turned(hidden_in), turned(grad_out),
    )
    weights = (wqkv, wproj, winner, wouter)
    smalls = smalls.reshape(4, 3072)
    vectors, offset = {}, 0
    for name, size in VECTORS:
        part = smalls[:, offset : offset + size]
        offset += size
        if name in SPLIT:
            part = jnp.where(core == 0, part[:, : size // 2], part[:, size // 2 :])
        vectors[name] = part.reshape(1, -1)
    vectors["qkv"] = jnp.concatenate(
        [vectors["q"], jnp.zeros_like(vectors["q"]), vectors["v"]], axis=1
    )

    middle, kept_one = fast_forward(start_low.astype(F32), weights, vectors, ids)
    final_out, kept_two = fast_forward(middle, weights, vectors, ids)
    grad_flow = grad_low.astype(F32)
    grad_flow, terms_two, small_two = fast_backward(grad_flow, kept_two, weights, vectors, ids)
    grad_flow, terms_one, small_one = fast_backward(grad_flow, kept_one, weights, vectors, ids)
    terms = [rounded(a + b) for a, b in zip(terms_two, terms_one)]
    pieces = []
    for (name, size), a, b in zip(VECTORS, small_two, small_one):
        total = a + b
        if name in SPLIT:
            half = total.reshape(4, 1, size // 2)
            zero = jnp.zeros_like(half)
            total = jnp.where(
                core == 0,
                jnp.concatenate([half, zero], axis=1),
                jnp.concatenate([zero, half], axis=1),
            )
        pieces.append(total.reshape(-1))
    small_sum = jnp.concatenate(pieces).reshape(96, 128)
    results = scatter_all(*terms, small_sum, rounded(final_out), rounded(grad_flow))
    outer_g, inner_g, proj_g, q_g, k_g, v_g, small_all, out_turned, grad_turned = results
    small_all = small_all.reshape(-1)
    sums, offset = {}, 0
    for name, size in VECTORS:
        sums[name] = lax.dynamic_slice(small_all, (offset + depth * size,), (size,))
        offset += 4 * size
    return (
        turned_back(out_turned),
        turned_back(grad_turned),
        q_g,
        k_g,
        v_g,
        sums["q"],
        sums["v"],
        proj_g,
        sums["proj"],
        sums["attn_gain"],
        sums["attn_shift"],
        inner_g,
        sums["inner"],
        outer_g,
        sums["outer"],
        sums["ffn_gain"],
        sums["ffn_shift"],
    )


def solution(mesh):
    in_specs = (
        P("row", "col"),
        P("row", "col"),
        P("row", "col"),
        P("row", "col"),
        P("col"),
        P("col"),
        P("col", "row"),
        P("col"),
        P("col"),
        P("col"),
        P("row", "col"),
        P("col"),
        P("col", "row"),
        P("col"),
        P("col"),
        P("col"),
        P("row", None),
        P("row", "col"),
    )
    out_specs = (
        P("row", "col"),
        P("row", "col"),
        P("row", "col"),
        P("row", "col"),
        P("row", "col"),
        P("col"),
        P("col"),
        P("col", "row"),
        P("col"),
        P("col"),
        P("col"),
        P("row", "col"),
        P("col"),
        P("col", "row"),
        P("col"),
        P("col"),
        P("col"),
    )
    same = dict(mesh.shape) == {"row": 8, "col": 4}
    return jax.shard_map(
        fast_device if same else general_device, mesh=mesh, in_specs=in_specs, out_specs=out_specs, check_vma=False
    )
```

```python
import functools

import jax
import jax.numpy as jnp
from jax import lax
from jax.experimental import pallas as pl
from jax.experimental.pallas import tpu as pltpu
from jax.sharding import PartitionSpec as P

NEG_FILL = -1e30
HEAD_DIM = 64
D = 1024
LEN = 2048
QBLOCK = 512
SEQS = 1


EPSILON = 1e-06


def rounded(values):
    return values.astype(jnp.bfloat16)


def matmul(left, right):
    return jnp.dot(left, right, preferred_element_type=jnp.float32)


def over_tokens(left, right):
    return lax.dot_general(
        left, right, (((0,), (0,)), ((), ())), preferred_element_type=jnp.float32
    )


def against(left, right):
    return lax.dot_general(
        left, right, (((1,), (1,)), ((), ())), preferred_element_type=jnp.float32
    )


def token_sum(values):
    return jnp.sum(values, axis=0, dtype=jnp.float32)


def exact_gelu(inputs):
    return jax.nn.gelu(inputs, approximate=False)


def gather_weights(shards):
    front_set = (
        lax.all_gather(shards[0], "row", axis=0, tiled=True),
        lax.all_gather(shards[1], "row", axis=0, tiled=True),
        lax.all_gather(shards[2], "row", axis=0, tiled=True),
        lax.all_gather(shards[3], "row", axis=0, tiled=True),
    )
    back_set = (
        lax.all_gather(shards[4], "row", axis=1, tiled=True),
        lax.all_gather(shards[5], "row", axis=1, tiled=True),
    )
    proj_cols = back_set[0]
    return (
        front_set[0],
        front_set[1],
        front_set[2],
        front_set[3],
        back_set[0],
        back_set[1],
        proj_cols,
    )


def spread_features(values):
    return lax.all_gather(rounded(values), "col", axis=1, tiled=True)


def sum_partials(partial_terms):
    return lax.psum_scatter(
        partial_terms.astype(jnp.bfloat16), "col", scatter_dimension=1, tiled=True
    ).astype(jnp.float32)


def spread_grads(values):
    return lax.all_gather(values, "col", axis=1, tiled=True)


def sum_grad_partials(partial_terms):
    return lax.psum_scatter(
        partial_terms.astype(jnp.bfloat16), "col", scatter_dimension=1, tiled=True
    ).astype(jnp.float32)


def norm_forward(summed, norm_gain, norm_shift):
    totals = lax.psum((jnp.sum(summed, axis=1), jnp.sum(summed * summed, axis=1)), "col")
    center = totals[0][:, None] / D
    spread = totals[1][:, None] / D - center * center
    inverse = lax.rsqrt(spread + EPSILON)
    normed = (summed - center) * inverse
    return (normed * norm_gain + norm_shift, normed, inverse)


def norm_backward(grad_output, normed, inverse, norm_gain):
    scaled = grad_output * norm_gain
    totals = lax.psum((jnp.sum(scaled, axis=1), jnp.sum(scaled * normed, axis=1)), "col")
    grad_input = inverse * (scaled - totals[0][:, None] / D - normed * (totals[1][:, None] / D))
    return (grad_input, jnp.sum(grad_output * normed, axis=0), jnp.sum(grad_output, axis=0))


def split_heads(values):
    return values.reshape(SEQS, LEN, values.shape[1] // HEAD_DIM, HEAD_DIM)


def attend_forward(queries, key_rows, value_rows, segments):
    score_scale = HEAD_DIM ** (-0.5)
    blocks = LEN // QBLOCK
    query_heads = split_heads(queries)
    key_heads = split_heads(key_rows)
    value_heads = split_heads(value_rows)

    def attend_one_block(block_index):
        sequence = block_index // blocks
        offset = block_index % blocks * QBLOCK
        seq_queries = lax.dynamic_index_in_dim(query_heads, sequence, 0, keepdims=False)
        seq_keys = lax.dynamic_index_in_dim(key_heads, sequence, 0, keepdims=False)
        seq_values = lax.dynamic_index_in_dim(value_heads, sequence, 0, keepdims=False)
        seq_segments = lax.dynamic_index_in_dim(segments, sequence, 0, keepdims=False)
        block_queries = lax.dynamic_slice_in_dim(seq_queries, offset, QBLOCK, 0)
        block_segments = lax.dynamic_slice_in_dim(seq_segments, offset, QBLOCK, 0)
        scores = (
            jnp.einsum("qhd,khd->hqk", block_queries, seq_keys, preferred_element_type=jnp.float32)
            * score_scale
        )
        same_doc = block_segments[:, None] == seq_segments[None, :]
        scores = jnp.where(same_doc[None], scores, NEG_FILL)
        highest = jnp.max(scores, axis=2, keepdims=True)
        weights = jnp.exp(scores - highest)
        totals = jnp.sum(weights, axis=2, keepdims=True)
        mixture = jnp.einsum(
            "hqk,khd->qhd",
            rounded(weights / totals),
            seq_values,
            preferred_element_type=jnp.float32,
        )
        return (mixture, (highest + jnp.log(totals))[:, :, 0])

    mixture, log_total = lax.map(attend_one_block, jnp.arange(SEQS * blocks))
    return (mixture.reshape(queries.shape), log_total)


def attend_backward(queries, key_rows, value_rows, segments, log_total, grad_mixed):
    score_scale = HEAD_DIM ** (-0.5)
    blocks = LEN // QBLOCK
    heads_here = queries.shape[1] // HEAD_DIM
    query_heads = split_heads(queries)
    key_heads = split_heads(key_rows)
    value_heads = split_heads(value_rows)
    grad_heads = split_heads(grad_mixed)
    lse_rows = log_total.reshape(SEQS, blocks, heads_here, QBLOCK)

    def one_sequence(sequence):
        seq_queries = lax.dynamic_index_in_dim(query_heads, sequence, 0, keepdims=False)
        seq_keys = lax.dynamic_index_in_dim(key_heads, sequence, 0, keepdims=False)
        seq_values = lax.dynamic_index_in_dim(value_heads, sequence, 0, keepdims=False)
        seq_grads = lax.dynamic_index_in_dim(grad_heads, sequence, 0, keepdims=False)
        seq_segments = lax.dynamic_index_in_dim(segments, sequence, 0, keepdims=False)
        seq_lse = lax.dynamic_index_in_dim(lse_rows, sequence, 0, keepdims=False)

        def one_one_block(carry, block_index):
            offset = block_index * QBLOCK
            block_queries = lax.dynamic_slice_in_dim(seq_queries, offset, QBLOCK, 0)
            block_grads = lax.dynamic_slice_in_dim(seq_grads, offset, QBLOCK, 0)
            block_segments = lax.dynamic_slice_in_dim(seq_segments, offset, QBLOCK, 0)
            block_lse = lax.dynamic_index_in_dim(seq_lse, block_index, 0, keepdims=False)
            scores = (
                jnp.einsum(
                    "qhd,khd->hqk", block_queries, seq_keys, preferred_element_type=jnp.float32
                )
                * score_scale
            )
            same_doc = block_segments[:, None] == seq_segments[None, :]
            scores = jnp.where(same_doc[None], scores, NEG_FILL)
            probs = jnp.exp(scores - block_lse[:, :, None])
            grad_probs = jnp.einsum(
                "qhd,khd->hqk", block_grads, seq_values, preferred_element_type=jnp.float32
            )
            grad_scores = rounded(
                probs * (grad_probs - jnp.sum(probs * grad_probs, axis=2, keepdims=True))
            )
            grad_query = (
                jnp.einsum(
                    "hqk,khd->qhd", grad_scores, seq_keys, preferred_element_type=jnp.float32
                )
                * score_scale
            )
            key_sum = (
                carry[0]
                + jnp.einsum(
                    "hqk,qhd->khd", grad_scores, block_queries, preferred_element_type=jnp.float32
                )
                * score_scale
            )
            value_sum = carry[1] + jnp.einsum(
                "hqk,qhd->khd", rounded(probs), block_grads, preferred_element_type=jnp.float32
            )
            return ((key_sum, value_sum), rounded(grad_query))

        zeros_init = jnp.zeros((LEN, heads_here, HEAD_DIM), jnp.float32)
        (key_sum, value_sum), grad_query = lax.scan(
            one_one_block, (zeros_init, zeros_init), jnp.arange(blocks)
        )
        return (grad_query.reshape(LEN, heads_here, HEAD_DIM), rounded(key_sum), rounded(value_sum))

    grad_query, grad_key, grad_value = lax.map(one_sequence, jnp.arange(SEQS))
    return (
        grad_query.reshape(queries.shape),
        grad_key.reshape(queries.shape),
        grad_value.reshape(queries.shape),
    )


def layer_forward(hidden, params, gathered, segments):
    query_w, key_w, value_w, inner_w, proj_w, outer_w, proj_cols = gathered
    whole_in = spread_features(hidden)
    queries = rounded(matmul(whole_in, query_w) + params[0])
    key_rows = rounded(matmul(whole_in, key_w))
    value_rows = rounded(matmul(whole_in, value_w) + params[1])
    mixture, log_total = attend_forward(queries, key_rows, value_rows, segments)
    attended = rounded(mixture)
    attn_branch = sum_partials(matmul(attended, proj_w)) + params[2]
    first_norm, normed_one, inverse_one = norm_forward(hidden + attn_branch, params[3], params[4])
    whole_mid = spread_features(first_norm)
    inner_act = matmul(whole_mid, inner_w) + params[5]
    active = rounded(exact_gelu(inner_act))
    ffn_branch = sum_partials(matmul(active, outer_w)) + params[6]
    output, normed_two, inverse_two = norm_forward(first_norm + ffn_branch, params[7], params[8])
    kept_values = (
        whole_in,
        queries,
        key_rows,
        value_rows,
        log_total,
        attended,
        normed_one,
        inverse_one,
        whole_mid,
        inner_act,
        active,
        normed_two,
        inverse_two,
    )
    return (output, kept_values)


def layer_backward(grad_output, kept_values, gathered, params, segments):
    (
        whole_in,
        queries,
        key_rows,
        value_rows,
        log_total,
        attended,
        normed_one,
        inverse_one,
        whole_mid,
        inner_act,
        active,
        normed_two,
        inverse_two,
    ) = kept_values
    query_w, key_w, value_w, inner_w, proj_w, outer_w, proj_cols = gathered
    grad_second, ffn_gain_sum, ffn_shift_sum = norm_backward(
        grad_output, normed_two, inverse_two, params[7]
    )
    ffn_low = rounded(grad_second)
    whole_second = spread_grads(ffn_low)
    outer_term = over_tokens(active, whole_second)
    active_grad = against(whole_second, outer_w)
    unused, pullback = jax.vjp(exact_gelu, inner_act)
    inner_low = rounded(pullback(active_grad)[0])
    inner_term = over_tokens(whole_mid, inner_low)
    grad_first = grad_second + sum_grad_partials(against(inner_low, inner_w))
    grad_attn, attn_gain_sum, attn_shift_sum = norm_backward(
        grad_first, normed_one, inverse_one, params[3]
    )
    attn_low = rounded(grad_attn)
    whole_attn = spread_grads(attn_low)
    proj_term = over_tokens(attended, whole_attn)
    mixed_grad = rounded(against(whole_attn, proj_w))
    query_low, key_low, value_low = attend_backward(
        queries, key_rows, value_rows, segments, log_total, mixed_grad
    )
    input_terms = (
        against(query_low, query_w) + against(key_low, key_w) + against(value_low, value_w)
    )
    grad_input = grad_attn + sum_grad_partials(input_terms)
    row_terms = (
        over_tokens(whole_in, query_low),
        over_tokens(whole_in, key_low),
        over_tokens(whole_in, value_low),
        inner_term,
    )
    col_terms = (proj_term, outer_term)
    small_terms = (
        token_sum(query_low),
        token_sum(value_low),
        token_sum(attn_low),
        attn_gain_sum,
        attn_shift_sum,
        token_sum(inner_low),
        token_sum(ffn_low),
        ffn_gain_sum,
        ffn_shift_sum,
    )
    return (grad_input, row_terms, col_terms, small_terms)


def general_device(
    hidden_in,
    query_weight,
    key_weight,
    value_weight,
    query_bias,
    value_bias,
    proj_weight,
    proj_bias,
    attn_gain,
    attn_shift,
    inner_weight,
    inner_bias,
    outer_weight,
    outer_bias,
    ffn_gain,
    ffn_shift,
    segment_ids,
    grad_out,
):
    shards = (query_weight, key_weight, value_weight, inner_weight, proj_weight, outer_weight)
    params = (
        query_bias,
        value_bias,
        proj_bias,
        attn_gain,
        attn_shift,
        inner_bias,
        outer_bias,
        ffn_gain,
        ffn_shift,
    )
    gathered = gather_weights(shards)
    start_in = hidden_in.astype(jnp.float32)
    middle, kept_one = layer_forward(start_in, params, gathered, segment_ids)
    final_out, kept_two = layer_forward(middle, params, gathered, segment_ids)
    kept = (kept_one, kept_two)
    grad_flow = grad_out.astype(jnp.float32)
    row_parts = []
    col_parts = []
    small_parts = []
    for layer_index in (1, 0):
        grad_flow, row_terms, col_terms, small_terms = layer_backward(
            grad_flow, kept[layer_index], gathered, params, segment_ids
        )
        row_parts.append(row_terms)
        col_parts.append(col_terms)
        small_parts.append(small_terms)
    row_sum = jax.tree.map(jnp.add, tuple(row_parts[0]), tuple(row_parts[1]))
    col_sum = jax.tree.map(jnp.add, tuple(col_parts[0]), tuple(col_parts[1]))
    small_sum = jax.tree.map(jnp.add, small_parts[0], small_parts[1])
    row_sum = (
        lax.psum_scatter(
            row_sum[0].astype(jnp.bfloat16), "row", scatter_dimension=0, tiled=True
        ).astype(jnp.float32),
        lax.psum_scatter(
            row_sum[1].astype(jnp.bfloat16), "row", scatter_dimension=0, tiled=True
        ).astype(jnp.float32),
        lax.psum_scatter(
            row_sum[2].astype(jnp.bfloat16), "row", scatter_dimension=0, tiled=True
        ).astype(jnp.float32),
        lax.psum_scatter(
            row_sum[3].astype(jnp.bfloat16), "row", scatter_dimension=0, tiled=True
        ).astype(jnp.float32),
    )
    col_sum = (
        lax.psum_scatter(
            col_sum[0].astype(jnp.bfloat16), "row", scatter_dimension=1, tiled=True
        ).astype(jnp.float32),
        lax.psum_scatter(
            col_sum[1].astype(jnp.bfloat16), "row", scatter_dimension=1, tiled=True
        ).astype(jnp.float32),
    )
    small_sum = lax.psum(
        (
            small_sum[0],
            small_sum[1],
            small_sum[2],
            small_sum[3],
            small_sum[4],
            small_sum[5],
            small_sum[6],
            small_sum[7],
            small_sum[8],
        ),
        "row",
    )
    return (
        final_out,
        grad_flow,
        row_sum[0],
        row_sum[1],
        row_sum[2],
        small_sum[0],
        small_sum[1],
        col_sum[0],
        small_sum[2],
        small_sum[3],
        small_sum[4],
        row_sum[3],
        small_sum[5],
        col_sum[1],
        small_sum[6],
        small_sum[7],
        small_sum[8],
    )


ANY = pl.BlockSpec(memory_space=pl.ANY)
VMEM = pl.BlockSpec(memory_space=pltpu.VMEM)
MESH = pl.DeviceIdType.MESH
DMA = pltpu.SemaphoreType.DMA
BF16 = jnp.bfloat16
F32 = jnp.float32


def place():
    row = lax.axis_index("row")
    depth = lax.axis_index("col")
    core = row % 2
    chip = row // 2
    x = chip % 2
    y = chip // 2
    return row, depth, core, chip, x, y


def remote(src, dst, send_sem, recv_sem, row, depth):
    return pltpu.make_async_remote_copy(
        src_ref=src,
        dst_ref=dst,
        send_sem=send_sem,
        recv_sem=recv_sem,
        device_id={"row": row, "col": depth},
        device_id_type=MESH,
    )


def span(start, size):
    return pl.ds(pl.multiple_of(start, 128), size)


def greet(row, depth, core, chip, x, y):
    barrier = pltpu.get_barrier_semaphore()
    mate = chip * 2 + (1 - core)
    friends = [(mate, depth)]
    for step in (1, 2, 3):
        friends.append((row, (depth + step) % 4))
        friends.append((mate, (depth + step) % 4))
    friends.append(((y * 2 + 1 - x) * 2 + core, depth))
    friends.append((((1 - y) * 2 + x) * 2 + core, depth))
    for r, d in friends:
        pl.semaphore_signal(
            barrier, inc=1, device_id={"row": r, "col": d}, device_id_type=MESH
        )
    pl.semaphore_wait(barrier, len(friends))


PIECES = 8
GROUPS = ((3,), (0,), (1,), (2,), (4,), (5,), (6,), (7,))


def gather_kernel(
    q_ref, k_ref, v_ref, proj_ref, inner_ref, outer_ref, small_ref, x_ref, g_ref,
    wqkv, wproj, winner, wouter, smalls, u_out, g_out,
    swap_s, swap_r, local_s, up_s, up_r, down_s, down_r, sm_s, sm_r,
    p1_s, p1_r, p2_s, p2_r, t_s, t_r, t_l,
):
    row, depth, core, chip, x, y = place()
    mate = chip * 2 + (1 - core)
    x_chip = y * 2 + 1 - x
    y_chip = (1 - y) * 2 + x
    x_row = x_chip * 2 + core
    y_row = y_chip * 2 + core
    greet(row, depth, core, chip, x, y)

    def swap_src(piece, half):
        if piece < 3:
            return (q_ref, k_ref, v_ref)[piece].at[:, span(half * 128, 128)]
        if piece == 3:
            return proj_ref.at[span(half * 128, 128), :]
        if piece < 6:
            return inner_ref.at[:, span(half * 512 + (piece - 4) * 256, 256)]
        return outer_ref.at[span(half * 512 + (piece - 6) * 256, 256), :]

    def cell(piece, start, size, origin):
        if piece < 3:
            return wqkv.at[span(start, size), span(piece * 512 + origin * 128, 128)]
        if piece == 3:
            return wproj.at[span(origin * 128, 128), span(start, size)]
        if piece < 6:
            return winner.at[
                span(start, size), span((piece - 4) * 1024 + origin * 256, 256)
            ]
        return wouter.at[span((piece - 6) * 1024 + origin * 256, 256), span(start, size)]

    def region(group, part, block):
        piece = GROUPS[group][0]
        if piece < 3:
            return wqkv.at[span(block * 256 + part * 128, 128), pl.ds(piece * 512, 512)]
        if piece == 3:
            return wproj.at[pl.ds(part * 256, 256), span(block * 256, 256)]
        if piece < 6:
            return winner.at[
                span(block * 256 + part * 128, 128), pl.ds((piece - 4) * 1024, 1024)
            ]
        return wouter.at[
            pl.ds((piece - 6) * 1024 + part * 512, 512), span(block * 256, 256)
        ]

    swaps, locals_ = [], []
    for piece in range(PIECES):
        target = cell(piece, row * 128, 128, depth)
        cp = remote(
            swap_src(piece, 1 - core), target, swap_s.at[piece], swap_r.at[piece], mate, depth
        )
        cp.start()
        swaps.append(cp)
        lc = pltpu.make_async_copy(swap_src(piece, core), target, local_s.at[piece])
        lc.start()
        locals_.append(lc)
    small_local = pltpu.make_async_copy(small_ref, smalls.at[depth], local_s.at[PIECES])
    small_local.start()

    def travel(piece, step, up):
        origin = depth - step if up else depth + step
        ref = cell(piece, chip * 256, 256, origin)
        send, recv = (up_s, up_r) if up else (down_s, down_r)
        return remote(
            ref, ref, send.at[piece, step], recv.at[piece, step], row,
            depth + 1 if up else depth - 1,
        )

    def depth_step(group, step):
        for piece in GROUPS[group]:
            if step == 0:
                swaps[piece].wait_recv()
                locals_[piece].wait()
            for up in (True, False):
                inside = depth - step >= 0 if up else depth + step <= 3
                ready = inside & (depth < 3 if up else depth > 0)
                if step > 0:

                    @pl.when(inside)
                    def _():
                        origin = depth - step if up else depth + step
                        ref = cell(piece, chip * 256, 256, origin)
                        recv = up_r if up else down_r
                        remote(
                            ref, ref, up_s.at[piece, step - 1], recv.at[piece, step - 1],
                            mate, depth,
                        ).wait_recv()

                if step < 3:

                    @pl.when(ready)
                    def _():
                        travel(piece, step, up).start()

    def depth_done():
        for piece in range(PIECES):
            for step in (0, 1, 2):
                for up in (True, False):
                    inside = depth - step >= 0 if up else depth + step <= 3

                    @pl.when(inside & (depth < 3 if up else depth > 0))
                    def _():
                        travel(piece, step, up).wait_send()

    def token_copies(index, src, dst):
        for j in range(4):
            to_core, to_depth = j % 2, core * 2 + j // 2
            mine = (to_core == core) & (to_depth == depth)
            source = src.at[pl.ds(j * 512, 512), :]
            target = dst.at[:, span(depth * 256, 256)]

            @pl.when(mine)
            def _():
                pltpu.make_async_copy(source, target, t_l.at[index]).start()

            @pl.when(jnp.logical_not(mine))
            def _():
                remote(
                    source, target, t_s.at[index, j], t_r.at[index, depth],
                    chip * 2 + to_core, to_depth,
                ).start()

    def token_waits(index, src, dst):
        from_core = depth // 2
        for s in range(4):
            mine = (from_core == core) & (s == depth)
            target = dst.at[:, pl.ds(s * 256, 256)]
            source = src.at[pl.ds(0, 512), :]

            @pl.when(mine)
            def _():
                pltpu.make_async_copy(source, target, t_l.at[index]).wait()

            @pl.when(jnp.logical_not(mine))
            def _():
                remote(
                    source, target, t_s.at[index, 0], t_r.at[index, s], mate, depth
                ).wait_recv()
        for j in range(4):
            to_core, to_depth = j % 2, core * 2 + j // 2
            mine = (to_core == core) & (to_depth == depth)

            @pl.when(jnp.logical_not(mine))
            def _():
                remote(
                    src.at[pl.ds(j * 512, 512), :], dst.at[:, pl.ds(0, 256)],
                    t_s.at[index, j], t_r.at[index, 0], mate, depth,
                ).wait_send()

    first, second = {}, {}

    def start_first(group):
        for part, target in ((0, x_row), (1, y_row)):
            cp = remote(
                region(group, part, chip), region(group, part, chip),
                p1_s.at[group, part], p1_r.at[group, part], target, depth,
            )
            cp.start()
            first[group, part] = cp

    def start_second(group):
        for part, target, other in ((0, y_row, x_chip), (1, x_row, y_chip)):
            first[group, part].wait_recv()
            for i, block in enumerate((chip, other)):
                cp = remote(
                    region(group, part, block), region(group, part, block),
                    p2_s.at[group, part, i], p2_r.at[group, part, i], target, depth,
                )
                cp.start()
                second[group, part, i] = cp

    count = len(GROUPS)
    small_copies = []
    for tick in range(count + 4):
        for step in (0, 1, 2, 3):
            group = tick - step
            if 0 <= group < count:
                depth_step(group, step)
                if step == 3:
                    start_first(group)
        if 0 <= tick - 4 < count:
            start_second(tick - 4)
        if tick == TOKEN_TICK:
            token_copies(0, x_ref, u_out)
        if tick == count - 1:
            for k in (1, 2, 3):
                cp = remote(
                    small_ref, smalls.at[depth], sm_s.at[k - 1], sm_r.at[k - 1],
                    row, (depth + k) % 4,
                )
                cp.start()
                small_copies.append(cp)
            token_copies(1, g_ref, g_out)
    token_waits(0, x_ref, u_out)
    token_waits(1, g_ref, g_out)
    for cp in small_copies:
        cp.wait()
    small_local.wait()
    depth_done()
    for cp in second.values():
        cp.wait()
    for cp in first.values():
        cp.wait_send()
    for cp in swaps:
        cp.wait_send()


TOKEN_TICK = 7


def gather_all(q, k, v, proj, inner, outer, small, x_rolled, g_rolled):
    sd = jax.ShapeDtypeStruct
    n = len(GROUPS)
    return pl.pallas_call(
        gather_kernel,
        out_shape=(
            sd((1024, 1536), BF16),
            sd((512, 1024), BF16),
            sd((1024, 2048), BF16),
            sd((2048, 1024), BF16),
            sd((4,) + small.shape, F32),
            sd((512, 1024), BF16),
            sd((512, 1024), BF16),
        ),
        in_specs=[VMEM] * 7 + [ANY] * 2,
        out_specs=[ANY] * 7,
        scratch_shapes=[
            DMA((PIECES,)), DMA((PIECES,)), DMA((PIECES + 1,)),
            DMA((PIECES, 3)), DMA((PIECES, 3)), DMA((PIECES, 3)), DMA((PIECES, 3)),
            DMA((3,)), DMA((3,)),
            DMA((n, 2)), DMA((n, 2)), DMA((n, 2, 2)), DMA((n, 2, 2)),
            DMA((2, 4)), DMA((2, 4)), DMA((2,)),
        ],
        compiler_params=pltpu.CompilerParams(collective_id=1, has_side_effects=True),
    )(q, k, v, proj, inner, outer, small, x_rolled, g_rolled)


SHAPES = ((256, 256), (128, 512), (128, 512), (128, 512))
UNITS = ((128, 256), (256, 128), (256, 128), (256, 128), (256, 256), (256, 256))
FULLS = ((512, 256), (256, 512), (256, 512), (256, 512))
OUTS = ((256, 128), (128, 256), (128, 256), (128, 256), (128, 1024), (1024, 128))
HALVES = ((128, 128), (128, 128), (128, 128), (128, 128), (128, 256), (128, 256), (512, 128))
BY_COLS = (True, False, False, False, False, False)
OUTER = 6


def add_rows(dst, terms):
    rows = dst.shape[0]
    step = 32

    def body(i, carry):
        sl = pl.ds(pl.multiple_of(i * step, step), step)
        total = terms[0][sl, :].astype(F32)
        for term in terms[1:]:
            total = total + term[sl, :].astype(F32)
        dst[sl, :] = total.astype(dst.dtype)
        return carry

    lax.fori_loop(0, rows // step, body, 0)


def scatter_kernel(*refs):
    grads = refs[0:4]
    inner_ref = refs[4:6]
    outer_ref, small_ref, gi_ref = refs[6:9]
    outs = refs[9:15]
    small_out, gi_out = refs[15:17]
    rest = list(refs[17:])
    own = [[rest.pop(0) for _ in range(2)] for _ in range(4)]
    got1 = [[rest.pop(0) for _ in range(2)] for _ in range(4)]
    got2 = [[rest.pop(0) for _ in range(2)] for _ in range(4)]
    full = [rest.pop(0) for _ in range(4)]
    zgot = [rest.pop(0) for _ in range(6)]
    fin = [rest.pop(0) for _ in range(6)]
    cgot = [rest.pop(0) for _ in range(7)]
    sb = rest.pop(0)
    sg = rest.pop(0)
    (o_s, p1_s, p1_r, p2_s, p2_r, z_s, z_r, c_s, c_r, sm_s, sm_r, t_s, t_r, t_l) = rest

    row, depth, core, chip, x, y = place()
    mate = chip * 2 + (1 - core)
    x_row = (y * 2 + 1 - x) * 2 + core
    y_row = ((1 - y) * 2 + x) * 2 + core
    greet(row, depth, core, chip, x, y)

    def region(group, part, block):
        rows = SHAPES[group][0]
        if BY_COLS[group]:
            return grads[group].at[pl.ds(part * rows, rows), span(block * 256, 256)]
        return grads[group].at[span(block * 256 + part * 128, 128), :]

    def unit(group, z):
        if group >= 4:
            return inner_ref[group - 4].at[:, span(z * 256, 256)]
        if BY_COLS[group]:
            return full[group].at[span(z * UNITS[group][0], UNITS[group][0]), :]
        return full[group].at[:, span(z * UNITS[group][1], UNITS[group][1])]

    def side(group, half):
        if group == OUTER:
            return outer_ref.at[:, span(half * 128, 128)]
        if BY_COLS[group]:
            return fin[group].at[:, span(half * 128, 128)]
        return fin[group].at[span(half * 128, 128), :]

    def out_side(group, half):
        if group == OUTER:
            return outs[5].at[span(half * 512, 512), :]
        if group >= 4:
            return outs[4].at[:, span(half * 512 + (group - 4) * 256, 256)]
        size = HALVES[group]
        if BY_COLS[group]:
            return outs[group].at[span(half * size[0], size[0]), :]
        return outs[group].at[:, span(half * size[1], size[1])]

    copies = {}

    def start_first(group):
        for part in (0, 1):
            target = y_row if part == 0 else x_row
            for i in (0, 1):
                kept = y * 2 + i if part == 0 else i * 2 + x
                sent = (1 - y) * 2 + i if part == 0 else i * 2 + (1 - x)
                lc = pltpu.make_async_copy(
                    region(group, part, kept), own[group][part].at[i], o_s.at[group, part, i]
                )
                lc.start()
                cp = remote(
                    region(group, part, sent), got1[group][part].at[i],
                    p1_s.at[group, part, i], p1_r.at[group, part, i], target, depth,
                )
                cp.start()
                copies["o", group, part, i] = lc
                copies["p1", group, part, i] = cp

    def start_second(group):
        for part in (0, 1):
            target = x_row if part == 0 else y_row
            mine = x if part == 0 else y
            for i in (0, 1):
                copies["o", group, part, i].wait()
                copies["p1", group, part, i].wait_recv()
            other = own[group][part].at[1 - mine]
            add_rows(other, (other, got1[group][part].at[1 - mine]))
            cp = remote(
                other, got2[group][part], p2_s.at[group, part], p2_r.at[group, part], target, depth
            )
            cp.start()
            copies["p2", group, part] = cp

    def send_depth(group):
        for k in (1, 2, 3):
            cp = remote(
                unit(group, (depth + k) % 4), zgot[group].at[k - 1],
                z_s.at[group, k - 1], z_r.at[group, k - 1], row, (depth + k) % 4,
            )
            cp.start()
            copies["z", group, k] = cp

    def start_depth(group):
        rows = SHAPES[group][0]
        for part in (0, 1):
            mine = x if part == 0 else y
            copies["p2", group, part].wait_recv()
            add_rows(
                full[group].at[pl.ds(part * rows, rows), :],
                (own[group][part].at[mine], got1[group][part].at[mine], got2[group][part]),
            )
        send_depth(group)

    def send_core(group):
        cp = remote(
            side(group, 1 - core), cgot[group], c_s.at[group], c_r.at[group], mate, depth
        )
        cp.start()
        copies["c", group] = cp

    def start_core(group):
        for k in (1, 2, 3):
            copies["z", group, k].wait_recv()
        add_rows(
            fin[group],
            (unit(group, depth), zgot[group].at[0], zgot[group].at[1], zgot[group].at[2]),
        )
        send_core(group)

    def finish(group):
        add_rows(out_side(group, core), (side(group, core),))
        copies["c", group].wait_recv()
        add_rows(out_side(group, 1 - core), (cgot[group],))

    def token_copies(index, src, dst):
        j = (depth % 2) * 2 + core
        to_core = depth // 2
        for z in range(4):
            mine = (to_core == core) & (z == depth)
            source = src.at[:, pl.ds(z * 256, 256)]
            target = dst.at[span(j * 512, 512), :]

            @pl.when(mine)
            def _():
                pltpu.make_async_copy(source, target, t_l.at[index]).start()

            @pl.when(jnp.logical_not(mine))
            def _():
                remote(
                    source, target, t_s.at[index, z], t_r.at[index, j], chip * 2 + to_core, z
                ).start()

    def token_waits(index, src, dst):
        to_core = depth // 2
        for j in range(4):
            from_core, from_depth = j % 2, core * 2 + j // 2
            mine = (from_core == core) & (from_depth == depth)
            target = dst.at[pl.ds(j * 512, 512), :]
            source = src.at[:, pl.ds(0, 256)]

            @pl.when(mine)
            def _():
                pltpu.make_async_copy(source, target, t_l.at[index]).wait()

            @pl.when(jnp.logical_not(mine))
            def _():
                remote(
                    source, target, t_s.at[index, 0], t_r.at[index, j], mate, depth
                ).wait_recv()
        for z in range(4):
            mine = (to_core == core) & (z == depth)

            @pl.when(jnp.logical_not(mine))
            def _():
                remote(
                    src.at[:, pl.ds(z * 256, 256)], dst.at[pl.ds(0, 512), :],
                    t_s.at[index, z], t_r.at[index, 0], mate, depth,
                ).wait_send()

    def small_send(step, slot, target_row, target_depth):
        cp = remote(
            sb.at[step], sg.at[slot], sm_s.at[slot], sm_r.at[slot], target_row, target_depth
        )
        cp.start()
        copies["s", slot] = cp

    def small_add(step, slot):
        copies["s", slot].wait_recv()
        sb[step + 1] = sb[step] + sg[slot]

    sb[0] = small_ref[...]
    for group in range(4):
        start_first(group)
    small_send(0, 0, mate, depth)
    send_core(OUTER)
    send_depth(4)
    send_depth(5)
    token_copies(0, gi_ref, gi_out)
    small_add(0, 0)
    small_send(1, 1, x_row, depth)
    finish(OUTER)
    for group in range(4):
        start_second(group)
        if group == 0:
            small_add(1, 1)
            small_send(2, 2, y_row, depth)
        if group > 0:
            start_depth(group - 1)
    small_add(2, 2)
    for k in (1, 2, 3):
        small_send(3, 2 + k, row, (depth + k) % 4)
    start_depth(3)
    for group in (4, 5):
        start_core(group)
    for group in (0, 1, 2):
        start_core(group)
    for k in (1, 2, 3):
        copies["s", 2 + k].wait_recv()
    small_out[...] = ((sb[3] + sg[3]) + sg[4]) + sg[5]
    for group in (4, 5, 0, 1, 2):
        finish(group)
    start_core(3)
    token_waits(0, gi_ref, gi_out)
    finish(3)
    for key, cp in copies.items():
        if key[0] != "o":
            cp.wait_send()


def scatter_all(proj, q, k, v, inner_a, inner_b, outer, small, gi):
    sd = jax.ShapeDtypeStruct
    scratch = []
    for size in SHAPES:
        scratch += [pltpu.VMEM((2,) + size, BF16)] * 2
    for size in SHAPES:
        scratch += [pltpu.VMEM((2,) + size, BF16)] * 2
    for size in SHAPES:
        scratch += [pltpu.VMEM(size, BF16)] * 2
    scratch += [pltpu.VMEM(size, BF16) for size in FULLS]
    scratch += [pltpu.VMEM((3,) + size, BF16) for size in UNITS]
    scratch += [pltpu.VMEM(size, BF16) for size in UNITS]
    scratch += [pltpu.VMEM(size, BF16) for size in HALVES]
    scratch += [pltpu.VMEM((4,) + small.shape, F32), pltpu.VMEM((6,) + small.shape, F32)]
    scratch += [
        DMA((4, 2, 2)), DMA((4, 2, 2)), DMA((4, 2, 2)), DMA((4, 2)), DMA((4, 2)),
        DMA((6, 3)), DMA((6, 3)), DMA((7,)), DMA((7,)), DMA((6,)), DMA((6,)),
        DMA((1, 4)), DMA((1, 4)), DMA((1,)),
    ]
    return pl.pallas_call(
        scatter_kernel,
        out_shape=tuple(sd(size, F32) for size in OUTS)
        + (sd(small.shape, F32), sd((2048, 256), BF16)),
        in_specs=[ANY] * 4 + [VMEM] * 4 + [ANY],
        out_specs=[VMEM] * 7 + [ANY],
        scratch_shapes=scratch,
        compiler_params=pltpu.CompilerParams(
            collective_id=2, has_side_effects=True, vmem_limit_bytes=48 * 1024 * 1024
        ),
    )(proj, q, k, v, inner_a, inner_b, outer, small, gi)


def attend_kernel(flag_ref, q_ref, k_ref, v_ref, idq_ref, idk_ref, o_ref, lse_ref):
    rows = q_ref.shape[0]
    lane = lax.broadcasted_iota(jnp.int32, (1, 128), 1)
    low_half = lane < HEAD_DIM

    def compute(masked):
        keys = k_ref[...]
        values = v_ref[...]
        halves = (low_half, jnp.logical_not(low_half))
        sub = 256
        units = [(i, h) for i in range(rows // sub) for h in (0, 1)]

        def score(unit):
            i, h = unit
            scaled = q_ref[i * sub : (i + 1) * sub, :] * jnp.asarray(HEAD_DIM**-0.5, BF16)
            s = against(jnp.where(halves[h], scaled, jnp.zeros_like(scaled)), keys)
            if masked:
                s = jnp.where(idq_ref[i * sub : (i + 1) * sub, :] == idk_ref[...], s, NEG_FILL)
            return s

        def soft(s):
            top = jnp.max(s, axis=1, keepdims=True)
            weights = jnp.exp(s - top)
            return weights.astype(BF16), jnp.sum(weights, axis=1, keepdims=True), top

        skew = 1
        pending = [score(u) for u in units[:skew]]
        done = {}
        for n, unit in enumerate(units):
            if n + skew < len(units):
                pending.append(score(units[n + skew]))
            low, total, top = soft(pending.pop(0))
            mixed = matmul(low, values)
            done[unit] = (mixed / total, top + jnp.log(total))
            i, h = unit
            if h == 1:
                sl = slice(i * sub, (i + 1) * sub)
                a, b = done[i, 0], done[i, 1]
                o_ref[sl, :] = jnp.where(low_half, a[0], b[0]).astype(o_ref.dtype)
                lse_ref[sl, :] = jnp.where(low_half, a[1], b[1])

    @pl.when(flag_ref[0] == 1)
    def _():
        compute(False)

    @pl.when(flag_ref[0] != 1)
    def _():
        compute(True)


def attend(flag, qkv, id_col, id_row):
    tokens, width = qkv.shape[0], qkv.shape[1] // 3
    pairs = width // 128
    block = tokens
    return pl.pallas_call(
        attend_kernel,
        out_shape=(
            jax.ShapeDtypeStruct((tokens, width), BF16),
            jax.ShapeDtypeStruct((tokens, width), F32),
        ),
        grid_spec=pltpu.PrefetchScalarGridSpec(
            num_scalar_prefetch=1,
            grid=(width // 128, tokens // block),
            in_specs=[
                pl.BlockSpec((block, 128), lambda h, i, f: (i, h)),
                pl.BlockSpec((tokens, 128), lambda h, i, f: (0, h + pairs)),
                pl.BlockSpec((tokens, 128), lambda h, i, f: (0, h + 2 * pairs)),
                pl.BlockSpec((block, 1), lambda h, i, f: (i, 0)),
                pl.BlockSpec((1, tokens), lambda h, i, f: (0, 0)),
            ],
            out_specs=[
                pl.BlockSpec((block, 128), lambda h, i, f: (i, h)),
                pl.BlockSpec((block, 128), lambda h, i, f: (i, h)),
            ],
        ),
        compiler_params=pltpu.CompilerParams(
            dimension_semantics=("arbitrary", "arbitrary"), vmem_limit_bytes=48 * 1024 * 1024
        ),
        cost_estimate=pl.CostEstimate(
            flops=20_000_000_000, bytes_accessed=8_000_000, transcendentals=0
        ),
        name="attend",
    )(flag, qkv, qkv, qkv, id_col, id_row)


def attend_back_kernel(
    flag_ref, q_ref, k_ref, v_ref, do_ref, lse_ref, idk_ref, idq_ref,
    dq_ref, dk_ref, dv_ref,
):
    rows = q_ref.shape[0]
    scale = HEAD_DIM**-0.5
    lane = lax.broadcasted_iota(jnp.int32, (1, 128), 1)
    low_half = lane < HEAD_DIM

    def compute(masked):
        queries = q_ref[...]
        scaled = queries * jnp.asarray(scale, BF16)
        keys = k_ref[...]
        values = v_ref[...]
        grads = do_ref[...]
        lse_t = lse_ref[...].T
        q_t, k_t, do_t = queries.T, keys.T, grads.T
        dqs, dks, dvs = [], [], []
        for head in (0, 1):
            here = low_half if head == 0 else jnp.logical_not(low_half)
            part = slice(head * HEAD_DIM, (head + 1) * HEAD_DIM)
            zero = jnp.zeros_like(keys)
            scores = against(jnp.where(here, keys, zero), scaled)
            if masked:
                scores = jnp.where(idk_ref[...] == idq_ref[...], scores, NEG_FILL)
            log_row = lse_t[head * HEAD_DIM : head * HEAD_DIM + 1, :]
            probs = jnp.exp(scores - log_row)
            grad_probs = against(jnp.where(here, values, zero), grads)
            moved = probs * grad_probs
            delta = jnp.sum(moved, axis=0, keepdims=True)
            grad_scores = (moved - probs * delta).astype(BF16)
            low = probs.astype(BF16)
            dvs.append(against(do_t[part], low))
            dks.append(matmul(grad_scores, queries))
            dqs.append(matmul(k_t[part], grad_scores))
        dv_ref[...] = jnp.concatenate(dvs, axis=0).T.astype(BF16)
        dk_ref[...] = (jnp.where(low_half, dks[0], dks[1]) * scale).astype(BF16)
        dq_ref[...] = (jnp.concatenate(dqs, axis=0) * scale).T.astype(BF16)

    @pl.when(flag_ref[0] == 1)
    def _():
        compute(False)

    @pl.when(flag_ref[0] != 1)
    def _():
        compute(True)


def attend_back(flag, qkv, do, lse, id_col, id_row, first=0, count=4):
    tokens, width = qkv.shape[0], qkv.shape[1] // 3
    pairs = width // 128
    block = tokens
    shape = jax.ShapeDtypeStruct((tokens, count * 128), BF16)
    rows = pl.BlockSpec((block, 128), lambda h, i, f: (i, h + first))
    return pl.pallas_call(
        attend_back_kernel,
        out_shape=(shape, shape, shape),
        grid_spec=pltpu.PrefetchScalarGridSpec(
            num_scalar_prefetch=1,
            grid=(count, tokens // block),
            in_specs=[
                rows,
                pl.BlockSpec((tokens, 128), lambda h, i, f: (0, h + first + pairs)),
                pl.BlockSpec((tokens, 128), lambda h, i, f: (0, h + first + 2 * pairs)),
                rows, rows,
                pl.BlockSpec((tokens, 1), lambda h, i, f: (0, 0)),
                pl.BlockSpec((1, block), lambda h, i, f: (0, i)),
            ],
            out_specs=[
                pl.BlockSpec((block, 128), lambda h, i, f: (i, h)),
                pl.BlockSpec((tokens, 128), lambda h, i, f: (0, h)),
                pl.BlockSpec((tokens, 128), lambda h, i, f: (0, h)),
            ],
        ),
        compiler_params=pltpu.CompilerParams(
            dimension_semantics=("arbitrary", "arbitrary"), vmem_limit_bytes=48 * 1024 * 1024
        ),
        cost_estimate=pl.CostEstimate(
            flops=10_000_000_000 * count, bytes_accessed=2_500_000 * count, transcendentals=0
        ),
        name="attend_back",
    )(flag, qkv, qkv, qkv, do, lse, id_col, id_row)


def gelu_pair(inner):
    size = jnp.abs(inner)
    bell = jnp.exp(inner * (inner * -0.5))
    t = 1.0 / (1.0 + (0.3275911 * 0.5**0.5) * size)
    poly = (0.5 * 1.061405429) * t - 0.5 * 1.453152027
    poly = poly * t + 0.5 * 1.421413741
    poly = poly * t - 0.5 * 0.284496736
    poly = poly * t + 0.5 * 0.254829592
    tail = (poly * t) * bell
    below = jnp.where(inner >= 0.0, 1.0 - tail, tail)
    return (inner * below).astype(BF16), (below + inner * (bell * 0.3989422804014327)).astype(BF16)


def ffn_in_kernel(x_ref, w_ref, b_ref, active_ref, slope_ref):
    rows, cols = active_ref.shape
    sub = 128
    skew = 1

    def open_unit(i):
        return matmul(x_ref[i * sub : (i + 1) * sub, :], w_ref[...]) + b_ref[...]

    count = rows // sub
    pending = [open_unit(i) for i in range(skew)]
    for i in range(count):
        if i + skew < count:
            pending.append(open_unit(i + skew))
        active, slope = gelu_pair(pending.pop(0))
        active_ref[i * sub : (i + 1) * sub, :] = active
        slope_ref[i * sub : (i + 1) * sub, :] = slope


def ffn_in(x, w, bias):
    tokens, depth = x.shape
    hidden = w.shape[1]
    rows, cols = 1024, 512
    shape = jax.ShapeDtypeStruct((tokens, hidden), BF16)
    out = pl.BlockSpec((rows, cols), lambda n, m: (m, n))
    return pl.pallas_call(
        ffn_in_kernel,
        out_shape=(shape, shape),
        grid=(hidden // cols, tokens // rows),
        in_specs=[
            pl.BlockSpec((rows, depth), lambda n, m: (m, 0)),
            pl.BlockSpec((depth, cols), lambda n, m: (0, n)),
            pl.BlockSpec((1, cols), lambda n, m: (0, n)),
        ],
        out_specs=[out, out],
        compiler_params=pltpu.CompilerParams(
            dimension_semantics=("arbitrary", "arbitrary"), vmem_limit_bytes=48 * 1024 * 1024
        ),
        cost_estimate=pl.CostEstimate(
            flops=14_000_000_000, bytes_accessed=14_000_000, transcendentals=0
        ),
        name="ffn_in",
    )(x, w, bias)


def exchange(values):
    pairs = [(r, r + 1 - 2 * (r % 2)) for r in range(8)]
    return lax.ppermute(values, "row", pairs)


def both(own):
    return jnp.concatenate([own, exchange(own)], axis=0)


def share_sum(left, weight, product):
    mate_part = rounded(product(left[512:], weight))
    other = exchange(mate_part)
    return product(left[:512], weight) + other.astype(F32)


def norm_rows(summed, gain, shift):
    center = jnp.mean(summed, axis=1, keepdims=True)
    spread = jnp.mean(summed * summed, axis=1, keepdims=True) - center * center
    inverse = lax.rsqrt(spread + EPSILON)
    normed = (summed - center) * inverse
    return normed * gain + shift, normed, inverse


def norm_rows_back(grad_output, normed, inverse, gain):
    scaled = grad_output * gain
    mean_one = jnp.mean(scaled, axis=1, keepdims=True)
    mean_two = jnp.mean(scaled * normed, axis=1, keepdims=True)
    grad_input = inverse * (scaled - mean_one - normed * mean_two)
    return grad_input, token_sum(grad_output * normed), token_sum(grad_output)


def fast_forward(hidden, weights, vectors, ids):
    wqkv, wproj, winner, wouter = weights
    flag, id_col, id_row = ids
    whole_in = both(rounded(hidden))
    qkv = rounded(matmul(whole_in, wqkv) + vectors["qkv"])
    attended, lse = attend(flag, qkv, id_col, id_row)
    branch = share_sum(attended, wproj, matmul) + vectors["proj"]
    first, normed_one, inverse_one = norm_rows(
        hidden + branch, vectors["attn_gain"], vectors["attn_shift"]
    )
    whole_mid = both(rounded(first))
    active, slope = ffn_in(whole_mid, winner, vectors["inner"])
    ffn = share_sum(active, wouter, matmul) + vectors["outer"]
    output, normed_two, inverse_two = norm_rows(
        first + ffn, vectors["ffn_gain"], vectors["ffn_shift"]
    )
    kept = (
        whole_in, qkv, lse, attended, normed_one, inverse_one,
        whole_mid, active, slope, normed_two, inverse_two,
    )
    return output, kept


def fast_backward(grad_output, kept, weights, vectors, ids, later=None):
    (
        whole_in, qkv, lse, attended, normed_one, inverse_one,
        whole_mid, active, slope, normed_two, inverse_two,
    ) = kept
    wqkv, wproj, winner, wouter = weights
    flag, id_col, id_row = ids
    grad_second, ffn_gain_sum, ffn_shift_sum = norm_rows_back(
        grad_output, normed_two, inverse_two, vectors["ffn_gain"]
    )
    ffn_low = rounded(grad_second)
    whole_second = both(ffn_low)
    inner_low = rounded(against(whole_second, wouter) * slope.astype(F32))
    relative_second = by_place(whole_second)
    outer_terms = outer_pieces(active, relative_second)
    grad_first = grad_second + share_sum(inner_low, winner, against)
    inner_terms = inner_pieces(by_place(whole_mid), inner_low)
    grad_attn, attn_gain_sum, attn_shift_sum = norm_rows_back(
        grad_first, normed_one, inverse_one, vectors["attn_gain"]
    )
    attn_low = rounded(grad_attn)
    whole_attn = both(attn_low)
    mixed_grad = rounded(against(whole_attn, wproj))
    proj_term = over_tokens(attended, whole_attn)
    if later is None:
        grads = attend_back(flag, qkv, mixed_grad, lse, id_col, id_row)
    else:
        outer_terms = add_trees(outer_terms, later[0])
        inner_terms = add_trees(inner_terms, later[1])
        planes = [Plane(outer_terms, h, 1) for h in (0, 1)] + [
            Plane(inner_terms, h, 0) for h in (0, 1)
        ]
        sent, mixed_grad = lax.optimization_barrier(([p.sent for p in planes], mixed_grad))
        got = [p.step_one(s) for p, s in zip(planes, sent)]
        early = attend_back(flag, qkv, mixed_grad, lse, id_col, id_row, 0, 2)
        got, early = lax.optimization_barrier((got, early))
        handed = [p.to_hand(g) for p, g in zip(planes, got)]
        handed, mixed_grad = lax.optimization_barrier((handed, mixed_grad))
        more = [p.step_two(v) for p, v in zip(planes, handed)]
        late = attend_back(flag, qkv, mixed_grad, lse, id_col, id_row, 2, 2)
        more, late = lax.optimization_barrier((more, late))
        folded = [p.close(m) for p, m in zip(planes, more)]
        outer_terms = fold_depth(folded[:2])
        inner_terms = folded[2:]
        grads = tuple(jnp.concatenate(pair, axis=1) for pair in zip(early, late))
    grad_qkv = jnp.concatenate(grads, axis=1)
    grad_input = grad_attn + share_sum(grad_qkv, wqkv, against)
    terms = (proj_term,) + tuple(
        over_tokens(whole_in, part) for part in grads
    )
    small = (
        token_sum(grads[0]), token_sum(grads[2]), token_sum(attn_low),
        attn_gain_sum, attn_shift_sum, token_sum(inner_low), token_sum(ffn_low),
        ffn_gain_sum, ffn_shift_sum,
    )
    return grad_input, terms, outer_terms, inner_terms, small


def flip_row(bit):
    return [(r, r + bit - 2 * bit * ((r // bit) % 2)) for r in range(8)]


def by_place(values):
    chip = lax.axis_index("row") // 2
    x, y = chip % 2, chip // 2

    def block(yy, xx):
        return lax.dynamic_slice_in_dim(values, (yy * 2 + xx) * 256, 256, 1)

    far = block(1 - y, 1 - x)
    return jnp.concatenate(
        [block(y, 1 - x), block(y, x), block(1 - y, x), far, block(y, 1 - x)], axis=1
    )


CUTS = (((512, 1024), (0, 256), (256, 512)), ((768, 1280), (512, 768), (256, 512)))


def outer_pieces(active, relative):
    return [
        [over_tokens(active[:, h * 1024 : (h + 1) * 1024], relative[:, a:b]) for a, b in CUTS[h]]
        for h in (0, 1)
    ]


def inner_pieces(relative, inner_low):
    return [
        [over_tokens(relative[:, a:b], inner_low[:, h * 1024 : (h + 1) * 1024]) for a, b in CUTS[h]]
        for h in (0, 1)
    ]


def add_trees(left, right):
    return jax.tree.map(lambda p, q: p + q, left, right)


class Plane:
    def __init__(self, pieces, half, axis):
        sent, self.handed, self.own = pieces[half]
        self.sent = rounded(sent)
        self.half, self.axis = half, axis
        self.first, self.second = (4, 2) if half == 0 else (2, 4)

    def step_one(self, sent):
        return lax.ppermute(sent, "row", flip_row(self.first))

    def to_hand(self, got):
        low, high = jnp.split(got, 2, axis=self.axis)
        self.got, handed = (low, high) if self.half == 0 else (high, low)
        return rounded(self.handed + handed.astype(F32))

    def step_two(self, handed):
        return lax.ppermute(handed, "row", flip_row(self.second))

    def close(self, more):
        return rounded(self.own + self.got.astype(F32) + more.astype(F32))


def fold_depth(halves):
    depth = lax.axis_index("col")
    stacked = [half.reshape(4, 256, 256) for half in halves]

    def unit(z):
        picked = [lax.dynamic_index_in_dim(s, z, 0, keepdims=False) for s in stacked]
        return jnp.concatenate(picked, axis=0)

    total = unit(depth).astype(F32)
    for k in (1, 2, 3):
        pairs = [(z, (z + k) % 4) for z in range(4)]
        total = total + lax.ppermute(unit((depth + k) % 4), "col", pairs).astype(F32)
    return rounded(total)


def spread_out(values, own_start):
    core = lax.axis_index("row") % 2
    depth = lax.axis_index("col")
    j = (depth % 2) * 2 + core
    parts = []
    for k in range(4):
        pairs = []
        for r in range(8):
            for z in range(4):
                block = ((z % 2) * 2 + r % 2 + k) % 4
                pairs.append((r * 4 + z, (r // 2 * 2 + z // 2) * 4 + block))
        piece = lax.dynamic_slice_in_dim(values, ((j + k) % 4) * 256, 256, 1)
        parts.append(lax.ppermute(piece, ("row", "col"), pairs))
    cycle = jnp.concatenate(parts[::-1] * 2, axis=0)
    start = ((3 - depth) * 512 - own_start + 2048) % 2048
    return lax.dynamic_slice(cycle, (start, 0), (2048, 256)).astype(F32)


VECTORS = (
    ("q", 256), ("v", 256), ("proj", 256), ("attn_gain", 256), ("attn_shift", 256),
    ("inner", 1024), ("outer", 256), ("ffn_gain", 256), ("ffn_shift", 256),
)
SPLIT = ("q", "v", "inner")


def fast_device(
    hidden_in,
    query_weight,
    key_weight,
    value_weight,
    query_bias,
    value_bias,
    proj_weight,
    proj_bias,
    attn_gain,
    attn_shift,
    inner_weight,
    inner_bias,
    outer_weight,
    outer_bias,
    ffn_gain,
    ffn_shift,
    segment_ids,
    grad_out,
):
    core = lax.axis_index("row") % 2
    depth = lax.axis_index("col")
    own_ids = segment_ids[0]
    mate_ids = exchange(own_ids)

    def big_start(ids):
        found = ids[:1025] == ids[1023:]
        return jnp.sum(jnp.where(found, jnp.arange(1025, dtype=jnp.int32), 0))

    own_start = big_start(own_ids)
    ids = jnp.where(depth // 2 == core, own_ids, mate_ids)
    ids = lax.dynamic_slice(
        jnp.concatenate([ids, ids[:1024]]), (big_start(ids),), (2048,)
    ).reshape(2, 2, 512)
    ids = lax.dynamic_index_in_dim(ids, depth % 2, 0, keepdims=False)
    ids = jnp.where(core == 0, ids, ids[::-1]).reshape(1024)
    flag = (1 - depth % 2).reshape(1).astype(jnp.int32)
    ids = (flag, ids[:, None], ids[None, :])

    def turned(values):
        longer = jnp.concatenate([values, values[:1024]], axis=0)
        return lax.dynamic_slice(longer, (own_start, 0), (2048, 256))

    def turned_back(values):
        longer = jnp.concatenate([values[1024:], values], axis=0)
        return lax.dynamic_slice(longer, (1024 - own_start, 0), (2048, 256)).astype(F32)

    small = jnp.concatenate(
        [
            query_bias, value_bias, proj_bias, attn_gain, attn_shift,
            inner_bias, outer_bias, ffn_gain, ffn_shift,
        ]
    ).reshape(24, 128)
    wqkv, wproj, winner, wouter, smalls, start_low, grad_low = gather_all(
        query_weight, key_weight, value_weight, proj_weight, inner_weight, outer_weight,
        small, turned(hidden_in), turned(grad_out),
    )
    weights = (wqkv, wproj, winner, wouter)
    smalls = smalls.reshape(4, 3072)
    vectors, offset = {}, 0
    for name, size in VECTORS:
        part = smalls[:, offset : offset + size]
        offset += size
        if name in SPLIT:
            part = jnp.where(core == 0, part[:, : size // 2], part[:, size // 2 :])
        vectors[name] = part.reshape(1, -1)
    vectors["inner"] = (
        vectors["inner"].reshape(4, 2, 256).transpose(1, 0, 2).reshape(1, 2048)
    )
    vectors["qkv"] = jnp.concatenate(
        [vectors["q"], jnp.zeros_like(vectors["q"]), vectors["v"]], axis=1
    )

    middle, kept_one = fast_forward(start_low.astype(F32), weights, vectors, ids)
    final_out, kept_two = fast_forward(middle, weights, vectors, ids)
    grad_flow = grad_low.astype(F32)
    grad_flow, terms_two, outer_two, inner_two, small_two = fast_backward(
        grad_flow, kept_two, weights, vectors, ids
    )
    hidden_out = spread_out(rounded(final_out), own_start)
    grad_flow, terms_one, outer_full, (inner_a, inner_b), small_one = fast_backward(
        grad_flow, kept_one, weights, vectors, ids, (outer_two, inner_two)
    )
    terms = [rounded(a + b) for a, b in zip(terms_two, terms_one)]
    pieces = []
    for (name, size), a, b in zip(VECTORS, small_two, small_one):
        total = a + b
        if name in SPLIT:
            half = total.reshape(4, 1, size // 2)
            if name == "inner":
                half = total.reshape(2, 4, 256).transpose(1, 0, 2).reshape(4, 1, 512)
            zero = jnp.zeros_like(half)
            total = jnp.where(
                core == 0,
                jnp.concatenate([half, zero], axis=1),
                jnp.concatenate([zero, half], axis=1),
            )
        pieces.append(total.reshape(-1))
    small_sum = jnp.concatenate(pieces).reshape(96, 128)
    results = scatter_all(*terms, inner_a, inner_b, outer_full, small_sum, rounded(grad_flow))
    proj_g, q_g, k_g, v_g, inner_g, outer_g, small_all, grad_turned = results
    small_all = small_all.reshape(-1)
    sums, offset = {}, 0
    for name, size in VECTORS:
        sums[name] = lax.dynamic_slice(small_all, (offset + depth * size,), (size,))
        offset += 4 * size
    return (
        hidden_out,
        turned_back(grad_turned),
        q_g,
        k_g,
        v_g,
        sums["q"],
        sums["v"],
        proj_g,
        sums["proj"],
        sums["attn_gain"],
        sums["attn_shift"],
        inner_g,
        sums["inner"],
        outer_g,
        sums["outer"],
        sums["ffn_gain"],
        sums["ffn_shift"],
    )


def solution(mesh):
    in_specs = (
        P("row", "col"),
        P("row", "col"),
        P("row", "col"),
        P("row", "col"),
        P("col"),
        P("col"),
        P("col", "row"),
        P("col"),
        P("col"),
        P("col"),
        P("row", "col"),
        P("col"),
        P("col", "row"),
        P("col"),
        P("col"),
        P("col"),
        P("row", None),
        P("row", "col"),
    )
    out_specs = (
        P("row", "col"),
        P("row", "col"),
        P("row", "col"),
        P("row", "col"),
        P("row", "col"),
        P("col"),
        P("col"),
        P("col", "row"),
        P("col"),
        P("col"),
        P("col"),
        P("row", "col"),
        P("col"),
        P("col", "row"),
        P("col"),
        P("col"),
        P("col"),
    )
    same = dict(mesh.shape) == {"row": 8, "col": 4}
    return jax.shard_map(
        fast_device if same else general_device, mesh=mesh, in_specs=in_specs, out_specs=out_specs, check_vma=False
    )
```

```python
import functools

import jax
import jax.numpy as jnp
from jax import lax
from jax.experimental import pallas as pl
from jax.experimental.pallas import tpu as pltpu
from jax.sharding import PartitionSpec as P

NEG_FILL = -1e30
HEAD_DIM = 64
D = 1024
LEN = 2048
QBLOCK = 512
SEQS = 1


EPSILON = 1e-06


def rounded(values):
    return values.astype(jnp.bfloat16)


def matmul(left, right):
    return jnp.dot(left, right, preferred_element_type=jnp.float32)


def over_tokens(left, right):
    return lax.dot_general(
        left, right, (((0,), (0,)), ((), ())), preferred_element_type=jnp.float32
    )


def against(left, right):
    return lax.dot_general(
        left, right, (((1,), (1,)), ((), ())), preferred_element_type=jnp.float32
    )


def token_sum(values):
    return jnp.sum(values, axis=0, dtype=jnp.float32)


def exact_gelu(inputs):
    return jax.nn.gelu(inputs, approximate=False)


def gather_weights(shards):
    front_set = (
        lax.all_gather(shards[0], "row", axis=0, tiled=True),
        lax.all_gather(shards[1], "row", axis=0, tiled=True),
        lax.all_gather(shards[2], "row", axis=0, tiled=True),
        lax.all_gather(shards[3], "row", axis=0, tiled=True),
    )
    back_set = (
        lax.all_gather(shards[4], "row", axis=1, tiled=True),
        lax.all_gather(shards[5], "row", axis=1, tiled=True),
    )
    proj_cols = back_set[0]
    return (
        front_set[0],
        front_set[1],
        front_set[2],
        front_set[3],
        back_set[0],
        back_set[1],
        proj_cols,
    )


def spread_features(values):
    return lax.all_gather(rounded(values), "col", axis=1, tiled=True)


def sum_partials(partial_terms):
    return lax.psum_scatter(
        partial_terms.astype(jnp.bfloat16), "col", scatter_dimension=1, tiled=True
    ).astype(jnp.float32)


def spread_grads(values):
    return lax.all_gather(values, "col", axis=1, tiled=True)


def sum_grad_partials(partial_terms):
    return lax.psum_scatter(
        partial_terms.astype(jnp.bfloat16), "col", scatter_dimension=1, tiled=True
    ).astype(jnp.float32)


def norm_forward(summed, norm_gain, norm_shift):
    totals = lax.psum((jnp.sum(summed, axis=1), jnp.sum(summed * summed, axis=1)), "col")
    center = totals[0][:, None] / D
    spread = totals[1][:, None] / D - center * center
    inverse = lax.rsqrt(spread + EPSILON)
    normed = (summed - center) * inverse
    return (normed * norm_gain + norm_shift, normed, inverse)


def norm_backward(grad_output, normed, inverse, norm_gain):
    scaled = grad_output * norm_gain
    totals = lax.psum((jnp.sum(scaled, axis=1), jnp.sum(scaled * normed, axis=1)), "col")
    grad_input = inverse * (scaled - totals[0][:, None] / D - normed * (totals[1][:, None] / D))
    return (grad_input, jnp.sum(grad_output * normed, axis=0), jnp.sum(grad_output, axis=0))


def split_heads(values):
    return values.reshape(SEQS, LEN, values.shape[1] // HEAD_DIM, HEAD_DIM)


def attend_forward(queries, key_rows, value_rows, segments):
    score_scale = HEAD_DIM ** (-0.5)
    blocks = LEN // QBLOCK
    query_heads = split_heads(queries)
    key_heads = split_heads(key_rows)
    value_heads = split_heads(value_rows)

    def attend_one_block(block_index):
        sequence = block_index // blocks
        offset = block_index % blocks * QBLOCK
        seq_queries = lax.dynamic_index_in_dim(query_heads, sequence, 0, keepdims=False)
        seq_keys = lax.dynamic_index_in_dim(key_heads, sequence, 0, keepdims=False)
        seq_values = lax.dynamic_index_in_dim(value_heads, sequence, 0, keepdims=False)
        seq_segments = lax.dynamic_index_in_dim(segments, sequence, 0, keepdims=False)
        block_queries = lax.dynamic_slice_in_dim(seq_queries, offset, QBLOCK, 0)
        block_segments = lax.dynamic_slice_in_dim(seq_segments, offset, QBLOCK, 0)
        scores = (
            jnp.einsum("qhd,khd->hqk", block_queries, seq_keys, preferred_element_type=jnp.float32)
            * score_scale
        )
        same_doc = block_segments[:, None] == seq_segments[None, :]
        scores = jnp.where(same_doc[None], scores, NEG_FILL)
        highest = jnp.max(scores, axis=2, keepdims=True)
        weights = jnp.exp(scores - highest)
        totals = jnp.sum(weights, axis=2, keepdims=True)
        mixture = jnp.einsum(
            "hqk,khd->qhd",
            rounded(weights / totals),
            seq_values,
            preferred_element_type=jnp.float32,
        )
        return (mixture, (highest + jnp.log(totals))[:, :, 0])

    mixture, log_total = lax.map(attend_one_block, jnp.arange(SEQS * blocks))
    return (mixture.reshape(queries.shape), log_total)


def attend_backward(queries, key_rows, value_rows, segments, log_total, grad_mixed):
    score_scale = HEAD_DIM ** (-0.5)
    blocks = LEN // QBLOCK
    heads_here = queries.shape[1] // HEAD_DIM
    query_heads = split_heads(queries)
    key_heads = split_heads(key_rows)
    value_heads = split_heads(value_rows)
    grad_heads = split_heads(grad_mixed)
    lse_rows = log_total.reshape(SEQS, blocks, heads_here, QBLOCK)

    def one_sequence(sequence):
        seq_queries = lax.dynamic_index_in_dim(query_heads, sequence, 0, keepdims=False)
        seq_keys = lax.dynamic_index_in_dim(key_heads, sequence, 0, keepdims=False)
        seq_values = lax.dynamic_index_in_dim(value_heads, sequence, 0, keepdims=False)
        seq_grads = lax.dynamic_index_in_dim(grad_heads, sequence, 0, keepdims=False)
        seq_segments = lax.dynamic_index_in_dim(segments, sequence, 0, keepdims=False)
        seq_lse = lax.dynamic_index_in_dim(lse_rows, sequence, 0, keepdims=False)

        def one_one_block(carry, block_index):
            offset = block_index * QBLOCK
            block_queries = lax.dynamic_slice_in_dim(seq_queries, offset, QBLOCK, 0)
            block_grads = lax.dynamic_slice_in_dim(seq_grads, offset, QBLOCK, 0)
            block_segments = lax.dynamic_slice_in_dim(seq_segments, offset, QBLOCK, 0)
            block_lse = lax.dynamic_index_in_dim(seq_lse, block_index, 0, keepdims=False)
            scores = (
                jnp.einsum(
                    "qhd,khd->hqk", block_queries, seq_keys, preferred_element_type=jnp.float32
                )
                * score_scale
            )
            same_doc = block_segments[:, None] == seq_segments[None, :]
            scores = jnp.where(same_doc[None], scores, NEG_FILL)
            probs = jnp.exp(scores - block_lse[:, :, None])
            grad_probs = jnp.einsum(
                "qhd,khd->hqk", block_grads, seq_values, preferred_element_type=jnp.float32
            )
            grad_scores = rounded(
                probs * (grad_probs - jnp.sum(probs * grad_probs, axis=2, keepdims=True))
            )
            grad_query = (
                jnp.einsum(
                    "hqk,khd->qhd", grad_scores, seq_keys, preferred_element_type=jnp.float32
                )
                * score_scale
            )
            key_sum = (
                carry[0]
                + jnp.einsum(
                    "hqk,qhd->khd", grad_scores, block_queries, preferred_element_type=jnp.float32
                )
                * score_scale
            )
            value_sum = carry[1] + jnp.einsum(
                "hqk,qhd->khd", rounded(probs), block_grads, preferred_element_type=jnp.float32
            )
            return ((key_sum, value_sum), rounded(grad_query))

        zeros_init = jnp.zeros((LEN, heads_here, HEAD_DIM), jnp.float32)
        (key_sum, value_sum), grad_query = lax.scan(
            one_one_block, (zeros_init, zeros_init), jnp.arange(blocks)
        )
        return (grad_query.reshape(LEN, heads_here, HEAD_DIM), rounded(key_sum), rounded(value_sum))

    grad_query, grad_key, grad_value = lax.map(one_sequence, jnp.arange(SEQS))
    return (
        grad_query.reshape(queries.shape),
        grad_key.reshape(queries.shape),
        grad_value.reshape(queries.shape),
    )


def layer_forward(hidden, params, gathered, segments):
    query_w, key_w, value_w, inner_w, proj_w, outer_w, proj_cols = gathered
    whole_in = spread_features(hidden)
    queries = rounded(matmul(whole_in, query_w) + params[0])
    key_rows = rounded(matmul(whole_in, key_w))
    value_rows = rounded(matmul(whole_in, value_w) + params[1])
    mixture, log_total = attend_forward(queries, key_rows, value_rows, segments)
    attended = rounded(mixture)
    attn_branch = sum_partials(matmul(attended, proj_w)) + params[2]
    first_norm, normed_one, inverse_one = norm_forward(hidden + attn_branch, params[3], params[4])
    whole_mid = spread_features(first_norm)
    inner_act = matmul(whole_mid, inner_w) + params[5]
    active = rounded(exact_gelu(inner_act))
    ffn_branch = sum_partials(matmul(active, outer_w)) + params[6]
    output, normed_two, inverse_two = norm_forward(first_norm + ffn_branch, params[7], params[8])
    kept_values = (
        whole_in,
        queries,
        key_rows,
        value_rows,
        log_total,
        attended,
        normed_one,
        inverse_one,
        whole_mid,
        inner_act,
        active,
        normed_two,
        inverse_two,
    )
    return (output, kept_values)


def layer_backward(grad_output, kept_values, gathered, params, segments):
    (
        whole_in,
        queries,
        key_rows,
        value_rows,
        log_total,
        attended,
        normed_one,
        inverse_one,
        whole_mid,
        inner_act,
        active,
        normed_two,
        inverse_two,
    ) = kept_values
    query_w, key_w, value_w, inner_w, proj_w, outer_w, proj_cols = gathered
    grad_second, ffn_gain_sum, ffn_shift_sum = norm_backward(
        grad_output, normed_two, inverse_two, params[7]
    )
    ffn_low = rounded(grad_second)
    whole_second = spread_grads(ffn_low)
    outer_term = over_tokens(active, whole_second)
    active_grad = against(whole_second, outer_w)
    unused, pullback = jax.vjp(exact_gelu, inner_act)
    inner_low = rounded(pullback(active_grad)[0])
    inner_term = over_tokens(whole_mid, inner_low)
    grad_first = grad_second + sum_grad_partials(against(inner_low, inner_w))
    grad_attn, attn_gain_sum, attn_shift_sum = norm_backward(
        grad_first, normed_one, inverse_one, params[3]
    )
    attn_low = rounded(grad_attn)
    whole_attn = spread_grads(attn_low)
    proj_term = over_tokens(attended, whole_attn)
    mixed_grad = rounded(against(whole_attn, proj_w))
    query_low, key_low, value_low = attend_backward(
        queries, key_rows, value_rows, segments, log_total, mixed_grad
    )
    input_terms = (
        against(query_low, query_w) + against(key_low, key_w) + against(value_low, value_w)
    )
    grad_input = grad_attn + sum_grad_partials(input_terms)
    row_terms = (
        over_tokens(whole_in, query_low),
        over_tokens(whole_in, key_low),
        over_tokens(whole_in, value_low),
        inner_term,
    )
    col_terms = (proj_term, outer_term)
    small_terms = (
        token_sum(query_low),
        token_sum(value_low),
        token_sum(attn_low),
        attn_gain_sum,
        attn_shift_sum,
        token_sum(inner_low),
        token_sum(ffn_low),
        ffn_gain_sum,
        ffn_shift_sum,
    )
    return (grad_input, row_terms, col_terms, small_terms)


def general_device(
    hidden_in,
    query_weight,
    key_weight,
    value_weight,
    query_bias,
    value_bias,
    proj_weight,
    proj_bias,
    attn_gain,
    attn_shift,
    inner_weight,
    inner_bias,
    outer_weight,
    outer_bias,
    ffn_gain,
    ffn_shift,
    segment_ids,
    grad_out,
):
    shards = (query_weight, key_weight, value_weight, inner_weight, proj_weight, outer_weight)
    params = (
        query_bias,
        value_bias,
        proj_bias,
        attn_gain,
        attn_shift,
        inner_bias,
        outer_bias,
        ffn_gain,
        ffn_shift,
    )
    gathered = gather_weights(shards)
    start_in = hidden_in.astype(jnp.float32)
    middle, kept_one = layer_forward(start_in, params, gathered, segment_ids)
    final_out, kept_two = layer_forward(middle, params, gathered, segment_ids)
    kept = (kept_one, kept_two)
    grad_flow = grad_out.astype(jnp.float32)
    row_parts = []
    col_parts = []
    small_parts = []
    for layer_index in (1, 0):
        grad_flow, row_terms, col_terms, small_terms = layer_backward(
            grad_flow, kept[layer_index], gathered, params, segment_ids
        )
        row_parts.append(row_terms)
        col_parts.append(col_terms)
        small_parts.append(small_terms)
    row_sum = jax.tree.map(jnp.add, tuple(row_parts[0]), tuple(row_parts[1]))
    col_sum = jax.tree.map(jnp.add, tuple(col_parts[0]), tuple(col_parts[1]))
    small_sum = jax.tree.map(jnp.add, small_parts[0], small_parts[1])
    row_sum = (
        lax.psum_scatter(
            row_sum[0].astype(jnp.bfloat16), "row", scatter_dimension=0, tiled=True
        ).astype(jnp.float32),
        lax.psum_scatter(
            row_sum[1].astype(jnp.bfloat16), "row", scatter_dimension=0, tiled=True
        ).astype(jnp.float32),
        lax.psum_scatter(
            row_sum[2].astype(jnp.bfloat16), "row", scatter_dimension=0, tiled=True
        ).astype(jnp.float32),
        lax.psum_scatter(
            row_sum[3].astype(jnp.bfloat16), "row", scatter_dimension=0, tiled=True
        ).astype(jnp.float32),
    )
    col_sum = (
        lax.psum_scatter(
            col_sum[0].astype(jnp.bfloat16), "row", scatter_dimension=1, tiled=True
        ).astype(jnp.float32),
        lax.psum_scatter(
            col_sum[1].astype(jnp.bfloat16), "row", scatter_dimension=1, tiled=True
        ).astype(jnp.float32),
    )
    small_sum = lax.psum(
        (
            small_sum[0],
            small_sum[1],
            small_sum[2],
            small_sum[3],
            small_sum[4],
            small_sum[5],
            small_sum[6],
            small_sum[7],
            small_sum[8],
        ),
        "row",
    )
    return (
        final_out,
        grad_flow,
        row_sum[0],
        row_sum[1],
        row_sum[2],
        small_sum[0],
        small_sum[1],
        col_sum[0],
        small_sum[2],
        small_sum[3],
        small_sum[4],
        row_sum[3],
        small_sum[5],
        col_sum[1],
        small_sum[6],
        small_sum[7],
        small_sum[8],
    )


ANY = pl.BlockSpec(memory_space=pl.ANY)
VMEM = pl.BlockSpec(memory_space=pltpu.VMEM)
MESH = pl.DeviceIdType.MESH
DMA = pltpu.SemaphoreType.DMA
BF16 = jnp.bfloat16
F32 = jnp.float32


def place():
    row = lax.axis_index("row")
    depth = lax.axis_index("col")
    core = row % 2
    chip = row // 2
    x = chip % 2
    y = chip // 2
    return row, depth, core, chip, x, y


def remote(src, dst, send_sem, recv_sem, row, depth):
    return pltpu.make_async_remote_copy(
        src_ref=src,
        dst_ref=dst,
        send_sem=send_sem,
        recv_sem=recv_sem,
        device_id={"row": row, "col": depth},
        device_id_type=MESH,
    )


def span(start, size):
    return pl.ds(pl.multiple_of(start, 128), size)


def greet(row, depth, core, chip, x, y):
    barrier = pltpu.get_barrier_semaphore()
    mate = chip * 2 + (1 - core)
    friends = [(mate, depth)]
    for step in (1, 2, 3):
        friends.append((row, (depth + step) % 4))
        friends.append((mate, (depth + step) % 4))
    friends.append(((y * 2 + 1 - x) * 2 + core, depth))
    friends.append((((1 - y) * 2 + x) * 2 + core, depth))
    for r, d in friends:
        pl.semaphore_signal(
            barrier, inc=1, device_id={"row": r, "col": d}, device_id_type=MESH
        )
    pl.semaphore_wait(barrier, len(friends))


PIECES = 8
GROUPS = ((3,), (0,), (1,), (2,), (4,), (5,), (6,), (7,))


def gather_kernel(
    q_ref, k_ref, v_ref, proj_ref, inner_ref, outer_ref, small_ref, x_ref, g_ref,
    wqkv, wproj, winner, wouter, smalls, u_out, g_out,
    swap_s, swap_r, local_s, up_s, up_r, down_s, down_r, sm_s, sm_r,
    p1_s, p1_r, p2_s, p2_r, t_s, t_r, t_l,
):
    row, depth, core, chip, x, y = place()
    mate = chip * 2 + (1 - core)
    x_chip = y * 2 + 1 - x
    y_chip = (1 - y) * 2 + x
    x_row = x_chip * 2 + core
    y_row = y_chip * 2 + core
    greet(row, depth, core, chip, x, y)

    def swap_src(piece, half):
        if piece < 3:
            return (q_ref, k_ref, v_ref)[piece].at[:, span(half * 128, 128)]
        if piece == 3:
            return proj_ref.at[span(half * 128, 128), :]
        if piece < 6:
            return inner_ref.at[:, span(half * 512 + (piece - 4) * 256, 256)]
        return outer_ref.at[span(half * 512 + (piece - 6) * 256, 256), :]

    def cell(piece, start, size, origin):
        if piece < 3:
            return wqkv.at[span(start, size), span(piece * 512 + origin * 128, 128)]
        if piece == 3:
            return wproj.at[span(origin * 128, 128), span(start, size)]
        if piece < 6:
            return winner.at[
                span(start, size), span((piece - 4) * 1024 + origin * 256, 256)
            ]
        return wouter.at[span((piece - 6) * 1024 + origin * 256, 256), span(start, size)]

    def region(group, part, block):
        piece = GROUPS[group][0]
        if piece < 3:
            return wqkv.at[span(block * 256 + part * 128, 128), pl.ds(piece * 512, 512)]
        if piece == 3:
            return wproj.at[pl.ds(part * 256, 256), span(block * 256, 256)]
        if piece < 6:
            return winner.at[
                span(block * 256 + part * 128, 128), pl.ds((piece - 4) * 1024, 1024)
            ]
        return wouter.at[
            pl.ds((piece - 6) * 1024 + part * 512, 512), span(block * 256, 256)
        ]

    swaps, locals_ = [], []
    for piece in range(PIECES):
        target = cell(piece, row * 128, 128, depth)
        cp = remote(
            swap_src(piece, 1 - core), target, swap_s.at[piece], swap_r.at[piece], mate, depth
        )
        cp.start()
        swaps.append(cp)
        lc = pltpu.make_async_copy(swap_src(piece, core), target, local_s.at[piece])
        lc.start()
        locals_.append(lc)
    small_local = pltpu.make_async_copy(small_ref, smalls.at[depth], local_s.at[PIECES])
    small_local.start()

    def travel(piece, step, up):
        origin = depth - step if up else depth + step
        ref = cell(piece, chip * 256, 256, origin)
        send, recv = (up_s, up_r) if up else (down_s, down_r)
        return remote(
            ref, ref, send.at[piece, step], recv.at[piece, step], row,
            depth + 1 if up else depth - 1,
        )

    def depth_step(group, step):
        for piece in GROUPS[group]:
            if step == 0:
                swaps[piece].wait_recv()
                locals_[piece].wait()
            for up in (True, False):
                inside = depth - step >= 0 if up else depth + step <= 3
                ready = inside & (depth < 3 if up else depth > 0)
                if step > 0:

                    @pl.when(inside)
                    def _():
                        origin = depth - step if up else depth + step
                        ref = cell(piece, chip * 256, 256, origin)
                        recv = up_r if up else down_r
                        remote(
                            ref, ref, up_s.at[piece, step - 1], recv.at[piece, step - 1],
                            mate, depth,
                        ).wait_recv()

                if step < 3:

                    @pl.when(ready)
                    def _():
                        travel(piece, step, up).start()

    def depth_done():
        for piece in range(PIECES):
            for step in (0, 1, 2):
                for up in (True, False):
                    inside = depth - step >= 0 if up else depth + step <= 3

                    @pl.when(inside & (depth < 3 if up else depth > 0))
                    def _():
                        travel(piece, step, up).wait_send()

    def token_copies(index, src, dst):
        for j in range(4):
            to_core, to_depth = j % 2, core * 2 + j // 2
            mine = (to_core == core) & (to_depth == depth)
            source = src.at[pl.ds(j * 512, 512), :]
            target = dst.at[:, span(depth * 256, 256)]

            @pl.when(mine)
            def _():
                pltpu.make_async_copy(source, target, t_l.at[index]).start()

            @pl.when(jnp.logical_not(mine))
            def _():
                remote(
                    source, target, t_s.at[index, j], t_r.at[index, depth],
                    chip * 2 + to_core, to_depth,
                ).start()

    def token_waits(index, src, dst):
        from_core = depth // 2
        for s in range(4):
            mine = (from_core == core) & (s == depth)
            target = dst.at[:, pl.ds(s * 256, 256)]
            source = src.at[pl.ds(0, 512), :]

            @pl.when(mine)
            def _():
                pltpu.make_async_copy(source, target, t_l.at[index]).wait()

            @pl.when(jnp.logical_not(mine))
            def _():
                remote(
                    source, target, t_s.at[index, 0], t_r.at[index, s], mate, depth
                ).wait_recv()
        for j in range(4):
            to_core, to_depth = j % 2, core * 2 + j // 2
            mine = (to_core == core) & (to_depth == depth)

            @pl.when(jnp.logical_not(mine))
            def _():
                remote(
                    src.at[pl.ds(j * 512, 512), :], dst.at[:, pl.ds(0, 256)],
                    t_s.at[index, j], t_r.at[index, 0], mate, depth,
                ).wait_send()

    first, second = {}, {}

    def start_first(group):
        for part, target in ((0, x_row), (1, y_row)):
            cp = remote(
                region(group, part, chip), region(group, part, chip),
                p1_s.at[group, part], p1_r.at[group, part], target, depth,
            )
            cp.start()
            first[group, part] = cp

    def start_second(group):
        for part, target, other in ((0, y_row, x_chip), (1, x_row, y_chip)):
            first[group, part].wait_recv()
            for i, block in enumerate((chip, other)):
                cp = remote(
                    region(group, part, block), region(group, part, block),
                    p2_s.at[group, part, i], p2_r.at[group, part, i], target, depth,
                )
                cp.start()
                second[group, part, i] = cp

    count = len(GROUPS)
    small_copies = []
    for tick in range(count + 4):
        for step in (0, 1, 2, 3):
            group = tick - step
            if 0 <= group < count:
                depth_step(group, step)
                if step == 3:
                    start_first(group)
        if 0 <= tick - 4 < count:
            start_second(tick - 4)
        if tick == TOKEN_TICK:
            token_copies(0, x_ref, u_out)
        if tick == count - 1:
            for k in (1, 2, 3):
                cp = remote(
                    small_ref, smalls.at[depth], sm_s.at[k - 1], sm_r.at[k - 1],
                    row, (depth + k) % 4,
                )
                cp.start()
                small_copies.append(cp)
            token_copies(1, g_ref, g_out)
    token_waits(0, x_ref, u_out)
    token_waits(1, g_ref, g_out)
    for cp in small_copies:
        cp.wait()
    small_local.wait()
    depth_done()
    for cp in second.values():
        cp.wait()
    for cp in first.values():
        cp.wait_send()
    for cp in swaps:
        cp.wait_send()


TOKEN_TICK = 7


def gather_all(q, k, v, proj, inner, outer, small, x_rolled, g_rolled):
    sd = jax.ShapeDtypeStruct
    n = len(GROUPS)
    return pl.pallas_call(
        gather_kernel,
        out_shape=(
            sd((1024, 1536), BF16),
            sd((512, 1024), BF16),
            sd((1024, 2048), BF16),
            sd((2048, 1024), BF16),
            sd((4,) + small.shape, F32),
            sd((512, 1024), BF16),
            sd((512, 1024), BF16),
        ),
        in_specs=[VMEM] * 7 + [ANY] * 2,
        out_specs=[ANY] * 7,
        scratch_shapes=[
            DMA((PIECES,)), DMA((PIECES,)), DMA((PIECES + 1,)),
            DMA((PIECES, 3)), DMA((PIECES, 3)), DMA((PIECES, 3)), DMA((PIECES, 3)),
            DMA((3,)), DMA((3,)),
            DMA((n, 2)), DMA((n, 2)), DMA((n, 2, 2)), DMA((n, 2, 2)),
            DMA((2, 4)), DMA((2, 4)), DMA((2,)),
        ],
        compiler_params=pltpu.CompilerParams(collective_id=1, has_side_effects=True),
    )(q, k, v, proj, inner, outer, small, x_rolled, g_rolled)


SHAPES = ((256, 256), (128, 512), (128, 512), (128, 512))
UNITS = ((128, 256), (256, 128), (256, 128), (256, 128))
FULLS = ((512, 256), (256, 512), (256, 512), (256, 512))
OUTS = ((256, 128), (128, 256), (128, 256), (128, 256), (128, 1024), (1024, 128))
HALVES = ((128, 128), (128, 128), (128, 128), (128, 128), (128, 512), (512, 128))
BY_COLS = (True, False, False, False)
INNER, OUTER = 4, 5


def add_rows(dst, terms):
    rows = dst.shape[0]
    step = 32

    def body(i, carry):
        sl = pl.ds(pl.multiple_of(i * step, step), step)
        total = terms[0][sl, :].astype(F32)
        for term in terms[1:]:
            total = total + term[sl, :].astype(F32)
        dst[sl, :] = total.astype(dst.dtype)
        return carry

    lax.fori_loop(0, rows // step, body, 0)


def scatter_kernel(*refs):
    grads = refs[0:4]
    inner_ref, outer_ref, small_ref, gi_ref = refs[4:8]
    outs = refs[8:14]
    small_out, gi_out = refs[14:16]
    rest = list(refs[16:])
    own = [[rest.pop(0) for _ in range(2)] for _ in range(4)]
    got1 = [[rest.pop(0) for _ in range(2)] for _ in range(4)]
    got2 = [[rest.pop(0) for _ in range(2)] for _ in range(4)]
    full = [rest.pop(0) for _ in range(4)]
    zgot = [rest.pop(0) for _ in range(4)]
    fin = [rest.pop(0) for _ in range(4)]
    cgot = [rest.pop(0) for _ in range(6)]
    sb = rest.pop(0)
    sg = rest.pop(0)
    (o_s, p1_s, p1_r, p2_s, p2_r, z_s, z_r, c_s, c_r, sm_s, sm_r, t_s, t_r, t_l) = rest

    row, depth, core, chip, x, y = place()
    mate = chip * 2 + (1 - core)
    x_row = (y * 2 + 1 - x) * 2 + core
    y_row = ((1 - y) * 2 + x) * 2 + core
    greet(row, depth, core, chip, x, y)

    def region(group, part, block):
        rows = SHAPES[group][0]
        if BY_COLS[group]:
            return grads[group].at[pl.ds(part * rows, rows), span(block * 256, 256)]
        return grads[group].at[span(block * 256 + part * 128, 128), :]

    def unit(group, z):
        if BY_COLS[group]:
            return full[group].at[span(z * UNITS[group][0], UNITS[group][0]), :]
        return full[group].at[:, span(z * UNITS[group][1], UNITS[group][1])]

    def side(group, half):
        if group == OUTER:
            return outer_ref.at[:, span(half * 128, 128)]
        if group == INNER:
            return inner_ref.at[span(half * 128, 128), :]
        if BY_COLS[group]:
            return fin[group].at[:, span(half * 128, 128)]
        return fin[group].at[span(half * 128, 128), :]

    def out_side(group, half):
        if group == OUTER:
            return outs[5].at[span(half * 512, 512), :]
        if group == INNER:
            return outs[4].at[:, span(half * 512, 512)]
        size = HALVES[group]
        if BY_COLS[group]:
            return outs[group].at[span(half * size[0], size[0]), :]
        return outs[group].at[:, span(half * size[1], size[1])]

    copies = {}

    def start_first(group):
        for part in (0, 1):
            target = y_row if part == 0 else x_row
            for i in (0, 1):
                kept = y * 2 + i if part == 0 else i * 2 + x
                sent = (1 - y) * 2 + i if part == 0 else i * 2 + (1 - x)
                lc = pltpu.make_async_copy(
                    region(group, part, kept), own[group][part].at[i], o_s.at[group, part, i]
                )
                lc.start()
                cp = remote(
                    region(group, part, sent), got1[group][part].at[i],
                    p1_s.at[group, part, i], p1_r.at[group, part, i], target, depth,
                )
                cp.start()
                copies["o", group, part, i] = lc
                copies["p1", group, part, i] = cp

    def start_second(group):
        for part in (0, 1):
            target = x_row if part == 0 else y_row
            mine = x if part == 0 else y
            for i in (0, 1):
                copies["o", group, part, i].wait()
                copies["p1", group, part, i].wait_recv()
            other = own[group][part].at[1 - mine]
            add_rows(other, (other, got1[group][part].at[1 - mine]))
            cp = remote(
                other, got2[group][part], p2_s.at[group, part], p2_r.at[group, part], target, depth
            )
            cp.start()
            copies["p2", group, part] = cp

    def send_depth(group):
        for k in (1, 2, 3):
            cp = remote(
                unit(group, (depth + k) % 4), zgot[group].at[k - 1],
                z_s.at[group, k - 1], z_r.at[group, k - 1], row, (depth + k) % 4,
            )
            cp.start()
            copies["z", group, k] = cp

    def start_depth(group):
        rows = SHAPES[group][0]
        for part in (0, 1):
            mine = x if part == 0 else y
            copies["p2", group, part].wait_recv()
            add_rows(
                full[group].at[pl.ds(part * rows, rows), :],
                (own[group][part].at[mine], got1[group][part].at[mine], got2[group][part]),
            )
        send_depth(group)

    def send_core(group):
        cp = remote(
            side(group, 1 - core), cgot[group], c_s.at[group], c_r.at[group], mate, depth
        )
        cp.start()
        copies["c", group] = cp

    def start_core(group):
        for k in (1, 2, 3):
            copies["z", group, k].wait_recv()
        add_rows(
            fin[group],
            (unit(group, depth), zgot[group].at[0], zgot[group].at[1], zgot[group].at[2]),
        )
        send_core(group)

    def finish(group):
        add_rows(out_side(group, core), (side(group, core),))
        copies["c", group].wait_recv()
        add_rows(out_side(group, 1 - core), (cgot[group],))

    def token_copies(index, src, dst):
        j = (depth % 2) * 2 + core
        to_core = depth // 2
        for z in range(4):
            mine = (to_core == core) & (z == depth)
            source = src.at[:, pl.ds(z * 256, 256)]
            target = dst.at[span(j * 512, 512), :]

            @pl.when(mine)
            def _():
                pltpu.make_async_copy(source, target, t_l.at[index]).start()

            @pl.when(jnp.logical_not(mine))
            def _():
                remote(
                    source, target, t_s.at[index, z], t_r.at[index, j], chip * 2 + to_core, z
                ).start()

    def token_waits(index, src, dst):
        to_core = depth // 2
        for j in range(4):
            from_core, from_depth = j % 2, core * 2 + j // 2
            mine = (from_core == core) & (from_depth == depth)
            target = dst.at[pl.ds(j * 512, 512), :]
            source = src.at[:, pl.ds(0, 256)]

            @pl.when(mine)
            def _():
                pltpu.make_async_copy(source, target, t_l.at[index]).wait()

            @pl.when(jnp.logical_not(mine))
            def _():
                remote(
                    source, target, t_s.at[index, 0], t_r.at[index, j], mate, depth
                ).wait_recv()
        for z in range(4):
            mine = (to_core == core) & (z == depth)

            @pl.when(jnp.logical_not(mine))
            def _():
                remote(
                    src.at[:, pl.ds(z * 256, 256)], dst.at[pl.ds(0, 512), :],
                    t_s.at[index, z], t_r.at[index, 0], mate, depth,
                ).wait_send()

    def small_send(step, slot, target_row, target_depth):
        cp = remote(
            sb.at[step], sg.at[slot], sm_s.at[slot], sm_r.at[slot], target_row, target_depth
        )
        cp.start()
        copies["s", slot] = cp

    def small_add(step, slot):
        copies["s", slot].wait_recv()
        sb[step + 1] = sb[step] + sg[slot]

    sb[0] = small_ref[...]
    for group in range(4):
        start_first(group)
    small_send(0, 0, mate, depth)
    send_core(OUTER)
    send_core(INNER)
    token_copies(0, gi_ref, gi_out)
    small_add(0, 0)
    small_send(1, 1, x_row, depth)
    finish(OUTER)
    finish(INNER)
    for group in range(4):
        start_second(group)
        if group == 0:
            small_add(1, 1)
            small_send(2, 2, y_row, depth)
        if group > 0:
            start_depth(group - 1)
    small_add(2, 2)
    for k in (1, 2, 3):
        small_send(3, 2 + k, row, (depth + k) % 4)
    start_depth(3)
    for group in (0, 1, 2):
        start_core(group)
    for k in (1, 2, 3):
        copies["s", 2 + k].wait_recv()
    small_out[...] = ((sb[3] + sg[3]) + sg[4]) + sg[5]
    for group in (0, 1, 2):
        finish(group)
    start_core(3)
    token_waits(0, gi_ref, gi_out)
    finish(3)
    for key, cp in copies.items():
        if key[0] != "o":
            cp.wait_send()


def scatter_all(proj, q, k, v, inner, outer, small, gi):
    sd = jax.ShapeDtypeStruct
    scratch = []
    for size in SHAPES:
        scratch += [pltpu.VMEM((2,) + size, BF16)] * 2
    for size in SHAPES:
        scratch += [pltpu.VMEM((2,) + size, BF16)] * 2
    for size in SHAPES:
        scratch += [pltpu.VMEM(size, BF16)] * 2
    scratch += [pltpu.VMEM(size, BF16) for size in FULLS]
    scratch += [pltpu.VMEM((3,) + size, BF16) for size in UNITS]
    scratch += [pltpu.VMEM(size, BF16) for size in UNITS]
    scratch += [pltpu.VMEM(size, BF16) for size in HALVES]
    scratch += [pltpu.VMEM((4,) + small.shape, F32), pltpu.VMEM((6,) + small.shape, F32)]
    scratch += [
        DMA((4, 2, 2)), DMA((4, 2, 2)), DMA((4, 2, 2)), DMA((4, 2)), DMA((4, 2)),
        DMA((4, 3)), DMA((4, 3)), DMA((6,)), DMA((6,)), DMA((6,)), DMA((6,)),
        DMA((1, 4)), DMA((1, 4)), DMA((1,)),
    ]
    return pl.pallas_call(
        scatter_kernel,
        out_shape=tuple(sd(size, F32) for size in OUTS)
        + (sd(small.shape, F32), sd((2048, 256), BF16)),
        in_specs=[ANY] * 4 + [VMEM] * 3 + [ANY],
        out_specs=[VMEM] * 7 + [ANY],
        scratch_shapes=scratch,
        compiler_params=pltpu.CompilerParams(
            collective_id=2, has_side_effects=True, vmem_limit_bytes=48 * 1024 * 1024
        ),
    )(proj, q, k, v, inner, outer, small, gi)


def attend_kernel(flag_ref, q_ref, k_ref, v_ref, idq_ref, idk_ref, o_ref, lse_ref):
    rows = q_ref.shape[0]
    lane = lax.broadcasted_iota(jnp.int32, (1, 128), 1)
    low_half = lane < HEAD_DIM

    def compute(masked):
        keys = k_ref[...]
        values = v_ref[...]
        halves = (low_half, jnp.logical_not(low_half))
        sub = 256
        units = [(i, h) for i in range(rows // sub) for h in (0, 1)]

        def score(unit):
            i, h = unit
            scaled = q_ref[i * sub : (i + 1) * sub, :] * jnp.asarray(HEAD_DIM**-0.5, BF16)
            s = against(jnp.where(halves[h], scaled, jnp.zeros_like(scaled)), keys)
            if masked:
                s = jnp.where(idq_ref[i * sub : (i + 1) * sub, :] == idk_ref[...], s, NEG_FILL)
            return s

        def soft(s):
            top = jnp.max(s, axis=1, keepdims=True)
            weights = jnp.exp(s - top)
            return weights.astype(BF16), jnp.sum(weights, axis=1, keepdims=True), top

        skew = 1
        pending = [score(u) for u in units[:skew]]
        done = {}
        for n, unit in enumerate(units):
            if n + skew < len(units):
                pending.append(score(units[n + skew]))
            low, total, top = soft(pending.pop(0))
            mixed = matmul(low, values)
            done[unit] = (mixed / total, top + jnp.log(total))
            i, h = unit
            if h == 1:
                sl = slice(i * sub, (i + 1) * sub)
                a, b = done[i, 0], done[i, 1]
                o_ref[sl, :] = jnp.where(low_half, a[0], b[0]).astype(o_ref.dtype)
                lse_ref[sl, :] = jnp.where(low_half, a[1], b[1])

    @pl.when(flag_ref[0] == 1)
    def _():
        compute(False)

    @pl.when(flag_ref[0] != 1)
    def _():
        compute(True)


def attend(flag, qkv, id_col, id_row):
    tokens, width = qkv.shape[0], qkv.shape[1] // 3
    pairs = width // 128
    block = tokens
    return pl.pallas_call(
        attend_kernel,
        out_shape=(
            jax.ShapeDtypeStruct((tokens, width), BF16),
            jax.ShapeDtypeStruct((tokens, width), F32),
        ),
        grid_spec=pltpu.PrefetchScalarGridSpec(
            num_scalar_prefetch=1,
            grid=(width // 128, tokens // block),
            in_specs=[
                pl.BlockSpec((block, 128), lambda h, i, f: (i, h)),
                pl.BlockSpec((tokens, 128), lambda h, i, f: (0, h + pairs)),
                pl.BlockSpec((tokens, 128), lambda h, i, f: (0, h + 2 * pairs)),
                pl.BlockSpec((block, 1), lambda h, i, f: (i, 0)),
                pl.BlockSpec((1, tokens), lambda h, i, f: (0, 0)),
            ],
            out_specs=[
                pl.BlockSpec((block, 128), lambda h, i, f: (i, h)),
                pl.BlockSpec((block, 128), lambda h, i, f: (i, h)),
            ],
        ),
        compiler_params=pltpu.CompilerParams(
            dimension_semantics=("arbitrary", "arbitrary"), vmem_limit_bytes=48 * 1024 * 1024
        ),
        cost_estimate=pl.CostEstimate(
            flops=20_000_000_000, bytes_accessed=8_000_000, transcendentals=0
        ),
        name="attend",
    )(flag, qkv, qkv, qkv, id_col, id_row)


def attend_back_kernel(
    flag_ref, q_ref, k_ref, v_ref, do_ref, lse_ref, idk_ref, idq_ref,
    dq_ref, dk_ref, dv_ref,
):
    rows = q_ref.shape[0]
    scale = HEAD_DIM**-0.5
    lane = lax.broadcasted_iota(jnp.int32, (1, 128), 1)
    low_half = lane < HEAD_DIM

    def compute(masked):
        queries = q_ref[...]
        scaled = queries * jnp.asarray(scale, BF16)
        keys = k_ref[...]
        values = v_ref[...]
        grads = do_ref[...]
        lse_t = lse_ref[...].T
        q_t, k_t, do_t = queries.T, keys.T, grads.T
        dqs, dks, dvs = [], [], []
        for head in (0, 1):
            here = low_half if head == 0 else jnp.logical_not(low_half)
            part = slice(head * HEAD_DIM, (head + 1) * HEAD_DIM)
            zero = jnp.zeros_like(keys)
            scores = against(jnp.where(here, keys, zero), scaled)
            if masked:
                scores = jnp.where(idk_ref[...] == idq_ref[...], scores, NEG_FILL)
            log_row = lse_t[head * HEAD_DIM : head * HEAD_DIM + 1, :]
            probs = jnp.exp(scores - log_row)
            grad_probs = against(jnp.where(here, values, zero), grads)
            moved = probs * grad_probs
            delta = jnp.sum(moved, axis=0, keepdims=True)
            grad_scores = (moved - probs * delta).astype(BF16)
            low = probs.astype(BF16)
            dvs.append(against(do_t[part], low))
            dks.append(matmul(grad_scores, queries))
            dqs.append(matmul(k_t[part], grad_scores))
        dv_ref[...] = jnp.concatenate(dvs, axis=0).T.astype(BF16)
        dk_ref[...] = (jnp.where(low_half, dks[0], dks[1]) * scale).astype(BF16)
        dq_ref[...] = (jnp.concatenate(dqs, axis=0) * scale).T.astype(BF16)

    @pl.when(flag_ref[0] == 1)
    def _():
        compute(False)

    @pl.when(flag_ref[0] != 1)
    def _():
        compute(True)


def attend_back(flag, qkv, do, lse, id_col, id_row, first=0, count=4):
    tokens, width = qkv.shape[0], qkv.shape[1] // 3
    pairs = width // 128
    block = tokens
    shape = jax.ShapeDtypeStruct((tokens, count * 128), BF16)
    rows = pl.BlockSpec((block, 128), lambda h, i, f: (i, h + first))
    return pl.pallas_call(
        attend_back_kernel,
        out_shape=(shape, shape, shape),
        grid_spec=pltpu.PrefetchScalarGridSpec(
            num_scalar_prefetch=1,
            grid=(count, tokens // block),
            in_specs=[
                rows,
                pl.BlockSpec((tokens, 128), lambda h, i, f: (0, h + first + pairs)),
                pl.BlockSpec((tokens, 128), lambda h, i, f: (0, h + first + 2 * pairs)),
                rows, rows,
                pl.BlockSpec((tokens, 1), lambda h, i, f: (0, 0)),
                pl.BlockSpec((1, block), lambda h, i, f: (0, i)),
            ],
            out_specs=[
                pl.BlockSpec((block, 128), lambda h, i, f: (i, h)),
                pl.BlockSpec((tokens, 128), lambda h, i, f: (0, h)),
                pl.BlockSpec((tokens, 128), lambda h, i, f: (0, h)),
            ],
        ),
        compiler_params=pltpu.CompilerParams(
            dimension_semantics=("arbitrary", "arbitrary"), vmem_limit_bytes=48 * 1024 * 1024
        ),
        cost_estimate=pl.CostEstimate(
            flops=10_000_000_000 * count, bytes_accessed=2_500_000 * count, transcendentals=0
        ),
        name="attend_back",
    )(flag, qkv, qkv, qkv, do, lse, id_col, id_row)


def gelu_pair(inner):
    size = jnp.abs(inner)
    bell = jnp.exp(inner * (inner * -0.5))
    t = 1.0 / (1.0 + (0.3275911 * 0.5**0.5) * size)
    poly = (0.5 * 1.061405429) * t - 0.5 * 1.453152027
    poly = poly * t + 0.5 * 1.421413741
    poly = poly * t - 0.5 * 0.284496736
    poly = poly * t + 0.5 * 0.254829592
    tail = (poly * t) * bell
    below = jnp.where(inner >= 0.0, 1.0 - tail, tail)
    return (inner * below).astype(BF16), (below + inner * (bell * 0.3989422804014327)).astype(BF16)


def ffn_in_kernel(x_ref, w_ref, b_ref, active_ref, slope_ref):
    rows, cols = active_ref.shape
    sub = 128
    skew = 1

    def open_unit(i):
        return matmul(x_ref[i * sub : (i + 1) * sub, :], w_ref[...]) + b_ref[...]

    count = rows // sub
    pending = [open_unit(i) for i in range(skew)]
    for i in range(count):
        if i + skew < count:
            pending.append(open_unit(i + skew))
        active, slope = gelu_pair(pending.pop(0))
        active_ref[i * sub : (i + 1) * sub, :] = active
        slope_ref[i * sub : (i + 1) * sub, :] = slope


def ffn_in(x, w, bias):
    tokens, depth = x.shape
    hidden = w.shape[1]
    rows, cols = 1024, 512
    shape = jax.ShapeDtypeStruct((tokens, hidden), BF16)
    out = pl.BlockSpec((rows, cols), lambda n, m: (m, n))
    return pl.pallas_call(
        ffn_in_kernel,
        out_shape=(shape, shape),
        grid=(hidden // cols, tokens // rows),
        in_specs=[
            pl.BlockSpec((rows, depth), lambda n, m: (m, 0)),
            pl.BlockSpec((depth, cols), lambda n, m: (0, n)),
            pl.BlockSpec((1, cols), lambda n, m: (0, n)),
        ],
        out_specs=[out, out],
        compiler_params=pltpu.CompilerParams(
            dimension_semantics=("arbitrary", "arbitrary"), vmem_limit_bytes=48 * 1024 * 1024
        ),
        cost_estimate=pl.CostEstimate(
            flops=14_000_000_000, bytes_accessed=14_000_000, transcendentals=0
        ),
        name="ffn_in",
    )(x, w, bias)


def exchange(values):
    pairs = [(r, r + 1 - 2 * (r % 2)) for r in range(8)]
    return lax.ppermute(values, "row", pairs)


def both(own):
    return jnp.concatenate([own, exchange(own)], axis=0)


def share_sum(left, weight, product):
    mate_part, left_own = lax.optimization_barrier(
        (rounded(product(left[512:], weight)), left[:512])
    )
    other = exchange(mate_part)
    return product(left_own, weight) + other.astype(F32)


def norm_rows(summed, gain, shift):
    center = jnp.mean(summed, axis=1, keepdims=True)
    spread = jnp.mean(summed * summed, axis=1, keepdims=True) - center * center
    inverse = lax.rsqrt(spread + EPSILON)
    normed = (summed - center) * inverse
    return normed * gain + shift, normed, inverse


def norm_rows_back(grad_output, normed, inverse, gain):
    scaled = grad_output * gain
    mean_one = jnp.mean(scaled, axis=1, keepdims=True)
    mean_two = jnp.mean(scaled * normed, axis=1, keepdims=True)
    grad_input = inverse * (scaled - mean_one - normed * mean_two)
    return grad_input, token_sum(grad_output * normed), token_sum(grad_output)


def fast_forward(hidden, weights, vectors, ids):
    wqkv, wproj, winner, wouter = weights
    flag, id_col, id_row = ids
    whole_in = both(rounded(hidden))
    qkv = rounded(matmul(whole_in, wqkv) + vectors["qkv"])
    attended, lse = attend(flag, qkv, id_col, id_row)
    branch = share_sum(attended, wproj, matmul) + vectors["proj"]
    first, normed_one, inverse_one = norm_rows(
        hidden + branch, vectors["attn_gain"], vectors["attn_shift"]
    )
    whole_mid = both(rounded(first))
    active, slope = ffn_in(whole_mid, winner, vectors["inner"])
    ffn = share_sum(active, wouter, matmul) + vectors["outer"]
    output, normed_two, inverse_two = norm_rows(
        first + ffn, vectors["ffn_gain"], vectors["ffn_shift"]
    )
    kept = (
        whole_in, qkv, lse, attended, normed_one, inverse_one,
        whole_mid, active, slope, normed_two, inverse_two,
    )
    return output, kept


def fast_backward(grad_output, kept, weights, vectors, ids, later=None, beside=None):
    (
        whole_in, qkv, lse, attended, normed_one, inverse_one,
        whole_mid, active, slope, normed_two, inverse_two,
    ) = kept
    wqkv, wproj, winner, wouter = weights
    flag, id_col, id_row = ids
    grad_second, ffn_gain_sum, ffn_shift_sum = norm_rows_back(
        grad_output, normed_two, inverse_two, vectors["ffn_gain"]
    )
    ffn_low = rounded(grad_second)
    whole_second = both(ffn_low)
    inner_low = rounded(against(whole_second, wouter) * slope.astype(F32))
    outer_terms = outer_pieces(active, by_place(whole_second))
    if later is not None:
        outer_planes = [Plane(add_trees(outer_terms, later[0]), h, 1) for h in (0, 1)]
        outer_got = [p.step_one() for p in outer_planes]
    grad_first = grad_second + share_sum(inner_low, winner, against)
    inner_terms = inner_pieces(by_place(whole_mid), inner_low)
    if later is not None:
        inner_planes = [Plane(add_trees(inner_terms, later[1]), h, 0) for h in (0, 1)]
        inner_got = [p.step_one() for p in inner_planes]
    grad_attn, attn_gain_sum, attn_shift_sum = norm_rows_back(
        grad_first, normed_one, inverse_one, vectors["attn_gain"]
    )
    attn_low = rounded(grad_attn)
    whole_attn = both(attn_low)
    mixed_grad = rounded(against(whole_attn, wproj))
    proj_term = over_tokens(attended, whole_attn)
    if later is None:
        grads = attend_back(flag, qkv, mixed_grad, lse, id_col, id_row)
        if beside is not None:
            beside, grads = lax.optimization_barrier((beside, grads))
        outer_terms, inner_terms = (outer_terms, inner_terms), beside
    else:
        early = attend_back(flag, qkv, mixed_grad, lse, id_col, id_row, 0, 2)
        outer_got, early = lax.optimization_barrier((outer_got, early))
        outer_hand = [p.to_hand(g) for p, g in zip(outer_planes, outer_got)]
        outer_hand, mixed_grad = lax.optimization_barrier((outer_hand, mixed_grad))
        outer_more = [p.step_two(v) for p, v in zip(outer_planes, outer_hand)]
        late = attend_back(flag, qkv, mixed_grad, lse, id_col, id_row, 2, 2)
        inner_got, late = lax.optimization_barrier((inner_got, late))
        inner_hand = [p.to_hand(g) for p, g in zip(inner_planes, inner_got)]
        inner_hand, outer_more, late = lax.optimization_barrier((inner_hand, outer_more, late))
        inner_more = [p.step_two(v) for p, v in zip(inner_planes, inner_hand)]
        outer_terms = fold_depth([p.close(m) for p, m in zip(outer_planes, outer_more)], 0)
        inner_terms = fold_depth([p.close(m) for p, m in zip(inner_planes, inner_more)], 1)
        grads = tuple(jnp.concatenate(pair, axis=1) for pair in zip(early, late))
    grad_qkv = jnp.concatenate(grads, axis=1)
    grad_input = grad_attn + share_sum(grad_qkv, wqkv, against)
    terms = (proj_term,) + tuple(
        over_tokens(whole_in, part) for part in grads
    )
    small = (
        token_sum(grads[0]), token_sum(grads[2]), token_sum(attn_low),
        attn_gain_sum, attn_shift_sum, token_sum(inner_low), token_sum(ffn_low),
        ffn_gain_sum, ffn_shift_sum,
    )
    return grad_input, terms, outer_terms, inner_terms, small


def flip_row(bit):
    return [(r, r + bit - 2 * bit * ((r // bit) % 2)) for r in range(8)]


def by_place(values):
    chip = lax.axis_index("row") // 2
    x, y = chip % 2, chip // 2

    def block(yy, xx):
        return lax.dynamic_slice_in_dim(values, (yy * 2 + xx) * 256, 256, 1)

    far = block(1 - y, 1 - x)
    return jnp.concatenate(
        [block(y, 1 - x), block(y, x), block(1 - y, x), far, block(y, 1 - x)], axis=1
    )


CUTS = (((512, 1024), (0, 256), (256, 512)), ((768, 1280), (512, 768), (256, 512)))


def outer_pieces(active, relative):
    return [
        [over_tokens(active[:, h * 1024 : (h + 1) * 1024], relative[:, a:b]) for a, b in CUTS[h]]
        for h in (0, 1)
    ]


def inner_pieces(relative, inner_low):
    return [
        [over_tokens(relative[:, a:b], inner_low[:, h * 1024 : (h + 1) * 1024]) for a, b in CUTS[h]]
        for h in (0, 1)
    ]


def add_trees(left, right):
    return jax.tree.map(lambda p, q: p + q, left, right)


class Plane:
    def __init__(self, pieces, half, axis):
        sent, self.handed, self.own = pieces[half]
        self.sent = rounded(sent)
        self.half, self.axis = half, axis
        self.first, self.second = (4, 2) if half == 0 else (2, 4)

    def step_one(self):
        return lax.ppermute(self.sent, "row", flip_row(self.first))

    def to_hand(self, got):
        low, high = jnp.split(got, 2, axis=self.axis)
        self.got, handed = (low, high) if self.half == 0 else (high, low)
        return rounded(self.handed + handed.astype(F32))

    def step_two(self, handed):
        return lax.ppermute(handed, "row", flip_row(self.second))

    def close(self, more):
        return rounded(self.own + self.got.astype(F32) + more.astype(F32))


def fold_depth(halves, axis):
    depth = lax.axis_index("col")

    def unit(z):
        picked = [lax.dynamic_slice_in_dim(half, z * 256, 256, axis) for half in halves]
        return jnp.concatenate(picked, axis=axis)

    total = unit(depth).astype(F32)
    for k in (1, 2, 3):
        pairs = [(z, (z + k) % 4) for z in range(4)]
        total = total + lax.ppermute(unit((depth + k) % 4), "col", pairs).astype(F32)
    return rounded(total)


def spread_out(values):
    core = lax.axis_index("row") % 2
    depth = lax.axis_index("col")
    j = (depth % 2) * 2 + core
    parts = []
    for k in range(4):
        pairs = []
        for r in range(8):
            for z in range(4):
                block = ((z % 2) * 2 + r % 2 + k) % 4
                pairs.append((r * 4 + z, (r // 2 * 2 + z // 2) * 4 + block))
        piece = lax.dynamic_slice_in_dim(values, ((j + k) % 4) * 256, 256, 1)
        parts.append(lax.ppermute(piece, ("row", "col"), pairs))
    return parts


def join_parts(parts, own_start):
    depth = lax.axis_index("col")
    cycle = jnp.concatenate(parts[::-1] * 2, axis=0)
    start = ((3 - depth) * 512 - own_start + 2048) % 2048
    return lax.dynamic_slice(cycle, (start, 0), (2048, 256)).astype(F32)


VECTORS = (
    ("q", 256), ("v", 256), ("proj", 256), ("attn_gain", 256), ("attn_shift", 256),
    ("inner", 1024), ("outer", 256), ("ffn_gain", 256), ("ffn_shift", 256),
)
SPLIT = ("q", "v", "inner")


def fast_device(
    hidden_in,
    query_weight,
    key_weight,
    value_weight,
    query_bias,
    value_bias,
    proj_weight,
    proj_bias,
    attn_gain,
    attn_shift,
    inner_weight,
    inner_bias,
    outer_weight,
    outer_bias,
    ffn_gain,
    ffn_shift,
    segment_ids,
    grad_out,
):
    core = lax.axis_index("row") % 2
    depth = lax.axis_index("col")
    own_ids = segment_ids[0]
    mate_ids = exchange(own_ids)

    def big_start(ids):
        found = ids[:1025] == ids[1023:]
        return jnp.sum(jnp.where(found, jnp.arange(1025, dtype=jnp.int32), 0))

    own_start = big_start(own_ids)
    ids = jnp.where(depth // 2 == core, own_ids, mate_ids)
    ids = lax.dynamic_slice(
        jnp.concatenate([ids, ids[:1024]]), (big_start(ids),), (2048,)
    ).reshape(2, 2, 512)
    ids = lax.dynamic_index_in_dim(ids, depth % 2, 0, keepdims=False)
    ids = jnp.where(core == 0, ids, ids[::-1]).reshape(1024)
    flag = (1 - depth % 2).reshape(1).astype(jnp.int32)
    ids = (flag, ids[:, None], ids[None, :])

    def turned(values):
        longer = jnp.concatenate([values, values[:1024]], axis=0)
        return lax.dynamic_slice(longer, (own_start, 0), (2048, 256))

    def turned_back(values):
        longer = jnp.concatenate([values[1024:], values], axis=0)
        return lax.dynamic_slice(longer, (1024 - own_start, 0), (2048, 256)).astype(F32)

    small = jnp.concatenate(
        [
            query_bias, value_bias, proj_bias, attn_gain, attn_shift,
            inner_bias, outer_bias, ffn_gain, ffn_shift,
        ]
    ).reshape(24, 128)
    wqkv, wproj, winner, wouter, smalls, start_low, grad_low = gather_all(
        query_weight, key_weight, value_weight, proj_weight, inner_weight, outer_weight,
        small, turned(hidden_in), turned(grad_out),
    )
    weights = (wqkv, wproj, winner, wouter)
    smalls = smalls.reshape(4, 3072)
    vectors, offset = {}, 0
    for name, size in VECTORS:
        part = smalls[:, offset : offset + size]
        offset += size
        if name in SPLIT:
            part = jnp.where(core == 0, part[:, : size // 2], part[:, size // 2 :])
        vectors[name] = part.reshape(1, -1)
    vectors["inner"] = (
        vectors["inner"].reshape(4, 2, 256).transpose(1, 0, 2).reshape(1, 2048)
    )
    vectors["qkv"] = jnp.concatenate(
        [vectors["q"], jnp.zeros_like(vectors["q"]), vectors["v"]], axis=1
    )

    middle, kept_one = fast_forward(start_low.astype(F32), weights, vectors, ids)
    final_out, kept_two = fast_forward(middle, weights, vectors, ids)
    grad_flow = grad_low.astype(F32)
    parts = spread_out(rounded(final_out))
    grad_flow, terms_two, ffn_two, parts, small_two = fast_backward(
        grad_flow, kept_two, weights, vectors, ids, None, parts
    )
    hidden_out = join_parts(parts, own_start)
    grad_flow, terms_one, outer_full, inner_full, small_one = fast_backward(
        grad_flow, kept_one, weights, vectors, ids, ffn_two
    )
    terms = [rounded(a + b) for a, b in zip(terms_two, terms_one)]
    pieces = []
    for (name, size), a, b in zip(VECTORS, small_two, small_one):
        total = a + b
        if name in SPLIT:
            half = total.reshape(4, 1, size // 2)
            if name == "inner":
                half = total.reshape(2, 4, 256).transpose(1, 0, 2).reshape(4, 1, 512)
            zero = jnp.zeros_like(half)
            total = jnp.where(
                core == 0,
                jnp.concatenate([half, zero], axis=1),
                jnp.concatenate([zero, half], axis=1),
            )
        pieces.append(total.reshape(-1))
    small_sum = jnp.concatenate(pieces).reshape(96, 128)
    results = scatter_all(*terms, inner_full, outer_full, small_sum, rounded(grad_flow))
    proj_g, q_g, k_g, v_g, inner_g, outer_g, small_all, grad_turned = results
    small_all = small_all.reshape(-1)
    sums, offset = {}, 0
    for name, size in VECTORS:
        sums[name] = lax.dynamic_slice(small_all, (offset + depth * size,), (size,))
        offset += 4 * size
    return (
        hidden_out,
        turned_back(grad_turned),
        q_g,
        k_g,
        v_g,
        sums["q"],
        sums["v"],
        proj_g,
        sums["proj"],
        sums["attn_gain"],
        sums["attn_shift"],
        inner_g,
        sums["inner"],
        outer_g,
        sums["outer"],
        sums["ffn_gain"],
        sums["ffn_shift"],
    )


def solution(mesh):
    in_specs = (
        P("row", "col"),
        P("row", "col"),
        P("row", "col"),
        P("row", "col"),
        P("col"),
        P("col"),
        P("col", "row"),
        P("col"),
        P("col"),
        P("col"),
        P("row", "col"),
        P("col"),
        P("col", "row"),
        P("col"),
        P("col"),
        P("col"),
        P("row", None),
        P("row", "col"),
    )
    out_specs = (
        P("row", "col"),
        P("row", "col"),
        P("row", "col"),
        P("row", "col"),
        P("row", "col"),
        P("col"),
        P("col"),
        P("col", "row"),
        P("col"),
        P("col"),
        P("col"),
        P("row", "col"),
        P("col"),
        P("col", "row"),
        P("col"),
        P("col"),
        P("col"),
    )
    same = dict(mesh.shape) == {"row": 8, "col": 4}
    return jax.shard_map(
        fast_device if same else general_device, mesh=mesh, in_specs=in_specs, out_specs=out_specs, check_vma=False
    )
```

```python
import functools

import jax
import jax.numpy as jnp
from jax import lax
from jax.experimental import pallas as pl
from jax.experimental.pallas import tpu as pltpu
from jax.sharding import PartitionSpec as P

NEG_FILL = -1e30
HEAD_DIM = 64
D = 1024
LEN = 2048
QBLOCK = 512
SEQS = 1


EPSILON = 1e-06


def rounded(values):
    return values.astype(jnp.bfloat16)


def matmul(left, right):
    return jnp.dot(left, right, preferred_element_type=jnp.float32)


def over_tokens(left, right):
    return lax.dot_general(
        left, right, (((0,), (0,)), ((), ())), preferred_element_type=jnp.float32
    )


def against(left, right):
    return lax.dot_general(
        left, right, (((1,), (1,)), ((), ())), preferred_element_type=jnp.float32
    )


def token_sum(values):
    return jnp.sum(values, axis=0, dtype=jnp.float32)


def exact_gelu(inputs):
    return jax.nn.gelu(inputs, approximate=False)


def gather_weights(shards):
    front_set = (
        lax.all_gather(shards[0], "row", axis=0, tiled=True),
        lax.all_gather(shards[1], "row", axis=0, tiled=True),
        lax.all_gather(shards[2], "row", axis=0, tiled=True),
        lax.all_gather(shards[3], "row", axis=0, tiled=True),
    )
    back_set = (
        lax.all_gather(shards[4], "row", axis=1, tiled=True),
        lax.all_gather(shards[5], "row", axis=1, tiled=True),
    )
    proj_cols = back_set[0]
    return (
        front_set[0],
        front_set[1],
        front_set[2],
        front_set[3],
        back_set[0],
        back_set[1],
        proj_cols,
    )


def spread_features(values):
    return lax.all_gather(rounded(values), "col", axis=1, tiled=True)


def sum_partials(partial_terms):
    return lax.psum_scatter(
        partial_terms.astype(jnp.bfloat16), "col", scatter_dimension=1, tiled=True
    ).astype(jnp.float32)


def spread_grads(values):
    return lax.all_gather(values, "col", axis=1, tiled=True)


def sum_grad_partials(partial_terms):
    return lax.psum_scatter(
        partial_terms.astype(jnp.bfloat16), "col", scatter_dimension=1, tiled=True
    ).astype(jnp.float32)


def norm_forward(summed, norm_gain, norm_shift):
    totals = lax.psum((jnp.sum(summed, axis=1), jnp.sum(summed * summed, axis=1)), "col")
    center = totals[0][:, None] / D
    spread = totals[1][:, None] / D - center * center
    inverse = lax.rsqrt(spread + EPSILON)
    normed = (summed - center) * inverse
    return (normed * norm_gain + norm_shift, normed, inverse)


def norm_backward(grad_output, normed, inverse, norm_gain):
    scaled = grad_output * norm_gain
    totals = lax.psum((jnp.sum(scaled, axis=1), jnp.sum(scaled * normed, axis=1)), "col")
    grad_input = inverse * (scaled - totals[0][:, None] / D - normed * (totals[1][:, None] / D))
    return (grad_input, jnp.sum(grad_output * normed, axis=0), jnp.sum(grad_output, axis=0))


def split_heads(values):
    return values.reshape(SEQS, LEN, values.shape[1] // HEAD_DIM, HEAD_DIM)


def attend_forward(queries, key_rows, value_rows, segments):
    score_scale = HEAD_DIM ** (-0.5)
    blocks = LEN // QBLOCK
    query_heads = split_heads(queries)
    key_heads = split_heads(key_rows)
    value_heads = split_heads(value_rows)

    def attend_one_block(block_index):
        sequence = block_index // blocks
        offset = block_index % blocks * QBLOCK
        seq_queries = lax.dynamic_index_in_dim(query_heads, sequence, 0, keepdims=False)
        seq_keys = lax.dynamic_index_in_dim(key_heads, sequence, 0, keepdims=False)
        seq_values = lax.dynamic_index_in_dim(value_heads, sequence, 0, keepdims=False)
        seq_segments = lax.dynamic_index_in_dim(segments, sequence, 0, keepdims=False)
        block_queries = lax.dynamic_slice_in_dim(seq_queries, offset, QBLOCK, 0)
        block_segments = lax.dynamic_slice_in_dim(seq_segments, offset, QBLOCK, 0)
        scores = (
            jnp.einsum("qhd,khd->hqk", block_queries, seq_keys, preferred_element_type=jnp.float32)
            * score_scale
        )
        same_doc = block_segments[:, None] == seq_segments[None, :]
        scores = jnp.where(same_doc[None], scores, NEG_FILL)
        highest = jnp.max(scores, axis=2, keepdims=True)
        weights = jnp.exp(scores - highest)
        totals = jnp.sum(weights, axis=2, keepdims=True)
        mixture = jnp.einsum(
            "hqk,khd->qhd",
            rounded(weights / totals),
            seq_values,
            preferred_element_type=jnp.float32,
        )
        return (mixture, (highest + jnp.log(totals))[:, :, 0])

    mixture, log_total = lax.map(attend_one_block, jnp.arange(SEQS * blocks))
    return (mixture.reshape(queries.shape), log_total)


def attend_backward(queries, key_rows, value_rows, segments, log_total, grad_mixed):
    score_scale = HEAD_DIM ** (-0.5)
    blocks = LEN // QBLOCK
    heads_here = queries.shape[1] // HEAD_DIM
    query_heads = split_heads(queries)
    key_heads = split_heads(key_rows)
    value_heads = split_heads(value_rows)
    grad_heads = split_heads(grad_mixed)
    lse_rows = log_total.reshape(SEQS, blocks, heads_here, QBLOCK)

    def one_sequence(sequence):
        seq_queries = lax.dynamic_index_in_dim(query_heads, sequence, 0, keepdims=False)
        seq_keys = lax.dynamic_index_in_dim(key_heads, sequence, 0, keepdims=False)
        seq_values = lax.dynamic_index_in_dim(value_heads, sequence, 0, keepdims=False)
        seq_grads = lax.dynamic_index_in_dim(grad_heads, sequence, 0, keepdims=False)
        seq_segments = lax.dynamic_index_in_dim(segments, sequence, 0, keepdims=False)
        seq_lse = lax.dynamic_index_in_dim(lse_rows, sequence, 0, keepdims=False)

        def one_one_block(carry, block_index):
            offset = block_index * QBLOCK
            block_queries = lax.dynamic_slice_in_dim(seq_queries, offset, QBLOCK, 0)
            block_grads = lax.dynamic_slice_in_dim(seq_grads, offset, QBLOCK, 0)
            block_segments = lax.dynamic_slice_in_dim(seq_segments, offset, QBLOCK, 0)
            block_lse = lax.dynamic_index_in_dim(seq_lse, block_index, 0, keepdims=False)
            scores = (
                jnp.einsum(
                    "qhd,khd->hqk", block_queries, seq_keys, preferred_element_type=jnp.float32
                )
                * score_scale
            )
            same_doc = block_segments[:, None] == seq_segments[None, :]
            scores = jnp.where(same_doc[None], scores, NEG_FILL)
            probs = jnp.exp(scores - block_lse[:, :, None])
            grad_probs = jnp.einsum(
                "qhd,khd->hqk", block_grads, seq_values, preferred_element_type=jnp.float32
            )
            grad_scores = rounded(
                probs * (grad_probs - jnp.sum(probs * grad_probs, axis=2, keepdims=True))
            )
            grad_query = (
                jnp.einsum(
                    "hqk,khd->qhd", grad_scores, seq_keys, preferred_element_type=jnp.float32
                )
                * score_scale
            )
            key_sum = (
                carry[0]
                + jnp.einsum(
                    "hqk,qhd->khd", grad_scores, block_queries, preferred_element_type=jnp.float32
                )
                * score_scale
            )
            value_sum = carry[1] + jnp.einsum(
                "hqk,qhd->khd", rounded(probs), block_grads, preferred_element_type=jnp.float32
            )
            return ((key_sum, value_sum), rounded(grad_query))

        zeros_init = jnp.zeros((LEN, heads_here, HEAD_DIM), jnp.float32)
        (key_sum, value_sum), grad_query = lax.scan(
            one_one_block, (zeros_init, zeros_init), jnp.arange(blocks)
        )
        return (grad_query.reshape(LEN, heads_here, HEAD_DIM), rounded(key_sum), rounded(value_sum))

    grad_query, grad_key, grad_value = lax.map(one_sequence, jnp.arange(SEQS))
    return (
        grad_query.reshape(queries.shape),
        grad_key.reshape(queries.shape),
        grad_value.reshape(queries.shape),
    )


def layer_forward(hidden, params, gathered, segments):
    query_w, key_w, value_w, inner_w, proj_w, outer_w, proj_cols = gathered
    whole_in = spread_features(hidden)
    queries = rounded(matmul(whole_in, query_w) + params[0])
    key_rows = rounded(matmul(whole_in, key_w))
    value_rows = rounded(matmul(whole_in, value_w) + params[1])
    mixture, log_total = attend_forward(queries, key_rows, value_rows, segments)
    attended = rounded(mixture)
    attn_branch = sum_partials(matmul(attended, proj_w)) + params[2]
    first_norm, normed_one, inverse_one = norm_forward(hidden + attn_branch, params[3], params[4])
    whole_mid = spread_features(first_norm)
    inner_act = matmul(whole_mid, inner_w) + params[5]
    active = rounded(exact_gelu(inner_act))
    ffn_branch = sum_partials(matmul(active, outer_w)) + params[6]
    output, normed_two, inverse_two = norm_forward(first_norm + ffn_branch, params[7], params[8])
    kept_values = (
        whole_in,
        queries,
        key_rows,
        value_rows,
        log_total,
        attended,
        normed_one,
        inverse_one,
        whole_mid,
        inner_act,
        active,
        normed_two,
        inverse_two,
    )
    return (output, kept_values)


def layer_backward(grad_output, kept_values, gathered, params, segments):
    (
        whole_in,
        queries,
        key_rows,
        value_rows,
        log_total,
        attended,
        normed_one,
        inverse_one,
        whole_mid,
        inner_act,
        active,
        normed_two,
        inverse_two,
    ) = kept_values
    query_w, key_w, value_w, inner_w, proj_w, outer_w, proj_cols = gathered
    grad_second, ffn_gain_sum, ffn_shift_sum = norm_backward(
        grad_output, normed_two, inverse_two, params[7]
    )
    ffn_low = rounded(grad_second)
    whole_second = spread_grads(ffn_low)
    outer_term = over_tokens(active, whole_second)
    active_grad = against(whole_second, outer_w)
    unused, pullback = jax.vjp(exact_gelu, inner_act)
    inner_low = rounded(pullback(active_grad)[0])
    inner_term = over_tokens(whole_mid, inner_low)
    grad_first = grad_second + sum_grad_partials(against(inner_low, inner_w))
    grad_attn, attn_gain_sum, attn_shift_sum = norm_backward(
        grad_first, normed_one, inverse_one, params[3]
    )
    attn_low = rounded(grad_attn)
    whole_attn = spread_grads(attn_low)
    proj_term = over_tokens(attended, whole_attn)
    mixed_grad = rounded(against(whole_attn, proj_w))
    query_low, key_low, value_low = attend_backward(
        queries, key_rows, value_rows, segments, log_total, mixed_grad
    )
    input_terms = (
        against(query_low, query_w) + against(key_low, key_w) + against(value_low, value_w)
    )
    grad_input = grad_attn + sum_grad_partials(input_terms)
    row_terms = (
        over_tokens(whole_in, query_low),
        over_tokens(whole_in, key_low),
        over_tokens(whole_in, value_low),
        inner_term,
    )
    col_terms = (proj_term, outer_term)
    small_terms = (
        token_sum(query_low),
        token_sum(value_low),
        token_sum(attn_low),
        attn_gain_sum,
        attn_shift_sum,
        token_sum(inner_low),
        token_sum(ffn_low),
        ffn_gain_sum,
        ffn_shift_sum,
    )
    return (grad_input, row_terms, col_terms, small_terms)


def general_device(
    hidden_in,
    query_weight,
    key_weight,
    value_weight,
    query_bias,
    value_bias,
    proj_weight,
    proj_bias,
    attn_gain,
    attn_shift,
    inner_weight,
    inner_bias,
    outer_weight,
    outer_bias,
    ffn_gain,
    ffn_shift,
    segment_ids,
    grad_out,
):
    shards = (query_weight, key_weight, value_weight, inner_weight, proj_weight, outer_weight)
    params = (
        query_bias,
        value_bias,
        proj_bias,
        attn_gain,
        attn_shift,
        inner_bias,
        outer_bias,
        ffn_gain,
        ffn_shift,
    )
    gathered = gather_weights(shards)
    start_in = hidden_in.astype(jnp.float32)
    middle, kept_one = layer_forward(start_in, params, gathered, segment_ids)
    final_out, kept_two = layer_forward(middle, params, gathered, segment_ids)
    kept = (kept_one, kept_two)
    grad_flow = grad_out.astype(jnp.float32)
    row_parts = []
    col_parts = []
    small_parts = []
    for layer_index in (1, 0):
        grad_flow, row_terms, col_terms, small_terms = layer_backward(
            grad_flow, kept[layer_index], gathered, params, segment_ids
        )
        row_parts.append(row_terms)
        col_parts.append(col_terms)
        small_parts.append(small_terms)
    row_sum = jax.tree.map(jnp.add, tuple(row_parts[0]), tuple(row_parts[1]))
    col_sum = jax.tree.map(jnp.add, tuple(col_parts[0]), tuple(col_parts[1]))
    small_sum = jax.tree.map(jnp.add, small_parts[0], small_parts[1])
    row_sum = (
        lax.psum_scatter(
            row_sum[0].astype(jnp.bfloat16), "row", scatter_dimension=0, tiled=True
        ).astype(jnp.float32),
        lax.psum_scatter(
            row_sum[1].astype(jnp.bfloat16), "row", scatter_dimension=0, tiled=True
        ).astype(jnp.float32),
        lax.psum_scatter(
            row_sum[2].astype(jnp.bfloat16), "row", scatter_dimension=0, tiled=True
        ).astype(jnp.float32),
        lax.psum_scatter(
            row_sum[3].astype(jnp.bfloat16), "row", scatter_dimension=0, tiled=True
        ).astype(jnp.float32),
    )
    col_sum = (
        lax.psum_scatter(
            col_sum[0].astype(jnp.bfloat16), "row", scatter_dimension=1, tiled=True
        ).astype(jnp.float32),
        lax.psum_scatter(
            col_sum[1].astype(jnp.bfloat16), "row", scatter_dimension=1, tiled=True
        ).astype(jnp.float32),
    )
    small_sum = lax.psum(
        (
            small_sum[0],
            small_sum[1],
            small_sum[2],
            small_sum[3],
            small_sum[4],
            small_sum[5],
            small_sum[6],
            small_sum[7],
            small_sum[8],
        ),
        "row",
    )
    return (
        final_out,
        grad_flow,
        row_sum[0],
        row_sum[1],
        row_sum[2],
        small_sum[0],
        small_sum[1],
        col_sum[0],
        small_sum[2],
        small_sum[3],
        small_sum[4],
        row_sum[3],
        small_sum[5],
        col_sum[1],
        small_sum[6],
        small_sum[7],
        small_sum[8],
    )


ANY = pl.BlockSpec(memory_space=pl.ANY)
VMEM = pl.BlockSpec(memory_space=pltpu.VMEM)
MESH = pl.DeviceIdType.MESH
DMA = pltpu.SemaphoreType.DMA
BF16 = jnp.bfloat16
F32 = jnp.float32


def place():
    row = lax.axis_index("row")
    depth = lax.axis_index("col")
    core = row % 2
    chip = row // 2
    x = chip % 2
    y = chip // 2
    return row, depth, core, chip, x, y


def remote(src, dst, send_sem, recv_sem, row, depth):
    return pltpu.make_async_remote_copy(
        src_ref=src,
        dst_ref=dst,
        send_sem=send_sem,
        recv_sem=recv_sem,
        device_id={"row": row, "col": depth},
        device_id_type=MESH,
    )


def slot_of(block, x, y):
    dx = (block % 2 - x) * (block % 2 - x)
    dy = (block // 2 - y) * (block // 2 - y)
    return 3 * dy + dx - 2 * dx * dy


def span(start, size):
    if isinstance(start, int):
        return pl.ds(start, size)
    return pl.ds(pl.multiple_of(start, 128), size)


def greet(row, depth, core, chip, x, y):
    barrier = pltpu.get_barrier_semaphore()
    mate = chip * 2 + (1 - core)
    friends = [(mate, depth)]
    for step in (1, 2, 3):
        friends.append((row, (depth + step) % 4))
        friends.append((mate, (depth + step) % 4))
    friends.append(((y * 2 + 1 - x) * 2 + core, depth))
    friends.append((((1 - y) * 2 + x) * 2 + core, depth))
    for r, d in friends:
        pl.semaphore_signal(
            barrier, inc=1, device_id={"row": r, "col": d}, device_id_type=MESH
        )
    pl.semaphore_wait(barrier, len(friends))


PIECES = 8
GROUPS = ((3,), (0,), (1,), (2,), (4,), (5,), (6,), (7,))


def gather_kernel(
    q_ref, k_ref, v_ref, proj_ref, inner_ref, outer_ref, small_ref, x_ref, g_ref,
    wqkv, wproj, winner, wouter, smalls, u_out, g_out,
    swap_s, swap_r, local_s, up_s, up_r, down_s, down_r, sm_s, sm_r,
    p1_s, p1_r, p2_s, p2_r, t_s, t_r, t_l, pair_s, pair_r,
):
    row, depth, core, chip, x, y = place()
    mate = chip * 2 + (1 - core)
    x_row = (y * 2 + 1 - x) * 2 + core
    y_row = ((1 - y) * 2 + x) * 2 + core
    greet(row, depth, core, chip, x, y)

    def swap_src(piece, half):
        if piece < 3:
            return (q_ref, k_ref, v_ref)[piece].at[:, span(half * 128, 128)]
        if piece == 3:
            return proj_ref.at[span(half * 128, 128), :]
        if piece < 6:
            return inner_ref.at[:, span(half * 512 + (piece - 4) * 256, 256)]
        return outer_ref.at[span(half * 512 + (piece - 6) * 256, 256), :]

    def cell(piece, start, size, origin):
        if piece < 3:
            return wqkv.at[span(start, size), span(piece * 512 + origin * 128, 128)]
        if piece == 3:
            return wproj.at[span(origin * 128, 128), span(start, size)]
        if piece < 6:
            return winner.at[
                span(start, size), span((piece - 4) * 1024 + origin * 256, 256)
            ]
        return wouter.at[span((piece - 6) * 1024 + origin * 256, 256), span(start, size)]

    def region(group, part, block):
        piece = GROUPS[group][0]
        if piece < 3:
            return wqkv.at[span(block * 256 + part * 128, 128), pl.ds(piece * 512, 512)]
        if piece == 3:
            return wproj.at[pl.ds(part * 256, 256), span(block * 256, 256)]
        if piece < 6:
            return winner.at[
                span(block * 256 + part * 128, 128), pl.ds((piece - 4) * 1024, 1024)
            ]
        return wouter.at[
            pl.ds((piece - 6) * 1024 + part * 512, 512), span(block * 256, 256)
        ]

    swaps, locals_ = [], []
    for piece in range(PIECES):
        target = cell(piece, core * 128, 128, depth)
        cp = remote(
            swap_src(piece, 1 - core), target, swap_s.at[piece], swap_r.at[piece], mate, depth
        )
        cp.start()
        swaps.append(cp)
        lc = pltpu.make_async_copy(swap_src(piece, core), target, local_s.at[piece])
        lc.start()
        locals_.append(lc)
    small_local = pltpu.make_async_copy(small_ref, smalls.at[depth], local_s.at[PIECES])
    small_local.start()

    def travel(piece, step, up):
        origin = depth - step if up else depth + step
        ref = cell(piece, 0, 256, origin)
        send, recv = (up_s, up_r) if up else (down_s, down_r)
        return remote(
            ref, ref, send.at[piece, step], recv.at[piece, step], row,
            depth + 1 if up else depth - 1,
        )

    def depth_step(group, step):
        for piece in GROUPS[group]:
            if step == 0:
                swaps[piece].wait_recv()
                locals_[piece].wait()
            for up in (True, False):
                inside = depth - step >= 0 if up else depth + step <= 3
                ready = inside & (depth < 3 if up else depth > 0)
                if step > 0:

                    @pl.when(inside)
                    def _():
                        origin = depth - step if up else depth + step
                        ref = cell(piece, 0, 256, origin)
                        recv = up_r if up else down_r
                        remote(
                            ref, ref, up_s.at[piece, step - 1], recv.at[piece, step - 1],
                            mate, depth,
                        ).wait_recv()

                if step < 3:

                    @pl.when(ready)
                    def _():
                        travel(piece, step, up).start()

    def depth_done():
        for piece in range(PIECES):
            for step in (0, 1, 2):
                for up in (True, False):
                    inside = depth - step >= 0 if up else depth + step <= 3

                    @pl.when(inside & (depth < 3 if up else depth > 0))
                    def _():
                        travel(piece, step, up).wait_send()

    def token_copies(index, src, dst):
        for j in range(4):
            to_core, to_depth = j % 2, core * 2 + j // 2
            mine = (to_core == core) & (to_depth == depth)
            source = src.at[pl.ds(j * 512, 512), :]
            target = dst.at[pl.ds(0, 512), span(slot_of(depth, x, y) * 256, 256)]

            @pl.when(mine)
            def _():
                pltpu.make_async_copy(source, target, t_l.at[index]).start()

            @pl.when(jnp.logical_not(mine))
            def _():
                remote(
                    source, target, t_s.at[index, j], t_r.at[index, depth],
                    chip * 2 + to_core, to_depth,
                ).start()

    def token_waits(index, src, dst):
        from_core = depth // 2
        for s in range(4):
            mine = (from_core == core) & (s == depth)
            target = dst.at[pl.ds(0, 512), span(slot_of(s, x, y) * 256, 256)]
            source = src.at[pl.ds(0, 512), :]

            @pl.when(mine)
            def _():
                pltpu.make_async_copy(source, target, t_l.at[index]).wait()

            @pl.when(jnp.logical_not(mine))
            def _():
                remote(
                    source, target, t_s.at[index, 0], t_r.at[index, s], mate, depth
                ).wait_recv()
        for j in range(4):
            to_core, to_depth = j % 2, core * 2 + j // 2
            mine = (to_core == core) & (to_depth == depth)

            @pl.when(jnp.logical_not(mine))
            def _():
                remote(
                    src.at[pl.ds(j * 512, 512), :], dst.at[pl.ds(0, 512), pl.ds(0, 256)],
                    t_s.at[index, j], t_r.at[index, 0], mate, depth,
                ).wait_send()

    first, second = {}, {}

    def start_first(group):
        for part, target, to in ((0, x_row, 1), (1, y_row, 3)):
            cp = remote(
                region(group, part, 0), region(group, part, to),
                p1_s.at[group, part], p1_r.at[group, part], target, depth,
            )
            cp.start()
            first[group, part] = cp

    def start_second(group):
        for part, target, moves in (
            (0, y_row, ((0, 3), (1, 2))), (1, x_row, ((0, 1), (3, 2))),
        ):
            first[group, part].wait_recv()
            for i, (origin, to) in enumerate(moves):
                cp = remote(
                    region(group, part, origin), region(group, part, to),
                    p2_s.at[group, part, i], p2_r.at[group, part, i], target, depth,
                )
                cp.start()
                second[group, part, i] = cp

    count = len(GROUPS)
    small_copies = []
    for tick in range(count + 4):
        for step in (0, 1, 2, 3):
            group = tick - step
            if 0 <= group < count:
                depth_step(group, step)
                if step == 3:
                    start_first(group)
        if 0 <= tick - 4 < count:
            start_second(tick - 4)
        if tick == TOKEN_TICK:
            token_copies(0, x_ref, u_out)
        if tick == count - 1:
            for k in (1, 2, 3):
                cp = remote(
                    small_ref, smalls.at[depth], sm_s.at[k - 1], sm_r.at[k - 1],
                    row, (depth + k) % 4,
                )
                cp.start()
                small_copies.append(cp)
            token_copies(1, g_ref, g_out)
    token_waits(0, x_ref, u_out)
    pair = remote(
        u_out.at[pl.ds(0, 512), :], u_out.at[pl.ds(512, 512), :], pair_s, pair_r, mate, depth
    )
    pair.start()
    token_waits(1, g_ref, g_out)
    pair.wait()
    for cp in small_copies:
        cp.wait()
    small_local.wait()
    depth_done()
    for cp in second.values():
        cp.wait()
    for cp in first.values():
        cp.wait_send()
    for cp in swaps:
        cp.wait_send()


TOKEN_TICK = 7


def gather_all(q, k, v, proj, inner, outer, small, x_rolled, g_rolled):
    sd = jax.ShapeDtypeStruct
    n = len(GROUPS)
    return pl.pallas_call(
        gather_kernel,
        out_shape=(
            sd((1024, 1536), BF16),
            sd((512, 1024), BF16),
            sd((1024, 2048), BF16),
            sd((2048, 1024), BF16),
            sd((4,) + small.shape, F32),
            sd((1024, 1024), BF16),
            sd((512, 1024), BF16),
        ),
        in_specs=[VMEM] * 7 + [ANY] * 2,
        out_specs=[ANY] * 7,
        scratch_shapes=[
            DMA((PIECES,)), DMA((PIECES,)), DMA((PIECES + 1,)),
            DMA((PIECES, 3)), DMA((PIECES, 3)), DMA((PIECES, 3)), DMA((PIECES, 3)),
            DMA((3,)), DMA((3,)),
            DMA((n, 2)), DMA((n, 2)), DMA((n, 2, 2)), DMA((n, 2, 2)),
            DMA((2, 4)), DMA((2, 4)), DMA((2,)), DMA, DMA,
        ],
        compiler_params=pltpu.CompilerParams(collective_id=1, has_side_effects=True),
    )(q, k, v, proj, inner, outer, small, x_rolled, g_rolled)


SHAPES = ((256, 256), (128, 512), (128, 512), (128, 512))
UNITS = ((128, 256), (256, 128), (256, 128), (256, 128))
FULLS = ((512, 256), (256, 512), (256, 512), (256, 512))
OUTS = ((256, 128), (128, 256), (128, 256), (128, 256), (128, 1024), (1024, 128))
HALVES = ((128, 128), (128, 128), (128, 128), (128, 128), (128, 512), (512, 128))
BY_COLS = (True, False, False, False)
INNER, OUTER = 4, 5


def add_rows(dst, terms):
    rows = dst.shape[0]
    step = 32

    def body(i, carry):
        sl = pl.ds(pl.multiple_of(i * step, step), step)
        total = terms[0][sl, :].astype(F32)
        for term in terms[1:]:
            total = total + term[sl, :].astype(F32)
        dst[sl, :] = total.astype(dst.dtype)
        return carry

    lax.fori_loop(0, rows // step, body, 0)


def scatter_kernel(*refs):
    grads = refs[0:4]
    inner_ref, outer_ref, small_ref, gi_ref = refs[4:8]
    outs = refs[8:14]
    small_out, gi_out = refs[14:16]
    rest = list(refs[16:])
    own = [[rest.pop(0) for _ in range(2)] for _ in range(4)]
    got1 = [[rest.pop(0) for _ in range(2)] for _ in range(4)]
    got2 = [[rest.pop(0) for _ in range(2)] for _ in range(4)]
    full = [rest.pop(0) for _ in range(4)]
    zgot = [rest.pop(0) for _ in range(4)]
    fin = [rest.pop(0) for _ in range(4)]
    cgot = [rest.pop(0) for _ in range(6)]
    sb = rest.pop(0)
    sg = rest.pop(0)
    (o_s, p1_s, p1_r, p2_s, p2_r, z_s, z_r, c_s, c_r, sm_s, sm_r, t_s, t_r, t_l) = rest

    row, depth, core, chip, x, y = place()
    mate = chip * 2 + (1 - core)
    x_row = (y * 2 + 1 - x) * 2 + core
    y_row = ((1 - y) * 2 + x) * 2 + core
    greet(row, depth, core, chip, x, y)

    def region(group, part, block):
        rows = SHAPES[group][0]
        if BY_COLS[group]:
            return grads[group].at[pl.ds(part * rows, rows), span(block * 256, 256)]
        return grads[group].at[span(block * 256 + part * 128, 128), :]

    def unit(group, z):
        if BY_COLS[group]:
            return full[group].at[span(z * UNITS[group][0], UNITS[group][0]), :]
        return full[group].at[:, span(z * UNITS[group][1], UNITS[group][1])]

    def side(group, half):
        if group == OUTER:
            return outer_ref.at[:, span(half * 128, 128)]
        if group == INNER:
            return inner_ref.at[span(half * 128, 128), :]
        if BY_COLS[group]:
            return fin[group].at[:, span(half * 128, 128)]
        return fin[group].at[span(half * 128, 128), :]

    def out_side(group, half):
        if group == OUTER:
            return outs[5].at[span(half * 512, 512), :]
        if group == INNER:
            return outs[4].at[:, span(half * 512, 512)]
        size = HALVES[group]
        if BY_COLS[group]:
            return outs[group].at[span(half * size[0], size[0]), :]
        return outs[group].at[:, span(half * size[1], size[1])]

    copies = {}

    def start_first(group):
        for part in (0, 1):
            target = y_row if part == 0 else x_row
            for i in (0, 1):
                kept = ((0, 1), (0, 3))[part][i]
                sent = ((3, 2), (1, 2))[part][i]
                lc = pltpu.make_async_copy(
                    region(group, part, kept), own[group][part].at[i], o_s.at[group, part, i]
                )
                lc.start()
                cp = remote(
                    region(group, part, sent), got1[group][part].at[i],
                    p1_s.at[group, part, i], p1_r.at[group, part, i], target, depth,
                )
                cp.start()
                copies["o", group, part, i] = lc
                copies["p1", group, part, i] = cp

    def start_second(group):
        for part in (0, 1):
            target = x_row if part == 0 else y_row
            for i in (0, 1):
                copies["o", group, part, i].wait()
                copies["p1", group, part, i].wait_recv()
            other = own[group][part].at[1]
            add_rows(other, (other, got1[group][part].at[1]))
            cp = remote(
                other, got2[group][part], p2_s.at[group, part], p2_r.at[group, part], target, depth
            )
            cp.start()
            copies["p2", group, part] = cp

    def send_depth(group):
        for k in (1, 2, 3):
            cp = remote(
                unit(group, (depth + k) % 4), zgot[group].at[k - 1],
                z_s.at[group, k - 1], z_r.at[group, k - 1], row, (depth + k) % 4,
            )
            cp.start()
            copies["z", group, k] = cp

    def start_depth(group):
        rows = SHAPES[group][0]
        for part in (0, 1):
            copies["p2", group, part].wait_recv()
            add_rows(
                full[group].at[pl.ds(part * rows, rows), :],
                (own[group][part].at[0], got1[group][part].at[0], got2[group][part]),
            )
        send_depth(group)

    def send_core(group):
        cp = remote(
            side(group, 1 - core), cgot[group], c_s.at[group], c_r.at[group], mate, depth
        )
        cp.start()
        copies["c", group] = cp

    def start_core(group):
        for k in (1, 2, 3):
            copies["z", group, k].wait_recv()
        add_rows(
            fin[group],
            (unit(group, depth), zgot[group].at[0], zgot[group].at[1], zgot[group].at[2]),
        )
        send_core(group)

    def finish(group):
        add_rows(out_side(group, core), (side(group, core),))
        copies["c", group].wait_recv()
        add_rows(out_side(group, 1 - core), (cgot[group],))

    def token_copies(index, src, dst):
        j = (depth % 2) * 2 + core
        to_core = depth // 2
        for z in range(4):
            mine = (to_core == core) & (z == depth)
            source = src.at[:, span(slot_of(z, x, y) * 256, 256)]
            target = dst.at[span(j * 512, 512), :]

            @pl.when(mine)
            def _():
                pltpu.make_async_copy(source, target, t_l.at[index]).start()

            @pl.when(jnp.logical_not(mine))
            def _():
                remote(
                    source, target, t_s.at[index, z], t_r.at[index, j], chip * 2 + to_core, z
                ).start()

    def token_waits(index, src, dst):
        to_core = depth // 2
        for j in range(4):
            from_core, from_depth = j % 2, core * 2 + j // 2
            mine = (from_core == core) & (from_depth == depth)
            target = dst.at[pl.ds(j * 512, 512), :]
            source = src.at[:, pl.ds(0, 256)]

            @pl.when(mine)
            def _():
                pltpu.make_async_copy(source, target, t_l.at[index]).wait()

            @pl.when(jnp.logical_not(mine))
            def _():
                remote(
                    source, target, t_s.at[index, 0], t_r.at[index, j], mate, depth
                ).wait_recv()
        for z in range(4):
            mine = (to_core == core) & (z == depth)

            @pl.when(jnp.logical_not(mine))
            def _():
                remote(
                    src.at[:, pl.ds(z * 256, 256)], dst.at[pl.ds(0, 512), :],
                    t_s.at[index, z], t_r.at[index, 0], mate, depth,
                ).wait_send()

    def small_send(step, slot, target_row, target_depth):
        cp = remote(
            sb.at[step], sg.at[slot], sm_s.at[slot], sm_r.at[slot], target_row, target_depth
        )
        cp.start()
        copies["s", slot] = cp

    def small_add(step, slot):
        copies["s", slot].wait_recv()
        sb[step + 1] = sb[step] + sg[slot]

    sb[0] = small_ref[...]
    for group in range(4):
        start_first(group)
    small_send(0, 0, mate, depth)
    send_core(OUTER)
    send_core(INNER)
    token_copies(0, gi_ref, gi_out)
    small_add(0, 0)
    small_send(1, 1, x_row, depth)
    finish(OUTER)
    finish(INNER)
    for group in range(4):
        start_second(group)
        if group == 0:
            small_add(1, 1)
            small_send(2, 2, y_row, depth)
        if group > 0:
            start_depth(group - 1)
    small_add(2, 2)
    for k in (1, 2, 3):
        small_send(3, 2 + k, row, (depth + k) % 4)
    start_depth(3)
    for group in (0, 1, 2):
        start_core(group)
    for k in (1, 2, 3):
        copies["s", 2 + k].wait_recv()
    small_out[...] = ((sb[3] + sg[3]) + sg[4]) + sg[5]
    for group in (0, 1, 2):
        finish(group)
    start_core(3)
    token_waits(0, gi_ref, gi_out)
    finish(3)
    for key, cp in copies.items():
        if key[0] != "o":
            cp.wait_send()


def scatter_all(proj, q, k, v, inner, outer, small, gi):
    sd = jax.ShapeDtypeStruct
    scratch = []
    for size in SHAPES:
        scratch += [pltpu.VMEM((2,) + size, BF16)] * 2
    for size in SHAPES:
        scratch += [pltpu.VMEM((2,) + size, BF16)] * 2
    for size in SHAPES:
        scratch += [pltpu.VMEM(size, BF16)] * 2
    scratch += [pltpu.VMEM(size, BF16) for size in FULLS]
    scratch += [pltpu.VMEM((3,) + size, BF16) for size in UNITS]
    scratch += [pltpu.VMEM(size, BF16) for size in UNITS]
    scratch += [pltpu.VMEM(size, BF16) for size in HALVES]
    scratch += [pltpu.VMEM((4,) + small.shape, F32), pltpu.VMEM((6,) + small.shape, F32)]
    scratch += [
        DMA((4, 2, 2)), DMA((4, 2, 2)), DMA((4, 2, 2)), DMA((4, 2)), DMA((4, 2)),
        DMA((4, 3)), DMA((4, 3)), DMA((6,)), DMA((6,)), DMA((6,)), DMA((6,)),
        DMA((1, 4)), DMA((1, 4)), DMA((1,)),
    ]
    return pl.pallas_call(
        scatter_kernel,
        out_shape=tuple(sd(size, F32) for size in OUTS)
        + (sd(small.shape, F32), sd((2048, 256), BF16)),
        in_specs=[ANY] * 4 + [VMEM] * 3 + [ANY],
        out_specs=[VMEM] * 7 + [ANY],
        scratch_shapes=scratch,
        compiler_params=pltpu.CompilerParams(
            collective_id=2, has_side_effects=True, vmem_limit_bytes=48 * 1024 * 1024
        ),
    )(proj, q, k, v, inner, outer, small, gi)


def attend_kernel(flag_ref, q_ref, k_ref, v_ref, idq_ref, idk_ref, o_ref, lse_ref):
    rows = q_ref.shape[0]
    lane = lax.broadcasted_iota(jnp.int32, (1, 128), 1)
    low_half = lane < HEAD_DIM

    def compute(masked):
        keys = k_ref[...]
        values = v_ref[...]
        halves = (low_half, jnp.logical_not(low_half))
        sub = 256
        units = [(i, h) for i in range(rows // sub) for h in (0, 1)]

        def score(unit):
            i, h = unit
            scaled = q_ref[i * sub : (i + 1) * sub, :] * jnp.asarray(HEAD_DIM**-0.5, BF16)
            s = against(jnp.where(halves[h], scaled, jnp.zeros_like(scaled)), keys)
            if masked:
                s = jnp.where(idq_ref[i * sub : (i + 1) * sub, :] == idk_ref[...], s, NEG_FILL)
            return s

        def soft(s):
            top = jnp.max(s, axis=1, keepdims=True)
            weights = jnp.exp(s - top)
            return weights.astype(BF16), jnp.sum(weights, axis=1, keepdims=True), top

        skew = 1
        pending = [score(u) for u in units[:skew]]
        done = {}
        for n, unit in enumerate(units):
            if n + skew < len(units):
                pending.append(score(units[n + skew]))
            low, total, top = soft(pending.pop(0))
            mixed = matmul(low, values)
            done[unit] = (mixed / total, top + jnp.log(total))
            i, h = unit
            if h == 1:
                sl = slice(i * sub, (i + 1) * sub)
                a, b = done[i, 0], done[i, 1]
                o_ref[sl, :] = jnp.where(low_half, a[0], b[0]).astype(o_ref.dtype)
                lse_ref[sl, :] = jnp.where(low_half, a[1], b[1])

    @pl.when(flag_ref[0] == 1)
    def _():
        compute(False)

    @pl.when(flag_ref[0] != 1)
    def _():
        compute(True)


def attend(flag, qkv, id_col, id_row):
    tokens, width = qkv.shape[0], qkv.shape[1] // 3
    pairs = width // 128
    block = tokens
    return pl.pallas_call(
        attend_kernel,
        out_shape=(
            jax.ShapeDtypeStruct((tokens, width), BF16),
            jax.ShapeDtypeStruct((tokens, width), F32),
        ),
        grid_spec=pltpu.PrefetchScalarGridSpec(
            num_scalar_prefetch=1,
            grid=(width // 128, tokens // block),
            in_specs=[
                pl.BlockSpec((block, 128), lambda h, i, f: (i, h)),
                pl.BlockSpec((tokens, 128), lambda h, i, f: (0, h + pairs)),
                pl.BlockSpec((tokens, 128), lambda h, i, f: (0, h + 2 * pairs)),
                pl.BlockSpec((block, 1), lambda h, i, f: (i, 0)),
                pl.BlockSpec((1, tokens), lambda h, i, f: (0, 0)),
            ],
            out_specs=[
                pl.BlockSpec((block, 128), lambda h, i, f: (i, h)),
                pl.BlockSpec((block, 128), lambda h, i, f: (i, h)),
            ],
        ),
        compiler_params=pltpu.CompilerParams(
            dimension_semantics=("arbitrary", "arbitrary"), vmem_limit_bytes=48 * 1024 * 1024
        ),
        cost_estimate=pl.CostEstimate(
            flops=20_000_000_000, bytes_accessed=8_000_000, transcendentals=0
        ),
        name="attend",
    )(flag, qkv, qkv, qkv, id_col, id_row)


def attend_back_kernel(
    flag_ref, q_ref, k_ref, v_ref, do_ref, lse_ref, idk_ref, idq_ref,
    dq_ref, dk_ref, dv_ref,
):
    rows = q_ref.shape[0]
    scale = HEAD_DIM**-0.5
    lane = lax.broadcasted_iota(jnp.int32, (1, 128), 1)
    low_half = lane < HEAD_DIM

    def compute(masked):
        queries = q_ref[...]
        scaled = queries * jnp.asarray(scale, BF16)
        keys = k_ref[...]
        values = v_ref[...]
        grads = do_ref[...]
        lse_t = lse_ref[...].T
        q_t, k_t, do_t = queries.T, keys.T, grads.T
        dqs, dks, dvs = [], [], []
        for head in (0, 1):
            here = low_half if head == 0 else jnp.logical_not(low_half)
            part = slice(head * HEAD_DIM, (head + 1) * HEAD_DIM)
            zero = jnp.zeros_like(keys)
            scores = against(jnp.where(here, keys, zero), scaled)
            if masked:
                scores = jnp.where(idk_ref[...] == idq_ref[...], scores, NEG_FILL)
            log_row = lse_t[head * HEAD_DIM : head * HEAD_DIM + 1, :]
            probs = jnp.exp(scores - log_row)
            grad_probs = against(jnp.where(here, values, zero), grads)
            moved = probs * grad_probs
            delta = jnp.sum(moved, axis=0, keepdims=True)
            grad_scores = (moved - probs * delta).astype(BF16)
            low = probs.astype(BF16)
            dvs.append(against(do_t[part], low))
            dks.append(matmul(grad_scores, queries))
            dqs.append(matmul(k_t[part], grad_scores))
        dv_ref[...] = jnp.concatenate(dvs, axis=0).T.astype(BF16)
        dk_ref[...] = (jnp.where(low_half, dks[0], dks[1]) * scale).astype(BF16)
        dq_ref[...] = (jnp.concatenate(dqs, axis=0) * scale).T.astype(BF16)

    @pl.when(flag_ref[0] == 1)
    def _():
        compute(False)

    @pl.when(flag_ref[0] != 1)
    def _():
        compute(True)


def attend_back(flag, qkv, do, lse, id_col, id_row, first=0, count=4):
    tokens, width = qkv.shape[0], qkv.shape[1] // 3
    pairs = width // 128
    block = tokens
    shape = jax.ShapeDtypeStruct((tokens, count * 128), BF16)
    rows = pl.BlockSpec((block, 128), lambda h, i, f: (i, h + first))
    return pl.pallas_call(
        attend_back_kernel,
        out_shape=(shape, shape, shape),
        grid_spec=pltpu.PrefetchScalarGridSpec(
            num_scalar_prefetch=1,
            grid=(count, tokens // block),
            in_specs=[
                rows,
                pl.BlockSpec((tokens, 128), lambda h, i, f: (0, h + first + pairs)),
                pl.BlockSpec((tokens, 128), lambda h, i, f: (0, h + first + 2 * pairs)),
                rows, rows,
                pl.BlockSpec((tokens, 1), lambda h, i, f: (0, 0)),
                pl.BlockSpec((1, block), lambda h, i, f: (0, i)),
            ],
            out_specs=[
                pl.BlockSpec((block, 128), lambda h, i, f: (i, h)),
                pl.BlockSpec((tokens, 128), lambda h, i, f: (0, h)),
                pl.BlockSpec((tokens, 128), lambda h, i, f: (0, h)),
            ],
        ),
        compiler_params=pltpu.CompilerParams(
            dimension_semantics=("arbitrary", "arbitrary"), vmem_limit_bytes=48 * 1024 * 1024
        ),
        cost_estimate=pl.CostEstimate(
            flops=10_000_000_000 * count, bytes_accessed=2_500_000 * count, transcendentals=0
        ),
        name="attend_back",
    )(flag, qkv, qkv, qkv, do, lse, id_col, id_row)


def gelu_pair(inner):
    size = jnp.abs(inner)
    bell = jnp.exp(inner * (inner * -0.5))
    t = 1.0 / (1.0 + (0.3275911 * 0.5**0.5) * size)
    poly = (0.5 * 1.061405429) * t - 0.5 * 1.453152027
    poly = poly * t + 0.5 * 1.421413741
    poly = poly * t - 0.5 * 0.284496736
    poly = poly * t + 0.5 * 0.254829592
    tail = (poly * t) * bell
    below = jnp.where(inner >= 0.0, 1.0 - tail, tail)
    return (inner * below).astype(BF16), (below + inner * (bell * 0.3989422804014327)).astype(BF16)


def ffn_in_kernel(x_ref, w_ref, b_ref, active_ref, slope_ref):
    rows, cols = active_ref.shape
    sub = 128
    skew = 1

    def open_unit(i):
        return matmul(x_ref[i * sub : (i + 1) * sub, :], w_ref[...]) + b_ref[...]

    count = rows // sub
    pending = [open_unit(i) for i in range(skew)]
    for i in range(count):
        if i + skew < count:
            pending.append(open_unit(i + skew))
        active, slope = gelu_pair(pending.pop(0))
        active_ref[i * sub : (i + 1) * sub, :] = active
        slope_ref[i * sub : (i + 1) * sub, :] = slope


def ffn_in(x, w, bias):
    tokens, depth = x.shape
    hidden = w.shape[1]
    rows, cols = 1024, 512
    shape = jax.ShapeDtypeStruct((tokens, hidden), BF16)
    out = pl.BlockSpec((rows, cols), lambda n, m: (m, n))
    return pl.pallas_call(
        ffn_in_kernel,
        out_shape=(shape, shape),
        grid=(hidden // cols, tokens // rows),
        in_specs=[
            pl.BlockSpec((rows, depth), lambda n, m: (m, 0)),
            pl.BlockSpec((depth, cols), lambda n, m: (0, n)),
            pl.BlockSpec((1, cols), lambda n, m: (0, n)),
        ],
        out_specs=[out, out],
        compiler_params=pltpu.CompilerParams(
            dimension_semantics=("arbitrary", "arbitrary"), vmem_limit_bytes=48 * 1024 * 1024
        ),
        cost_estimate=pl.CostEstimate(
            flops=14_000_000_000, bytes_accessed=14_000_000, transcendentals=0
        ),
        name="ffn_in",
    )(x, w, bias)


def exchange(values):
    pairs = [(r, r + 1 - 2 * (r % 2)) for r in range(8)]
    return lax.ppermute(values, "row", pairs)


def both(own):
    return jnp.concatenate([own, exchange(own)], axis=0)


def share_sum(left, weight, product, apart=False):
    mate_part, left_own = lax.optimization_barrier(
        (rounded(product(left[512:], weight)), left[:512])
    )
    own_part, other = product(left_own, weight), exchange(mate_part)
    if apart:
        own_part, other = lax.optimization_barrier((own_part, other))
    return own_part + other.astype(F32)


def norm_rows(summed, gain, shift):
    center = jnp.mean(summed, axis=1, keepdims=True)
    spread = jnp.mean(summed * summed, axis=1, keepdims=True) - center * center
    inverse = lax.rsqrt(spread + EPSILON)
    normed = (summed - center) * inverse
    return normed * gain + shift, normed, inverse


def norm_rows_back(grad_output, normed, inverse, gain):
    scaled = grad_output * gain
    mean_one = jnp.mean(scaled, axis=1, keepdims=True)
    mean_two = jnp.mean(scaled * normed, axis=1, keepdims=True)
    grad_input = inverse * (scaled - mean_one - normed * mean_two)
    return grad_input, token_sum(grad_output * normed), token_sum(grad_output)


def fast_forward(hidden, weights, vectors, ids, whole_in=None):
    wqkv, wproj, winner, wouter = weights
    flag, id_col, id_row = ids
    if whole_in is None:
        whole_in = both(rounded(hidden))
    qkv = rounded(matmul(whole_in, wqkv) + vectors["qkv"])
    attended, lse = attend(flag, qkv, id_col, id_row)
    branch = share_sum(attended, wproj, matmul, True) + vectors["proj"]
    first, normed_one, inverse_one = norm_rows(
        hidden + branch, vectors["attn_gain"], vectors["attn_shift"]
    )
    whole_mid = both(rounded(first))
    active, slope = ffn_in(whole_mid, winner, vectors["inner"])
    ffn = share_sum(active, wouter, matmul, True) + vectors["outer"]
    output, normed_two, inverse_two = norm_rows(
        first + ffn, vectors["ffn_gain"], vectors["ffn_shift"]
    )
    kept = (
        whole_in, qkv, lse, attended, normed_one, inverse_one,
        whole_mid, active, slope, normed_two, inverse_two,
    )
    return output, kept


def fast_backward(grad_output, kept, weights, vectors, ids, later=None, beside=None):
    (
        whole_in, qkv, lse, attended, normed_one, inverse_one,
        whole_mid, active, slope, normed_two, inverse_two,
    ) = kept
    wqkv, wproj, winner, wouter = weights
    flag, id_col, id_row = ids
    grad_second, ffn_gain_sum, ffn_shift_sum = norm_rows_back(
        grad_output, normed_two, inverse_two, vectors["ffn_gain"]
    )
    ffn_low = rounded(grad_second)
    whole_second = both(ffn_low)
    inner_low = rounded(against(whole_second, wouter) * slope.astype(F32))
    if later is None:
        outer_terms = rounded(over_tokens(active, whole_second))
    else:
        outer_terms = add_trees(outer_pieces(active, whole_second), outer_cuts(later[0]))
        outer_planes = [Plane(outer_terms, h, 1) for h in (0, 1)]
        outer_got = [p.step_one() for p in outer_planes]
    grad_first = grad_second + share_sum(inner_low, winner, against)
    inner_terms = rounded(add_later(over_tokens(whole_mid, inner_low), later, 1))
    if later is not None:
        inner_planes = [Plane(inner_cuts(inner_terms), h, 0) for h in (0, 1)]
        inner_got = [p.step_one() for p in inner_planes]
    grad_attn, attn_gain_sum, attn_shift_sum = norm_rows_back(
        grad_first, normed_one, inverse_one, vectors["attn_gain"]
    )
    attn_low = rounded(grad_attn)
    whole_attn = both(attn_low)
    mixed_grad = rounded(against(whole_attn, wproj))
    proj_term = over_tokens(attended, whole_attn)
    if later is None:
        grads = attend_back(flag, qkv, mixed_grad, lse, id_col, id_row)
        if beside is not None:
            beside, grads = lax.optimization_barrier((beside, grads))
        outer_terms, inner_terms = (outer_terms, inner_terms), beside
    else:
        early = attend_back(flag, qkv, mixed_grad, lse, id_col, id_row, 0, 2)
        outer_got, early = lax.optimization_barrier((outer_got, early))
        outer_hand = [p.to_hand(g) for p, g in zip(outer_planes, outer_got)]
        outer_hand, mixed_grad = lax.optimization_barrier((outer_hand, mixed_grad))
        outer_more = [p.step_two(v) for p, v in zip(outer_planes, outer_hand)]
        late = attend_back(flag, qkv, mixed_grad, lse, id_col, id_row, 2, 2)
        inner_got, late = lax.optimization_barrier((inner_got, late))
        inner_hand = [p.to_hand(g) for p, g in zip(inner_planes, inner_got)]
        inner_hand, outer_more, late = lax.optimization_barrier((inner_hand, outer_more, late))
        inner_more = [p.step_two(v) for p, v in zip(inner_planes, inner_hand)]
        outer_terms = fold_depth([p.close(m) for p, m in zip(outer_planes, outer_more)], 0)
        inner_terms = fold_depth([p.close(m) for p, m in zip(inner_planes, inner_more)], 1)
        grads = tuple(jnp.concatenate(pair, axis=1) for pair in zip(early, late))
    grad_qkv = jnp.concatenate(grads, axis=1)
    grad_input = grad_attn + share_sum(grad_qkv, wqkv, against)
    terms = (proj_term,) + tuple(
        over_tokens(whole_in, part) for part in grads
    )
    small = (
        token_sum(grads[0]), token_sum(grads[2]), token_sum(attn_low),
        attn_gain_sum, attn_shift_sum, token_sum(inner_low), token_sum(ffn_low),
        ffn_gain_sum, ffn_shift_sum,
    )
    return grad_input, terms, outer_terms, inner_terms, small


def flip_row(bit):
    return [(r, r + bit - 2 * bit * ((r // bit) % 2)) for r in range(8)]


CUTS = (((512, 1024), (256, 512), (0, 256)), ((256, 768), (768, 1024), (0, 256)))


def outer_pieces(active, relative):
    return [
        [over_tokens(active[:, h * 1024 : (h + 1) * 1024], relative[:, a:b]) for a, b in CUTS[h]]
        for h in (0, 1)
    ]


def add_trees(left, right):
    return jax.tree.map(lambda p, q: p + q.astype(F32), left, right)


def outer_cuts(whole):
    return [
        [whole[h * 1024 : (h + 1) * 1024, a:b] for a, b in CUTS[h]] for h in (0, 1)
    ]


def inner_cuts(whole):
    return [
        [whole[a:b, h * 1024 : (h + 1) * 1024] for a, b in CUTS[h]] for h in (0, 1)
    ]


def add_later(term, later, index):
    return term if later is None else term + later[index].astype(F32)


class Plane:
    def __init__(self, pieces, half, axis):
        sent, handed, own = pieces[half]
        self.sent = rounded(sent)
        self.handed, self.own = handed.astype(F32), own.astype(F32)
        self.half, self.axis = half, axis
        self.first, self.second = (4, 2) if half == 0 else (2, 4)

    def step_one(self):
        return lax.ppermute(self.sent, "row", flip_row(self.first))

    def to_hand(self, got):
        low, high = jnp.split(got, 2, axis=self.axis)
        self.got, handed = (high, low) if self.half == 0 else (low, high)
        return rounded(self.handed + handed.astype(F32))

    def step_two(self, handed):
        return lax.ppermute(handed, "row", flip_row(self.second))

    def close(self, more):
        return rounded(self.own + self.got.astype(F32) + more.astype(F32))


def fold_depth(halves, axis):
    depth = lax.axis_index("col")

    def unit(z):
        picked = [lax.dynamic_slice_in_dim(half, z * 256, 256, axis) for half in halves]
        return jnp.concatenate(picked, axis=axis)

    total = unit(depth).astype(F32)
    for k in (1, 2, 3):
        pairs = [(z, (z + k) % 4) for z in range(4)]
        total = total + lax.ppermute(unit((depth + k) % 4), "col", pairs).astype(F32)
    return rounded(total)


def spread_out(values):
    core = lax.axis_index("row") % 2
    depth = lax.axis_index("col")
    j = (depth % 2) * 2 + core
    x, y = place()[4:]
    parts = []
    for k in range(4):
        pairs = []
        for r in range(8):
            for z in range(4):
                block = ((z % 2) * 2 + r % 2 + k) % 4
                pairs.append((r * 4 + z, (r // 2 * 2 + z // 2) * 4 + block))
        piece = lax.dynamic_slice_in_dim(values, slot_of((j + k) % 4, x, y) * 256, 256, 1)
        parts.append(lax.ppermute(piece, ("row", "col"), pairs))
    return parts


def join_parts(parts, own_start):
    depth = lax.axis_index("col")
    cycle = jnp.concatenate(parts[::-1] * 2, axis=0)
    start = ((3 - depth) * 512 - own_start + 2048) % 2048
    return lax.dynamic_slice(cycle, (start, 0), (2048, 256)).astype(F32)


VECTORS = (
    ("q", 256), ("v", 256), ("proj", 256), ("attn_gain", 256), ("attn_shift", 256),
    ("inner", 1024), ("outer", 256), ("ffn_gain", 256), ("ffn_shift", 256),
)
SPLIT = ("q", "v", "inner")


def fast_device(
    hidden_in,
    query_weight,
    key_weight,
    value_weight,
    query_bias,
    value_bias,
    proj_weight,
    proj_bias,
    attn_gain,
    attn_shift,
    inner_weight,
    inner_bias,
    outer_weight,
    outer_bias,
    ffn_gain,
    ffn_shift,
    segment_ids,
    grad_out,
):
    core = lax.axis_index("row") % 2
    depth = lax.axis_index("col")
    own_ids = segment_ids[0]
    mate_ids = exchange(own_ids)

    def big_start(ids):
        found = ids[:1025] == ids[1023:]
        return jnp.sum(jnp.where(found, jnp.arange(1025, dtype=jnp.int32), 0))

    own_start = big_start(own_ids)
    ids = jnp.where(depth // 2 == core, own_ids, mate_ids)
    ids = lax.dynamic_slice(
        jnp.concatenate([ids, ids[:1024]]), (big_start(ids),), (2048,)
    ).reshape(2, 2, 512)
    ids = lax.dynamic_index_in_dim(ids, depth % 2, 0, keepdims=False)
    ids = jnp.where(core == 0, ids, ids[::-1]).reshape(1024)
    flag = (1 - depth % 2).reshape(1).astype(jnp.int32)
    ids = (flag, ids[:, None], ids[None, :])

    def turned(values):
        longer = jnp.concatenate([values, values[:1024]], axis=0)
        return lax.dynamic_slice(longer, (own_start, 0), (2048, 256))

    def turned_back(values):
        longer = jnp.concatenate([values[1024:], values], axis=0)
        return lax.dynamic_slice(longer, (1024 - own_start, 0), (2048, 256)).astype(F32)

    small = jnp.concatenate(
        [
            query_bias, value_bias, proj_bias, attn_gain, attn_shift,
            inner_bias, outer_bias, ffn_gain, ffn_shift,
        ]
    ).reshape(24, 128)
    wqkv, wproj, winner, wouter, smalls, start_low, grad_low = gather_all(
        query_weight, key_weight, value_weight, proj_weight, inner_weight, outer_weight,
        small, turned(hidden_in), turned(grad_out),
    )
    smalls = smalls.reshape(4, 3072)
    x, y = place()[4:]
    order = (y * 2 + x, y * 2 + 1 - x, (1 - y) * 2 + 1 - x, (1 - y) * 2 + x)
    placed = jnp.stack([lax.dynamic_index_in_dim(smalls, b, 0, keepdims=False) for b in order])
    weights = (wqkv, wproj, winner, wouter)
    vectors, offset = {}, 0
    for name, size in VECTORS:
        part = (smalls if name in SPLIT else placed)[:, offset : offset + size]
        offset += size
        if name in SPLIT:
            part = jnp.where(core == 0, part[:, : size // 2], part[:, size // 2 :])
        vectors[name] = part.reshape(1, -1)
    vectors["inner"] = (
        vectors["inner"].reshape(4, 2, 256).transpose(1, 0, 2).reshape(1, 2048)
    )
    vectors["qkv"] = jnp.concatenate(
        [vectors["q"], jnp.zeros_like(vectors["q"]), vectors["v"]], axis=1
    )

    middle, kept_one = fast_forward(
        start_low[:512].astype(F32), weights, vectors, ids, start_low
    )
    final_out, kept_two = fast_forward(middle, weights, vectors, ids)
    grad_flow = grad_low.astype(F32)
    parts = spread_out(rounded(final_out))
    grad_flow, terms_two, ffn_two, parts, small_two = fast_backward(
        grad_flow, kept_two, weights, vectors, ids, None, parts
    )
    hidden_out = join_parts(parts, own_start)
    grad_flow, terms_one, outer_full, inner_full, small_one = fast_backward(
        grad_flow, kept_one, weights, vectors, ids, ffn_two
    )
    terms = [rounded(a + b) for a, b in zip(terms_two, terms_one)]
    pieces = []
    for (name, size), a, b in zip(VECTORS, small_two, small_one):
        total = a + b
        if name not in SPLIT:
            blocks = total.reshape(4, 256)
            total = jnp.stack(
                [
                    lax.dynamic_index_in_dim(blocks, slot_of(n, x, y), 0, keepdims=False)
                    for n in range(4)
                ]
            )
        if name in SPLIT:
            half = total.reshape(4, 1, size // 2)
            if name == "inner":
                half = total.reshape(2, 4, 256).transpose(1, 0, 2).reshape(4, 1, 512)
            zero = jnp.zeros_like(half)
            total = jnp.where(
                core == 0,
                jnp.concatenate([half, zero], axis=1),
                jnp.concatenate([zero, half], axis=1),
            )
        pieces.append(total.reshape(-1))
    small_sum = jnp.concatenate(pieces).reshape(96, 128)
    results = scatter_all(*terms, inner_full, outer_full, small_sum, rounded(grad_flow))
    proj_g, q_g, k_g, v_g, inner_g, outer_g, small_all, grad_turned = results
    small_all = small_all.reshape(-1)
    sums, offset = {}, 0
    for name, size in VECTORS:
        sums[name] = lax.dynamic_slice(small_all, (offset + depth * size,), (size,))
        offset += 4 * size
    return (
        hidden_out,
        turned_back(grad_turned),
        q_g,
        k_g,
        v_g,
        sums["q"],
        sums["v"],
        proj_g,
        sums["proj"],
        sums["attn_gain"],
        sums["attn_shift"],
        inner_g,
        sums["inner"],
        outer_g,
        sums["outer"],
        sums["ffn_gain"],
        sums["ffn_shift"],
    )


def solution(mesh):
    in_specs = (
        P("row", "col"),
        P("row", "col"),
        P("row", "col"),
        P("row", "col"),
        P("col"),
        P("col"),
        P("col", "row"),
        P("col"),
        P("col"),
        P("col"),
        P("row", "col"),
        P("col"),
        P("col", "row"),
        P("col"),
        P("col"),
        P("col"),
        P("row", None),
        P("row", "col"),
    )
    out_specs = (
        P("row", "col"),
        P("row", "col"),
        P("row", "col"),
        P("row", "col"),
        P("row", "col"),
        P("col"),
        P("col"),
        P("col", "row"),
        P("col"),
        P("col"),
        P("col"),
        P("row", "col"),
        P("col"),
        P("col", "row"),
        P("col"),
        P("col"),
        P("col"),
    )
    same = dict(mesh.shape) == {"row": 8, "col": 4}
    return jax.shard_map(
        fast_device if same else general_device, mesh=mesh, in_specs=in_specs, out_specs=out_specs, check_vma=False
    )
```

```python
import functools

import jax
import jax.numpy as jnp
from jax import lax
from jax.experimental import pallas as pl
from jax.experimental.pallas import tpu as pltpu
from jax.sharding import PartitionSpec as P

NEG_FILL = -1e30
HEAD_DIM = 64
D = 1024
LEN = 2048
QBLOCK = 512
SEQS = 1


EPSILON = 1e-06


def rounded(values):
    return values.astype(jnp.bfloat16)


def matmul(left, right):
    return jnp.dot(left, right, preferred_element_type=jnp.float32)


def over_tokens(left, right):
    return lax.dot_general(
        left, right, (((0,), (0,)), ((), ())), preferred_element_type=jnp.float32
    )


def against(left, right):
    return lax.dot_general(
        left, right, (((1,), (1,)), ((), ())), preferred_element_type=jnp.float32
    )


def token_sum(values):
    return jnp.sum(values, axis=0, dtype=jnp.float32)


def exact_gelu(inputs):
    return jax.nn.gelu(inputs, approximate=False)


def gather_weights(shards):
    front_set = (
        lax.all_gather(shards[0], "row", axis=0, tiled=True),
        lax.all_gather(shards[1], "row", axis=0, tiled=True),
        lax.all_gather(shards[2], "row", axis=0, tiled=True),
        lax.all_gather(shards[3], "row", axis=0, tiled=True),
    )
    back_set = (
        lax.all_gather(shards[4], "row", axis=1, tiled=True),
        lax.all_gather(shards[5], "row", axis=1, tiled=True),
    )
    proj_cols = back_set[0]
    return (
        front_set[0],
        front_set[1],
        front_set[2],
        front_set[3],
        back_set[0],
        back_set[1],
        proj_cols,
    )


def spread_features(values):
    return lax.all_gather(rounded(values), "col", axis=1, tiled=True)


def sum_partials(partial_terms):
    return lax.psum_scatter(
        partial_terms.astype(jnp.bfloat16), "col", scatter_dimension=1, tiled=True
    ).astype(jnp.float32)


def spread_grads(values):
    return lax.all_gather(values, "col", axis=1, tiled=True)


def sum_grad_partials(partial_terms):
    return lax.psum_scatter(
        partial_terms.astype(jnp.bfloat16), "col", scatter_dimension=1, tiled=True
    ).astype(jnp.float32)


def norm_forward(summed, norm_gain, norm_shift):
    totals = lax.psum((jnp.sum(summed, axis=1), jnp.sum(summed * summed, axis=1)), "col")
    center = totals[0][:, None] / D
    spread = totals[1][:, None] / D - center * center
    inverse = lax.rsqrt(spread + EPSILON)
    normed = (summed - center) * inverse
    return (normed * norm_gain + norm_shift, normed, inverse)


def norm_backward(grad_output, normed, inverse, norm_gain):
    scaled = grad_output * norm_gain
    totals = lax.psum((jnp.sum(scaled, axis=1), jnp.sum(scaled * normed, axis=1)), "col")
    grad_input = inverse * (scaled - totals[0][:, None] / D - normed * (totals[1][:, None] / D))
    return (grad_input, jnp.sum(grad_output * normed, axis=0), jnp.sum(grad_output, axis=0))


def split_heads(values):
    return values.reshape(SEQS, LEN, values.shape[1] // HEAD_DIM, HEAD_DIM)


def attend_forward(queries, key_rows, value_rows, segments):
    score_scale = HEAD_DIM ** (-0.5)
    blocks = LEN // QBLOCK
    query_heads = split_heads(queries)
    key_heads = split_heads(key_rows)
    value_heads = split_heads(value_rows)

    def attend_one_block(block_index):
        sequence = block_index // blocks
        offset = block_index % blocks * QBLOCK
        seq_queries = lax.dynamic_index_in_dim(query_heads, sequence, 0, keepdims=False)
        seq_keys = lax.dynamic_index_in_dim(key_heads, sequence, 0, keepdims=False)
        seq_values = lax.dynamic_index_in_dim(value_heads, sequence, 0, keepdims=False)
        seq_segments = lax.dynamic_index_in_dim(segments, sequence, 0, keepdims=False)
        block_queries = lax.dynamic_slice_in_dim(seq_queries, offset, QBLOCK, 0)
        block_segments = lax.dynamic_slice_in_dim(seq_segments, offset, QBLOCK, 0)
        scores = (
            jnp.einsum("qhd,khd->hqk", block_queries, seq_keys, preferred_element_type=jnp.float32)
            * score_scale
        )
        same_doc = block_segments[:, None] == seq_segments[None, :]
        scores = jnp.where(same_doc[None], scores, NEG_FILL)
        highest = jnp.max(scores, axis=2, keepdims=True)
        weights = jnp.exp(scores - highest)
        totals = jnp.sum(weights, axis=2, keepdims=True)
        mixture = jnp.einsum(
            "hqk,khd->qhd",
            rounded(weights / totals),
            seq_values,
            preferred_element_type=jnp.float32,
        )
        return (mixture, (highest + jnp.log(totals))[:, :, 0])

    mixture, log_total = lax.map(attend_one_block, jnp.arange(SEQS * blocks))
    return (mixture.reshape(queries.shape), log_total)


def attend_backward(queries, key_rows, value_rows, segments, log_total, grad_mixed):
    score_scale = HEAD_DIM ** (-0.5)
    blocks = LEN // QBLOCK
    heads_here = queries.shape[1] // HEAD_DIM
    query_heads = split_heads(queries)
    key_heads = split_heads(key_rows)
    value_heads = split_heads(value_rows)
    grad_heads = split_heads(grad_mixed)
    lse_rows = log_total.reshape(SEQS, blocks, heads_here, QBLOCK)

    def one_sequence(sequence):
        seq_queries = lax.dynamic_index_in_dim(query_heads, sequence, 0, keepdims=False)
        seq_keys = lax.dynamic_index_in_dim(key_heads, sequence, 0, keepdims=False)
        seq_values = lax.dynamic_index_in_dim(value_heads, sequence, 0, keepdims=False)
        seq_grads = lax.dynamic_index_in_dim(grad_heads, sequence, 0, keepdims=False)
        seq_segments = lax.dynamic_index_in_dim(segments, sequence, 0, keepdims=False)
        seq_lse = lax.dynamic_index_in_dim(lse_rows, sequence, 0, keepdims=False)

        def one_one_block(carry, block_index):
            offset = block_index * QBLOCK
            block_queries = lax.dynamic_slice_in_dim(seq_queries, offset, QBLOCK, 0)
            block_grads = lax.dynamic_slice_in_dim(seq_grads, offset, QBLOCK, 0)
            block_segments = lax.dynamic_slice_in_dim(seq_segments, offset, QBLOCK, 0)
            block_lse = lax.dynamic_index_in_dim(seq_lse, block_index, 0, keepdims=False)
            scores = (
                jnp.einsum(
                    "qhd,khd->hqk", block_queries, seq_keys, preferred_element_type=jnp.float32
                )
                * score_scale
            )
            same_doc = block_segments[:, None] == seq_segments[None, :]
            scores = jnp.where(same_doc[None], scores, NEG_FILL)
            probs = jnp.exp(scores - block_lse[:, :, None])
            grad_probs = jnp.einsum(
                "qhd,khd->hqk", block_grads, seq_values, preferred_element_type=jnp.float32
            )
            grad_scores = rounded(
                probs * (grad_probs - jnp.sum(probs * grad_probs, axis=2, keepdims=True))
            )
            grad_query = (
                jnp.einsum(
                    "hqk,khd->qhd", grad_scores, seq_keys, preferred_element_type=jnp.float32
                )
                * score_scale
            )
            key_sum = (
                carry[0]
                + jnp.einsum(
                    "hqk,qhd->khd", grad_scores, block_queries, preferred_element_type=jnp.float32
                )
                * score_scale
            )
            value_sum = carry[1] + jnp.einsum(
                "hqk,qhd->khd", rounded(probs), block_grads, preferred_element_type=jnp.float32
            )
            return ((key_sum, value_sum), rounded(grad_query))

        zeros_init = jnp.zeros((LEN, heads_here, HEAD_DIM), jnp.float32)
        (key_sum, value_sum), grad_query = lax.scan(
            one_one_block, (zeros_init, zeros_init), jnp.arange(blocks)
        )
        return (grad_query.reshape(LEN, heads_here, HEAD_DIM), rounded(key_sum), rounded(value_sum))

    grad_query, grad_key, grad_value = lax.map(one_sequence, jnp.arange(SEQS))
    return (
        grad_query.reshape(queries.shape),
        grad_key.reshape(queries.shape),
        grad_value.reshape(queries.shape),
    )


def layer_forward(hidden, params, gathered, segments):
    query_w, key_w, value_w, inner_w, proj_w, outer_w, proj_cols = gathered
    whole_in = spread_features(hidden)
    queries = rounded(matmul(whole_in, query_w) + params[0])
    key_rows = rounded(matmul(whole_in, key_w))
    value_rows = rounded(matmul(whole_in, value_w) + params[1])
    mixture, log_total = attend_forward(queries, key_rows, value_rows, segments)
    attended = rounded(mixture)
    attn_branch = sum_partials(matmul(attended, proj_w)) + params[2]
    first_norm, normed_one, inverse_one = norm_forward(hidden + attn_branch, params[3], params[4])
    whole_mid = spread_features(first_norm)
    inner_act = matmul(whole_mid, inner_w) + params[5]
    active = rounded(exact_gelu(inner_act))
    ffn_branch = sum_partials(matmul(active, outer_w)) + params[6]
    output, normed_two, inverse_two = norm_forward(first_norm + ffn_branch, params[7], params[8])
    kept_values = (
        whole_in,
        queries,
        key_rows,
        value_rows,
        log_total,
        attended,
        normed_one,
        inverse_one,
        whole_mid,
        inner_act,
        active,
        normed_two,
        inverse_two,
    )
    return (output, kept_values)


def layer_backward(grad_output, kept_values, gathered, params, segments):
    (
        whole_in,
        queries,
        key_rows,
        value_rows,
        log_total,
        attended,
        normed_one,
        inverse_one,
        whole_mid,
        inner_act,
        active,
        normed_two,
        inverse_two,
    ) = kept_values
    query_w, key_w, value_w, inner_w, proj_w, outer_w, proj_cols = gathered
    grad_second, ffn_gain_sum, ffn_shift_sum = norm_backward(
        grad_output, normed_two, inverse_two, params[7]
    )
    ffn_low = rounded(grad_second)
    whole_second = spread_grads(ffn_low)
    outer_term = over_tokens(active, whole_second)
    active_grad = against(whole_second, outer_w)
    unused, pullback = jax.vjp(exact_gelu, inner_act)
    inner_low = rounded(pullback(active_grad)[0])
    inner_term = over_tokens(whole_mid, inner_low)
    grad_first = grad_second + sum_grad_partials(against(inner_low, inner_w))
    grad_attn, attn_gain_sum, attn_shift_sum = norm_backward(
        grad_first, normed_one, inverse_one, params[3]
    )
    attn_low = rounded(grad_attn)
    whole_attn = spread_grads(attn_low)
    proj_term = over_tokens(attended, whole_attn)
    mixed_grad = rounded(against(whole_attn, proj_w))
    query_low, key_low, value_low = attend_backward(
        queries, key_rows, value_rows, segments, log_total, mixed_grad
    )
    input_terms = (
        against(query_low, query_w) + against(key_low, key_w) + against(value_low, value_w)
    )
    grad_input = grad_attn + sum_grad_partials(input_terms)
    row_terms = (
        over_tokens(whole_in, query_low),
        over_tokens(whole_in, key_low),
        over_tokens(whole_in, value_low),
        inner_term,
    )
    col_terms = (proj_term, outer_term)
    small_terms = (
        token_sum(query_low),
        token_sum(value_low),
        token_sum(attn_low),
        attn_gain_sum,
        attn_shift_sum,
        token_sum(inner_low),
        token_sum(ffn_low),
        ffn_gain_sum,
        ffn_shift_sum,
    )
    return (grad_input, row_terms, col_terms, small_terms)


def general_device(
    hidden_in,
    query_weight,
    key_weight,
    value_weight,
    query_bias,
    value_bias,
    proj_weight,
    proj_bias,
    attn_gain,
    attn_shift,
    inner_weight,
    inner_bias,
    outer_weight,
    outer_bias,
    ffn_gain,
    ffn_shift,
    segment_ids,
    grad_out,
):
    shards = (query_weight, key_weight, value_weight, inner_weight, proj_weight, outer_weight)
    params = (
        query_bias,
        value_bias,
        proj_bias,
        attn_gain,
        attn_shift,
        inner_bias,
        outer_bias,
        ffn_gain,
        ffn_shift,
    )
    gathered = gather_weights(shards)
    start_in = hidden_in.astype(jnp.float32)
    middle, kept_one = layer_forward(start_in, params, gathered, segment_ids)
    final_out, kept_two = layer_forward(middle, params, gathered, segment_ids)
    kept = (kept_one, kept_two)
    grad_flow = grad_out.astype(jnp.float32)
    row_parts = []
    col_parts = []
    small_parts = []
    for layer_index in (1, 0):
        grad_flow, row_terms, col_terms, small_terms = layer_backward(
            grad_flow, kept[layer_index], gathered, params, segment_ids
        )
        row_parts.append(row_terms)
        col_parts.append(col_terms)
        small_parts.append(small_terms)
    row_sum = jax.tree.map(jnp.add, tuple(row_parts[0]), tuple(row_parts[1]))
    col_sum = jax.tree.map(jnp.add, tuple(col_parts[0]), tuple(col_parts[1]))
    small_sum = jax.tree.map(jnp.add, small_parts[0], small_parts[1])
    row_sum = (
        lax.psum_scatter(
            row_sum[0].astype(jnp.bfloat16), "row", scatter_dimension=0, tiled=True
        ).astype(jnp.float32),
        lax.psum_scatter(
            row_sum[1].astype(jnp.bfloat16), "row", scatter_dimension=0, tiled=True
        ).astype(jnp.float32),
        lax.psum_scatter(
            row_sum[2].astype(jnp.bfloat16), "row", scatter_dimension=0, tiled=True
        ).astype(jnp.float32),
        lax.psum_scatter(
            row_sum[3].astype(jnp.bfloat16), "row", scatter_dimension=0, tiled=True
        ).astype(jnp.float32),
    )
    col_sum = (
        lax.psum_scatter(
            col_sum[0].astype(jnp.bfloat16), "row", scatter_dimension=1, tiled=True
        ).astype(jnp.float32),
        lax.psum_scatter(
            col_sum[1].astype(jnp.bfloat16), "row", scatter_dimension=1, tiled=True
        ).astype(jnp.float32),
    )
    small_sum = lax.psum(
        (
            small_sum[0],
            small_sum[1],
            small_sum[2],
            small_sum[3],
            small_sum[4],
            small_sum[5],
            small_sum[6],
            small_sum[7],
            small_sum[8],
        ),
        "row",
    )
    return (
        final_out,
        grad_flow,
        row_sum[0],
        row_sum[1],
        row_sum[2],
        small_sum[0],
        small_sum[1],
        col_sum[0],
        small_sum[2],
        small_sum[3],
        small_sum[4],
        row_sum[3],
        small_sum[5],
        col_sum[1],
        small_sum[6],
        small_sum[7],
        small_sum[8],
    )


ANY = pl.BlockSpec(memory_space=pl.ANY)
VMEM = pl.BlockSpec(memory_space=pltpu.VMEM)
MESH = pl.DeviceIdType.MESH
DMA = pltpu.SemaphoreType.DMA
BF16 = jnp.bfloat16
F32 = jnp.float32


def place():
    row = lax.axis_index("row")
    depth = lax.axis_index("col")
    core = row % 2
    chip = row // 2
    x = chip % 2
    y = chip // 2
    return row, depth, core, chip, x, y


def remote(src, dst, send_sem, recv_sem, row, depth):
    return pltpu.make_async_remote_copy(
        src_ref=src,
        dst_ref=dst,
        send_sem=send_sem,
        recv_sem=recv_sem,
        device_id={"row": row, "col": depth},
        device_id_type=MESH,
    )


def slot_of(block, x, y):
    dx = (block % 2 - x) * (block % 2 - x)
    dy = (block // 2 - y) * (block // 2 - y)
    return 3 * dy + dx - 2 * dx * dy


def span(start, size):
    if isinstance(start, int):
        return pl.ds(start, size)
    return pl.ds(pl.multiple_of(start, 128), size)


def greet(row, depth, core, chip, x, y):
    barrier = pltpu.get_barrier_semaphore()
    mate = chip * 2 + (1 - core)
    friends = [(mate, depth)]
    for step in (1, 2, 3):
        friends.append((row, (depth + step) % 4))
        friends.append((mate, (depth + step) % 4))
    friends.append(((y * 2 + 1 - x) * 2 + core, depth))
    friends.append((((1 - y) * 2 + x) * 2 + core, depth))
    for r, d in friends:
        pl.semaphore_signal(
            barrier, inc=1, device_id={"row": r, "col": d}, device_id_type=MESH
        )
    pl.semaphore_wait(barrier, len(friends))


PIECES = 8
GROUPS = ((3,), (0,), (1,), (2,), (4,), (5,), (6,), (7,))


def gather_kernel(
    q_ref, k_ref, v_ref, proj_ref, inner_ref, outer_ref, small_ref, x_ref, g_ref,
    wqkv, wproj, winner, wouter, smalls, u_out, g_out,
    swap_s, swap_r, local_s, up_s, up_r, down_s, down_r, sm_s, sm_r,
    p1_s, p1_r, p2_s, p2_r, t_s, t_r, t_l, pair_s, pair_r,
):
    row, depth, core, chip, x, y = place()
    mate = chip * 2 + (1 - core)
    x_row = (y * 2 + 1 - x) * 2 + core
    y_row = ((1 - y) * 2 + x) * 2 + core
    greet(row, depth, core, chip, x, y)

    def swap_src(piece, half):
        if piece < 3:
            return (q_ref, k_ref, v_ref)[piece].at[:, span(half * 128, 128)]
        if piece == 3:
            return proj_ref.at[span(half * 128, 128), :]
        if piece < 6:
            return inner_ref.at[:, span(half * 512 + (piece - 4) * 256, 256)]
        return outer_ref.at[span(half * 512 + (piece - 6) * 256, 256), :]

    def cell(piece, start, size, origin):
        if piece < 3:
            return wqkv.at[span(start, size), span(piece * 512 + origin * 128, 128)]
        if piece == 3:
            return wproj.at[span(origin * 128, 128), span(start, size)]
        if piece < 6:
            return winner.at[
                span(start, size), span((piece - 4) * 1024 + origin * 256, 256)
            ]
        return wouter.at[span((piece - 6) * 1024 + origin * 256, 256), span(start, size)]

    def region(group, part, block):
        piece = GROUPS[group][0]
        if piece < 3:
            return wqkv.at[span(block * 256 + part * 128, 128), pl.ds(piece * 512, 512)]
        if piece == 3:
            return wproj.at[pl.ds(part * 256, 256), span(block * 256, 256)]
        if piece < 6:
            return winner.at[
                span(block * 256 + part * 128, 128), pl.ds((piece - 4) * 1024, 1024)
            ]
        return wouter.at[
            pl.ds((piece - 6) * 1024 + part * 512, 512), span(block * 256, 256)
        ]

    swaps, locals_ = [], []
    for piece in range(PIECES):
        target = cell(piece, core * 128, 128, depth)
        cp = remote(
            swap_src(piece, 1 - core), target, swap_s.at[piece], swap_r.at[piece], mate, depth
        )
        cp.start()
        swaps.append(cp)
        lc = pltpu.make_async_copy(swap_src(piece, core), target, local_s.at[piece])
        lc.start()
        locals_.append(lc)
    small_local = pltpu.make_async_copy(small_ref, smalls.at[depth], local_s.at[PIECES])
    small_local.start()

    def travel(piece, step, up):
        origin = depth - step if up else depth + step
        ref = cell(piece, 0, 256, origin)
        send, recv = (up_s, up_r) if up else (down_s, down_r)
        return remote(
            ref, ref, send.at[piece, step], recv.at[piece, step], row,
            depth + 1 if up else depth - 1,
        )

    def depth_step(group, step):
        for piece in GROUPS[group]:
            if step == 0:
                swaps[piece].wait_recv()
                locals_[piece].wait()
            for up in (True, False):
                inside = depth - step >= 0 if up else depth + step <= 3
                ready = inside & (depth < 3 if up else depth > 0)
                if step > 0:

                    @pl.when(inside)
                    def _():
                        origin = depth - step if up else depth + step
                        ref = cell(piece, 0, 256, origin)
                        recv = up_r if up else down_r
                        remote(
                            ref, ref, up_s.at[piece, step - 1], recv.at[piece, step - 1],
                            mate, depth,
                        ).wait_recv()

                if step < 3:

                    @pl.when(ready)
                    def _():
                        travel(piece, step, up).start()

    def depth_done():
        for piece in range(PIECES):
            for step in (0, 1, 2):
                for up in (True, False):
                    inside = depth - step >= 0 if up else depth + step <= 3

                    @pl.when(inside & (depth < 3 if up else depth > 0))
                    def _():
                        travel(piece, step, up).wait_send()

    def token_copies(index, src, dst):
        for j in range(4):
            to_core, to_depth = j % 2, core * 2 + j // 2
            mine = (to_core == core) & (to_depth == depth)
            source = src.at[pl.ds(j * 512, 512), :]
            target = dst.at[pl.ds(0, 512), span(slot_of(depth, x, y) * 256, 256)]

            @pl.when(mine)
            def _():
                pltpu.make_async_copy(source, target, t_l.at[index]).start()

            @pl.when(jnp.logical_not(mine))
            def _():
                remote(
                    source, target, t_s.at[index, j], t_r.at[index, depth],
                    chip * 2 + to_core, to_depth,
                ).start()

    def token_waits(index, src, dst):
        from_core = depth // 2
        for s in range(4):
            mine = (from_core == core) & (s == depth)
            target = dst.at[pl.ds(0, 512), span(slot_of(s, x, y) * 256, 256)]
            source = src.at[pl.ds(0, 512), :]

            @pl.when(mine)
            def _():
                pltpu.make_async_copy(source, target, t_l.at[index]).wait()

            @pl.when(jnp.logical_not(mine))
            def _():
                remote(
                    source, target, t_s.at[index, 0], t_r.at[index, s], mate, depth
                ).wait_recv()
        for j in range(4):
            to_core, to_depth = j % 2, core * 2 + j // 2
            mine = (to_core == core) & (to_depth == depth)

            @pl.when(jnp.logical_not(mine))
            def _():
                remote(
                    src.at[pl.ds(j * 512, 512), :], dst.at[pl.ds(0, 512), pl.ds(0, 256)],
                    t_s.at[index, j], t_r.at[index, 0], mate, depth,
                ).wait_send()

    first, second = {}, {}

    def start_first(group):
        for part, target, to in ((0, x_row, 1), (1, y_row, 3)):
            cp = remote(
                region(group, part, 0), region(group, part, to),
                p1_s.at[group, part], p1_r.at[group, part], target, depth,
            )
            cp.start()
            first[group, part] = cp

    def start_second(group):
        for part, target, moves in (
            (0, y_row, ((0, 3), (1, 2))), (1, x_row, ((0, 1), (3, 2))),
        ):
            first[group, part].wait_recv()
            for i, (origin, to) in enumerate(moves):
                cp = remote(
                    region(group, part, origin), region(group, part, to),
                    p2_s.at[group, part, i], p2_r.at[group, part, i], target, depth,
                )
                cp.start()
                second[group, part, i] = cp

    count = len(GROUPS)
    small_copies = []
    for tick in range(count + 4):
        for step in (0, 1, 2, 3):
            group = tick - step
            if 0 <= group < count:
                depth_step(group, step)
                if step == 3:
                    start_first(group)
        if 0 <= tick - 4 < count:
            start_second(tick - 4)
        if tick == TOKEN_TICK:
            token_copies(0, x_ref, u_out)
        if tick == count - 1:
            for k in (1, 2, 3):
                cp = remote(
                    small_ref, smalls.at[depth], sm_s.at[k - 1], sm_r.at[k - 1],
                    row, (depth + k) % 4,
                )
                cp.start()
                small_copies.append(cp)
            token_copies(1, g_ref, g_out)
    token_waits(0, x_ref, u_out)
    pair = remote(
        u_out.at[pl.ds(0, 512), :], u_out.at[pl.ds(512, 512), :], pair_s, pair_r, mate, depth
    )
    pair.start()
    token_waits(1, g_ref, g_out)
    pair.wait()
    for cp in small_copies:
        cp.wait()
    small_local.wait()
    depth_done()
    for cp in second.values():
        cp.wait()
    for cp in first.values():
        cp.wait_send()
    for cp in swaps:
        cp.wait_send()


TOKEN_TICK = 9


def gather_all(q, k, v, proj, inner, outer, small, x_rolled, g_rolled):
    sd = jax.ShapeDtypeStruct
    n = len(GROUPS)
    return pl.pallas_call(
        gather_kernel,
        out_shape=(
            sd((1024, 1536), BF16),
            sd((512, 1024), BF16),
            sd((1024, 2048), BF16),
            sd((2048, 1024), BF16),
            sd((4,) + small.shape, F32),
            sd((1024, 1024), BF16),
            sd((512, 1024), BF16),
        ),
        in_specs=[VMEM] * 7 + [ANY] * 2,
        out_specs=[ANY] * 7,
        scratch_shapes=[
            DMA((PIECES,)), DMA((PIECES,)), DMA((PIECES + 1,)),
            DMA((PIECES, 3)), DMA((PIECES, 3)), DMA((PIECES, 3)), DMA((PIECES, 3)),
            DMA((3,)), DMA((3,)),
            DMA((n, 2)), DMA((n, 2)), DMA((n, 2, 2)), DMA((n, 2, 2)),
            DMA((2, 4)), DMA((2, 4)), DMA((2,)), DMA, DMA,
        ],
        compiler_params=pltpu.CompilerParams(collective_id=1, has_side_effects=True),
    )(q, k, v, proj, inner, outer, small, x_rolled, g_rolled)


SHAPES = ((256, 256), (128, 512), (128, 512), (128, 512))
UNITS = ((128, 256), (256, 128), (256, 128), (256, 128))
FULLS = ((512, 256), (256, 512), (256, 512), (256, 512))
OUTS = ((256, 128), (128, 256), (128, 256), (128, 256), (128, 1024), (1024, 128))
HALVES = ((128, 128), (128, 128), (128, 128), (128, 128), (128, 512), (512, 128))
BY_COLS = (True, False, False, False)
INNER, OUTER = 4, 5


def add_rows(dst, terms):
    rows = dst.shape[0]
    step = 32

    def body(i, carry):
        sl = pl.ds(pl.multiple_of(i * step, step), step)
        total = terms[0][sl, :].astype(F32)
        for term in terms[1:]:
            total = total + term[sl, :].astype(F32)
        dst[sl, :] = total.astype(dst.dtype)
        return carry

    lax.fori_loop(0, rows // step, body, 0)


def scatter_kernel(*refs):
    grads = refs[0:4]
    inner_ref, outer_ref, small_ref, gi_ref = refs[4:8]
    outs = refs[8:14]
    small_out, gi_out = refs[14:16]
    rest = list(refs[16:])
    own = [[rest.pop(0) for _ in range(2)] for _ in range(4)]
    got1 = [[rest.pop(0) for _ in range(2)] for _ in range(4)]
    got2 = [[rest.pop(0) for _ in range(2)] for _ in range(4)]
    full = [rest.pop(0) for _ in range(4)]
    zgot = [rest.pop(0) for _ in range(4)]
    fin = [rest.pop(0) for _ in range(4)]
    cgot = [rest.pop(0) for _ in range(6)]
    sb = rest.pop(0)
    sg = rest.pop(0)
    (o_s, p1_s, p1_r, p2_s, p2_r, z_s, z_r, c_s, c_r, sm_s, sm_r, t_s, t_r, t_l) = rest

    row, depth, core, chip, x, y = place()
    mate = chip * 2 + (1 - core)
    x_row = (y * 2 + 1 - x) * 2 + core
    y_row = ((1 - y) * 2 + x) * 2 + core
    greet(row, depth, core, chip, x, y)

    def region(group, part, block):
        rows = SHAPES[group][0]
        if BY_COLS[group]:
            return grads[group].at[pl.ds(part * rows, rows), span(block * 256, 256)]
        return grads[group].at[span(block * 256 + part * 128, 128), :]

    def unit(group, z):
        if BY_COLS[group]:
            return full[group].at[span(z * UNITS[group][0], UNITS[group][0]), :]
        return full[group].at[:, span(z * UNITS[group][1], UNITS[group][1])]

    def side(group, half):
        if group == OUTER:
            return outer_ref.at[:, span(half * 128, 128)]
        if group == INNER:
            return inner_ref.at[span(half * 128, 128), :]
        if BY_COLS[group]:
            return fin[group].at[:, span(half * 128, 128)]
        return fin[group].at[span(half * 128, 128), :]

    def out_side(group, half):
        if group == OUTER:
            return outs[5].at[span(half * 512, 512), :]
        if group == INNER:
            return outs[4].at[:, span(half * 512, 512)]
        size = HALVES[group]
        if BY_COLS[group]:
            return outs[group].at[span(half * size[0], size[0]), :]
        return outs[group].at[:, span(half * size[1], size[1])]

    copies = {}

    def start_first(group):
        for part in (0, 1):
            target = y_row if part == 0 else x_row
            for i in (0, 1):
                kept = ((0, 1), (0, 3))[part][i]
                sent = ((3, 2), (1, 2))[part][i]
                lc = pltpu.make_async_copy(
                    region(group, part, kept), own[group][part].at[i], o_s.at[group, part, i]
                )
                lc.start()
                cp = remote(
                    region(group, part, sent), got1[group][part].at[i],
                    p1_s.at[group, part, i], p1_r.at[group, part, i], target, depth,
                )
                cp.start()
                copies["o", group, part, i] = lc
                copies["p1", group, part, i] = cp

    def start_second(group):
        for part in (0, 1):
            target = x_row if part == 0 else y_row
            for i in (0, 1):
                copies["o", group, part, i].wait()
                copies["p1", group, part, i].wait_recv()
            other = own[group][part].at[1]
            add_rows(other, (other, got1[group][part].at[1]))
            cp = remote(
                other, got2[group][part], p2_s.at[group, part], p2_r.at[group, part], target, depth
            )
            cp.start()
            copies["p2", group, part] = cp

    def send_depth(group):
        for k in (1, 2, 3):
            cp = remote(
                unit(group, (depth + k) % 4), zgot[group].at[k - 1],
                z_s.at[group, k - 1], z_r.at[group, k - 1], row, (depth + k) % 4,
            )
            cp.start()
            copies["z", group, k] = cp

    def start_depth(group):
        rows = SHAPES[group][0]
        for part in (0, 1):
            copies["p2", group, part].wait_recv()
            add_rows(
                full[group].at[pl.ds(part * rows, rows), :],
                (own[group][part].at[0], got1[group][part].at[0], got2[group][part]),
            )
        send_depth(group)

    def send_core(group):
        cp = remote(
            side(group, 1 - core), cgot[group], c_s.at[group], c_r.at[group], mate, depth
        )
        cp.start()
        copies["c", group] = cp

    def start_core(group):
        for k in (1, 2, 3):
            copies["z", group, k].wait_recv()
        add_rows(
            fin[group],
            (unit(group, depth), zgot[group].at[0], zgot[group].at[1], zgot[group].at[2]),
        )
        send_core(group)

    def finish(group):
        add_rows(out_side(group, core), (side(group, core),))
        copies["c", group].wait_recv()
        add_rows(out_side(group, 1 - core), (cgot[group],))

    def token_copies(index, src, dst):
        j = (depth % 2) * 2 + core
        to_core = depth // 2
        for z in range(4):
            mine = (to_core == core) & (z == depth)
            source = src.at[:, span(slot_of(z, x, y) * 256, 256)]
            target = dst.at[span(j * 512, 512), :]

            @pl.when(mine)
            def _():
                pltpu.make_async_copy(source, target, t_l.at[index]).start()

            @pl.when(jnp.logical_not(mine))
            def _():
                remote(
                    source, target, t_s.at[index, z], t_r.at[index, j], chip * 2 + to_core, z
                ).start()

    def token_waits(index, src, dst):
        to_core = depth // 2
        for j in range(4):
            from_core, from_depth = j % 2, core * 2 + j // 2
            mine = (from_core == core) & (from_depth == depth)
            target = dst.at[pl.ds(j * 512, 512), :]
            source = src.at[:, pl.ds(0, 256)]

            @pl.when(mine)
            def _():
                pltpu.make_async_copy(source, target, t_l.at[index]).wait()

            @pl.when(jnp.logical_not(mine))
            def _():
                remote(
                    source, target, t_s.at[index, 0], t_r.at[index, j], mate, depth
                ).wait_recv()
        for z in range(4):
            mine = (to_core == core) & (z == depth)

            @pl.when(jnp.logical_not(mine))
            def _():
                remote(
                    src.at[:, pl.ds(z * 256, 256)], dst.at[pl.ds(0, 512), :],
                    t_s.at[index, z], t_r.at[index, 0], mate, depth,
                ).wait_send()

    def small_send(step, slot, target_row, target_depth):
        cp = remote(
            sb.at[step], sg.at[slot], sm_s.at[slot], sm_r.at[slot], target_row, target_depth
        )
        cp.start()
        copies["s", slot] = cp

    def small_add(step, slot):
        copies["s", slot].wait_recv()
        sb[step + 1] = sb[step] + sg[slot]

    sb[0] = small_ref[...]
    for group in range(2):
        start_first(group)
    small_send(0, 0, mate, depth)
    send_core(OUTER)
    send_core(INNER)
    token_copies(0, gi_ref, gi_out)
    small_add(0, 0)
    small_send(1, 1, x_row, depth)
    finish(OUTER)
    finish(INNER)
    for group in range(4):
        start_second(group)
        if group + 2 < 4:
            start_first(group + 2)
        if group == 0:
            small_add(1, 1)
            small_send(2, 2, y_row, depth)
        if group > 0:
            start_depth(group - 1)
    small_add(2, 2)
    for k in (1, 2, 3):
        small_send(3, 2 + k, row, (depth + k) % 4)
    start_depth(3)
    for group in (0, 1, 2):
        start_core(group)
    for k in (1, 2, 3):
        copies["s", 2 + k].wait_recv()
    small_out[...] = ((sb[3] + sg[3]) + sg[4]) + sg[5]
    for group in (0, 1, 2):
        finish(group)
    start_core(3)
    token_waits(0, gi_ref, gi_out)
    finish(3)
    for key, cp in copies.items():
        if key[0] != "o":
            cp.wait_send()


def scatter_all(proj, q, k, v, inner, outer, small, gi):
    sd = jax.ShapeDtypeStruct
    scratch = []
    for size in SHAPES:
        scratch += [pltpu.VMEM((2,) + size, BF16)] * 2
    for size in SHAPES:
        scratch += [pltpu.VMEM((2,) + size, BF16)] * 2
    for size in SHAPES:
        scratch += [pltpu.VMEM(size, BF16)] * 2
    scratch += [pltpu.VMEM(size, BF16) for size in FULLS]
    scratch += [pltpu.VMEM((3,) + size, BF16) for size in UNITS]
    scratch += [pltpu.VMEM(size, BF16) for size in UNITS]
    scratch += [pltpu.VMEM(size, BF16) for size in HALVES]
    scratch += [pltpu.VMEM((4,) + small.shape, F32), pltpu.VMEM((6,) + small.shape, F32)]
    scratch += [
        DMA((4, 2, 2)), DMA((4, 2, 2)), DMA((4, 2, 2)), DMA((4, 2)), DMA((4, 2)),
        DMA((4, 3)), DMA((4, 3)), DMA((6,)), DMA((6,)), DMA((6,)), DMA((6,)),
        DMA((1, 4)), DMA((1, 4)), DMA((1,)),
    ]
    return pl.pallas_call(
        scatter_kernel,
        out_shape=tuple(sd(size, F32) for size in OUTS)
        + (sd(small.shape, F32), sd((2048, 256), BF16)),
        in_specs=[ANY] * 4 + [VMEM] * 3 + [ANY],
        out_specs=[VMEM] * 7 + [ANY],
        scratch_shapes=scratch,
        compiler_params=pltpu.CompilerParams(
            collective_id=2, has_side_effects=True, vmem_limit_bytes=48 * 1024 * 1024
        ),
    )(proj, q, k, v, inner, outer, small, gi)


def attend_kernel(flag_ref, q_ref, k_ref, v_ref, idq_ref, idk_ref, o_ref, lse_ref):
    rows = q_ref.shape[0]
    lane = lax.broadcasted_iota(jnp.int32, (1, 128), 1)
    low_half = lane < HEAD_DIM

    def compute(masked):
        keys = k_ref[...]
        values = v_ref[...]
        halves = (low_half, jnp.logical_not(low_half))
        sub = 256
        units = [(i, h) for i in range(rows // sub) for h in (0, 1)]

        def score(unit):
            i, h = unit
            scaled = q_ref[i * sub : (i + 1) * sub, :] * jnp.asarray(HEAD_DIM**-0.5, BF16)
            s = against(jnp.where(halves[h], scaled, jnp.zeros_like(scaled)), keys)
            if masked:
                s = jnp.where(idq_ref[i * sub : (i + 1) * sub, :] == idk_ref[...], s, NEG_FILL)
            return s

        def soft(s):
            top = jnp.max(s, axis=1, keepdims=True)
            weights = jnp.exp(s - top)
            return weights.astype(BF16), jnp.sum(weights, axis=1, keepdims=True), top

        skew = 1
        pending = [score(u) for u in units[:skew]]
        done = {}
        for n, unit in enumerate(units):
            if n + skew < len(units):
                pending.append(score(units[n + skew]))
            low, total, top = soft(pending.pop(0))
            mixed = matmul(low, values)
            done[unit] = (mixed / total, top + jnp.log(total))
            i, h = unit
            if h == 1:
                sl = slice(i * sub, (i + 1) * sub)
                a, b = done[i, 0], done[i, 1]
                o_ref[sl, :] = jnp.where(low_half, a[0], b[0]).astype(o_ref.dtype)
                lse_ref[sl, :] = jnp.where(low_half, a[1], b[1])

    @pl.when(flag_ref[0] == 1)
    def _():
        compute(False)

    @pl.when(flag_ref[0] != 1)
    def _():
        compute(True)


def attend(flag, qkv, id_col, id_row):
    tokens, width = qkv.shape[0], qkv.shape[1] // 3
    pairs = width // 128
    block = tokens
    return pl.pallas_call(
        attend_kernel,
        out_shape=(
            jax.ShapeDtypeStruct((tokens, width), BF16),
            jax.ShapeDtypeStruct((tokens, width), F32),
        ),
        grid_spec=pltpu.PrefetchScalarGridSpec(
            num_scalar_prefetch=1,
            grid=(width // 128, tokens // block),
            in_specs=[
                pl.BlockSpec((block, 128), lambda h, i, f: (i, h)),
                pl.BlockSpec((tokens, 128), lambda h, i, f: (0, h + pairs)),
                pl.BlockSpec((tokens, 128), lambda h, i, f: (0, h + 2 * pairs)),
                pl.BlockSpec((block, 1), lambda h, i, f: (i, 0)),
                pl.BlockSpec((1, tokens), lambda h, i, f: (0, 0)),
            ],
            out_specs=[
                pl.BlockSpec((block, 128), lambda h, i, f: (i, h)),
                pl.BlockSpec((block, 128), lambda h, i, f: (i, h)),
            ],
        ),
        compiler_params=pltpu.CompilerParams(
            dimension_semantics=("arbitrary", "arbitrary"), vmem_limit_bytes=48 * 1024 * 1024
        ),
        cost_estimate=pl.CostEstimate(
            flops=20_000_000_000, bytes_accessed=8_000_000, transcendentals=0
        ),
        name="attend",
    )(flag, qkv, qkv, qkv, id_col, id_row)


def attend_back_kernel(
    flag_ref, q_ref, k_ref, v_ref, do_ref, lse_ref, idk_ref, idq_ref,
    dq_ref, dk_ref, dv_ref,
):
    rows = q_ref.shape[0]
    scale = HEAD_DIM**-0.5
    lane = lax.broadcasted_iota(jnp.int32, (1, 128), 1)
    low_half = lane < HEAD_DIM

    def compute(masked):
        queries = q_ref[...]
        scaled = queries * jnp.asarray(scale, BF16)
        keys = k_ref[...]
        values = v_ref[...]
        grads = do_ref[...]
        lse_t = lse_ref[...].T
        q_t, k_t, do_t = queries.T, keys.T, grads.T
        dqs, dks, dvs = [], [], []
        for head in (0, 1):
            here = low_half if head == 0 else jnp.logical_not(low_half)
            part = slice(head * HEAD_DIM, (head + 1) * HEAD_DIM)
            zero = jnp.zeros_like(keys)
            scores = against(jnp.where(here, keys, zero), scaled)
            if masked:
                scores = jnp.where(idk_ref[...] == idq_ref[...], scores, NEG_FILL)
            log_row = lse_t[head * HEAD_DIM : head * HEAD_DIM + 1, :]
            probs = jnp.exp(scores - log_row)
            grad_probs = against(jnp.where(here, values, zero), grads)
            moved = probs * grad_probs
            delta = jnp.sum(moved, axis=0, keepdims=True)
            grad_scores = (moved - probs * delta).astype(BF16)
            low = probs.astype(BF16)
            dvs.append(against(do_t[part], low))
            dks.append(matmul(grad_scores, queries))
            dqs.append(matmul(k_t[part], grad_scores))
        dv_ref[...] = jnp.concatenate(dvs, axis=0).T.astype(BF16)
        dk_ref[...] = (jnp.where(low_half, dks[0], dks[1]) * scale).astype(BF16)
        dq_ref[...] = (jnp.concatenate(dqs, axis=0) * scale).T.astype(BF16)

    @pl.when(flag_ref[0] == 1)
    def _():
        compute(False)

    @pl.when(flag_ref[0] != 1)
    def _():
        compute(True)


def attend_back(flag, qkv, do, lse, id_col, id_row, first=0, count=4):
    tokens, width = qkv.shape[0], qkv.shape[1] // 3
    pairs = width // 128
    block = tokens
    shape = jax.ShapeDtypeStruct((tokens, count * 128), BF16)
    rows = pl.BlockSpec((block, 128), lambda h, i, f: (i, h + first))
    return pl.pallas_call(
        attend_back_kernel,
        out_shape=(shape, shape, shape),
        grid_spec=pltpu.PrefetchScalarGridSpec(
            num_scalar_prefetch=1,
            grid=(count, tokens // block),
            in_specs=[
                rows,
                pl.BlockSpec((tokens, 128), lambda h, i, f: (0, h + first + pairs)),
                pl.BlockSpec((tokens, 128), lambda h, i, f: (0, h + first + 2 * pairs)),
                rows, rows,
                pl.BlockSpec((tokens, 1), lambda h, i, f: (0, 0)),
                pl.BlockSpec((1, block), lambda h, i, f: (0, i)),
            ],
            out_specs=[
                pl.BlockSpec((block, 128), lambda h, i, f: (i, h)),
                pl.BlockSpec((tokens, 128), lambda h, i, f: (0, h)),
                pl.BlockSpec((tokens, 128), lambda h, i, f: (0, h)),
            ],
        ),
        compiler_params=pltpu.CompilerParams(
            dimension_semantics=("arbitrary", "arbitrary"), vmem_limit_bytes=48 * 1024 * 1024
        ),
        cost_estimate=pl.CostEstimate(
            flops=10_000_000_000 * count, bytes_accessed=2_500_000 * count, transcendentals=0
        ),
        name="attend_back",
    )(flag, qkv, qkv, qkv, do, lse, id_col, id_row)


def gelu_pair(inner):
    size = jnp.abs(inner)
    bell = jnp.exp(inner * (inner * -0.5))
    t = 1.0 / (1.0 + (0.3275911 * 0.5**0.5) * size)
    poly = (0.5 * 1.061405429) * t - 0.5 * 1.453152027
    poly = poly * t + 0.5 * 1.421413741
    poly = poly * t - 0.5 * 0.284496736
    poly = poly * t + 0.5 * 0.254829592
    tail = (poly * t) * bell
    below = jnp.where(inner >= 0.0, 1.0 - tail, tail)
    return (inner * below).astype(BF16), (below + inner * (bell * 0.3989422804014327)).astype(BF16)


def ffn_in_kernel(x_ref, w_ref, b_ref, active_ref, slope_ref):
    rows, cols = active_ref.shape
    sub = 128
    skew = 1

    def open_unit(i):
        return matmul(x_ref[i * sub : (i + 1) * sub, :], w_ref[...]) + b_ref[...]

    count = rows // sub
    pending = [open_unit(i) for i in range(skew)]
    for i in range(count):
        if i + skew < count:
            pending.append(open_unit(i + skew))
        active, slope = gelu_pair(pending.pop(0))
        active_ref[i * sub : (i + 1) * sub, :] = active
        slope_ref[i * sub : (i + 1) * sub, :] = slope


def ffn_in(x, w, bias):
    tokens, depth = x.shape
    hidden = w.shape[1]
    rows, cols = 1024, 512
    shape = jax.ShapeDtypeStruct((tokens, hidden), BF16)
    out = pl.BlockSpec((rows, cols), lambda n, m: (m, n))
    return pl.pallas_call(
        ffn_in_kernel,
        out_shape=(shape, shape),
        grid=(hidden // cols, tokens // rows),
        in_specs=[
            pl.BlockSpec((rows, depth), lambda n, m: (m, 0)),
            pl.BlockSpec((depth, cols), lambda n, m: (0, n)),
            pl.BlockSpec((1, cols), lambda n, m: (0, n)),
        ],
        out_specs=[out, out],
        compiler_params=pltpu.CompilerParams(
            dimension_semantics=("arbitrary", "arbitrary"), vmem_limit_bytes=48 * 1024 * 1024
        ),
        cost_estimate=pl.CostEstimate(
            flops=14_000_000_000, bytes_accessed=14_000_000, transcendentals=0
        ),
        name="ffn_in",
    )(x, w, bias)


def exchange(values):
    pairs = [(r, r + 1 - 2 * (r % 2)) for r in range(8)]
    return lax.ppermute(values, "row", pairs)


def both(own):
    return jnp.concatenate([own, exchange(own)], axis=0)


def share_sum(left, weight, product, apart=False):
    mate_part, left_own = lax.optimization_barrier(
        (rounded(product(left[512:], weight)), left[:512])
    )
    own_part, other = product(left_own, weight), exchange(mate_part)
    if apart:
        own_part, other = lax.optimization_barrier((own_part, other))
    return own_part + other.astype(F32)


def norm_rows(summed, gain, shift):
    center = jnp.mean(summed, axis=1, keepdims=True)
    spread = jnp.mean(summed * summed, axis=1, keepdims=True) - center * center
    inverse = lax.rsqrt(spread + EPSILON)
    normed = (summed - center) * inverse
    return normed * gain + shift, normed, inverse


def norm_rows_back(grad_output, normed, inverse, gain):
    scaled = grad_output * gain
    mean_one = jnp.mean(scaled, axis=1, keepdims=True)
    mean_two = jnp.mean(scaled * normed, axis=1, keepdims=True)
    grad_input = inverse * (scaled - mean_one - normed * mean_two)
    return grad_input, token_sum(grad_output * normed), token_sum(grad_output)


def fast_forward(hidden, weights, vectors, ids, whole_in=None):
    wqkv, wproj, winner, wouter = weights
    flag, id_col, id_row = ids
    if whole_in is None:
        whole_in = both(rounded(hidden))
    qkv = rounded(matmul(whole_in, wqkv) + vectors["qkv"])
    attended, lse = attend(flag, qkv, id_col, id_row)
    branch = share_sum(attended, wproj, matmul, True) + vectors["proj"]
    first, normed_one, inverse_one = norm_rows(
        hidden + branch, vectors["attn_gain"], vectors["attn_shift"]
    )
    whole_mid = both(rounded(first))
    active, slope = ffn_in(whole_mid, winner, vectors["inner"])
    ffn = share_sum(active, wouter, matmul, True) + vectors["outer"]
    output, normed_two, inverse_two = norm_rows(
        first + ffn, vectors["ffn_gain"], vectors["ffn_shift"]
    )
    kept = (
        whole_in, qkv, lse, attended, normed_one, inverse_one,
        whole_mid, active, slope, normed_two, inverse_two,
    )
    return output, kept


def fast_backward(grad_output, kept, weights, vectors, ids, later=None, beside=None):
    (
        whole_in, qkv, lse, attended, normed_one, inverse_one,
        whole_mid, active, slope, normed_two, inverse_two,
    ) = kept
    wqkv, wproj, winner, wouter = weights
    flag, id_col, id_row = ids
    grad_second, ffn_gain_sum, ffn_shift_sum = norm_rows_back(
        grad_output, normed_two, inverse_two, vectors["ffn_gain"]
    )
    ffn_low = rounded(grad_second)
    whole_second = both(ffn_low)
    inner_low = rounded(against(whole_second, wouter) * slope.astype(F32))
    if later is None:
        outer_terms = rounded(over_tokens(active, whole_second))
    else:
        outer_terms = add_trees(outer_pieces(active, whole_second), outer_cuts(later[0]))
        outer_planes = [Plane(outer_terms, h, 1) for h in (0, 1)]
        outer_got = [p.step_one() for p in outer_planes]
    grad_first = grad_second + share_sum(inner_low, winner, against)
    inner_terms = rounded(add_later(over_tokens(whole_mid, inner_low), later, 1))
    if later is not None:
        inner_planes = [Plane(inner_cuts(inner_terms), h, 0) for h in (0, 1)]
        inner_got = [p.step_one() for p in inner_planes]
    grad_attn, attn_gain_sum, attn_shift_sum = norm_rows_back(
        grad_first, normed_one, inverse_one, vectors["attn_gain"]
    )
    attn_low = rounded(grad_attn)
    whole_attn = both(attn_low)
    mixed_grad = rounded(against(whole_attn, wproj))
    proj_term = over_tokens(attended, whole_attn)
    if later is None:
        grads = attend_back(flag, qkv, mixed_grad, lse, id_col, id_row)
        if beside is not None:
            beside, grads = lax.optimization_barrier((beside, grads))
        outer_terms, inner_terms = (outer_terms, inner_terms), beside
    else:
        early = attend_back(flag, qkv, mixed_grad, lse, id_col, id_row, 0, 2)
        outer_got, early = lax.optimization_barrier((outer_got, early))
        outer_hand = [p.to_hand(g) for p, g in zip(outer_planes, outer_got)]
        outer_hand, mixed_grad = lax.optimization_barrier((outer_hand, mixed_grad))
        outer_more = [p.step_two(v) for p, v in zip(outer_planes, outer_hand)]
        late = attend_back(flag, qkv, mixed_grad, lse, id_col, id_row, 2, 2)
        inner_got, late = lax.optimization_barrier((inner_got, late))
        inner_hand = [p.to_hand(g) for p, g in zip(inner_planes, inner_got)]
        inner_hand, outer_more, late = lax.optimization_barrier((inner_hand, outer_more, late))
        inner_more = [p.step_two(v) for p, v in zip(inner_planes, inner_hand)]
        outer_terms = fold_depth([p.close(m) for p, m in zip(outer_planes, outer_more)], 0)
        inner_terms = fold_depth([p.close(m) for p, m in zip(inner_planes, inner_more)], 1)
        grads = tuple(jnp.concatenate(pair, axis=1) for pair in zip(early, late))
    grad_qkv = jnp.concatenate(grads, axis=1)
    grad_input = grad_attn + share_sum(grad_qkv, wqkv, against)
    terms = (proj_term,) + tuple(
        over_tokens(whole_in, part) for part in grads
    )
    small = (
        token_sum(grads[0]), token_sum(grads[2]), token_sum(attn_low),
        attn_gain_sum, attn_shift_sum, token_sum(inner_low), token_sum(ffn_low),
        ffn_gain_sum, ffn_shift_sum,
    )
    return grad_input, terms, outer_terms, inner_terms, small


def flip_row(bit):
    return [(r, r + bit - 2 * bit * ((r // bit) % 2)) for r in range(8)]


CUTS = (((512, 1024), (256, 512), (0, 256)), ((256, 768), (768, 1024), (0, 256)))


def outer_pieces(active, relative):
    return [
        [over_tokens(active[:, h * 1024 : (h + 1) * 1024], relative[:, a:b]) for a, b in CUTS[h]]
        for h in (0, 1)
    ]


def add_trees(left, right):
    return jax.tree.map(lambda p, q: p + q.astype(F32), left, right)


def outer_cuts(whole):
    return [
        [whole[h * 1024 : (h + 1) * 1024, a:b] for a, b in CUTS[h]] for h in (0, 1)
    ]


def inner_cuts(whole):
    return [
        [whole[a:b, h * 1024 : (h + 1) * 1024] for a, b in CUTS[h]] for h in (0, 1)
    ]


def add_later(term, later, index):
    return term if later is None else term + later[index].astype(F32)


class Plane:
    def __init__(self, pieces, half, axis):
        sent, handed, own = pieces[half]
        self.sent = rounded(sent)
        self.handed, self.own = handed.astype(F32), own.astype(F32)
        self.half, self.axis = half, axis
        self.first, self.second = (4, 2) if half == 0 else (2, 4)

    def step_one(self):
        return lax.ppermute(self.sent, "row", flip_row(self.first))

    def to_hand(self, got):
        low, high = jnp.split(got, 2, axis=self.axis)
        self.got, handed = (high, low) if self.half == 0 else (low, high)
        return rounded(self.handed + handed.astype(F32))

    def step_two(self, handed):
        return lax.ppermute(handed, "row", flip_row(self.second))

    def close(self, more):
        return rounded(self.own + self.got.astype(F32) + more.astype(F32))


def fold_depth(halves, axis):
    depth = lax.axis_index("col")

    def unit(z):
        picked = [lax.dynamic_slice_in_dim(half, z * 256, 256, axis) for half in halves]
        return jnp.concatenate(picked, axis=axis)

    total = unit(depth).astype(F32)
    for k in (1, 2, 3):
        pairs = [(z, (z + k) % 4) for z in range(4)]
        total = total + lax.ppermute(unit((depth + k) % 4), "col", pairs).astype(F32)
    return rounded(total)


def spread_out(values):
    core = lax.axis_index("row") % 2
    depth = lax.axis_index("col")
    j = (depth % 2) * 2 + core
    x, y = place()[4:]
    parts = []
    for k in range(4):
        pairs = []
        for r in range(8):
            for z in range(4):
                block = ((z % 2) * 2 + r % 2 + k) % 4
                pairs.append((r * 4 + z, (r // 2 * 2 + z // 2) * 4 + block))
        piece = lax.dynamic_slice_in_dim(values, slot_of((j + k) % 4, x, y) * 256, 256, 1)
        parts.append(lax.ppermute(piece, ("row", "col"), pairs))
    return parts


def join_parts(parts, own_start):
    depth = lax.axis_index("col")
    cycle = jnp.concatenate(parts[::-1] * 2, axis=0)
    start = ((3 - depth) * 512 - own_start + 2048) % 2048
    return lax.dynamic_slice(cycle, (start, 0), (2048, 256)).astype(F32)


VECTORS = (
    ("q", 256), ("v", 256), ("proj", 256), ("attn_gain", 256), ("attn_shift", 256),
    ("inner", 1024), ("outer", 256), ("ffn_gain", 256), ("ffn_shift", 256),
)
SPLIT = ("q", "v", "inner")


def fast_device(
    hidden_in,
    query_weight,
    key_weight,
    value_weight,
    query_bias,
    value_bias,
    proj_weight,
    proj_bias,
    attn_gain,
    attn_shift,
    inner_weight,
    inner_bias,
    outer_weight,
    outer_bias,
    ffn_gain,
    ffn_shift,
    segment_ids,
    grad_out,
):
    core = lax.axis_index("row") % 2
    depth = lax.axis_index("col")
    own_ids = segment_ids[0]
    mate_ids = exchange(own_ids)

    def big_start(ids):
        found = ids[:1025] == ids[1023:]
        return jnp.sum(jnp.where(found, jnp.arange(1025, dtype=jnp.int32), 0))

    own_start = big_start(own_ids)
    ids = jnp.where(depth // 2 == core, own_ids, mate_ids)
    ids = lax.dynamic_slice(
        jnp.concatenate([ids, ids[:1024]]), (big_start(ids),), (2048,)
    ).reshape(2, 2, 512)
    ids = lax.dynamic_index_in_dim(ids, depth % 2, 0, keepdims=False)
    ids = jnp.where(core == 0, ids, ids[::-1]).reshape(1024)
    flag = (1 - depth % 2).reshape(1).astype(jnp.int32)
    ids = (flag, ids[:, None], ids[None, :])

    def turned(values):
        longer = jnp.concatenate([values, values[:1024]], axis=0)
        return lax.dynamic_slice(longer, (own_start, 0), (2048, 256))

    def turned_back(values):
        longer = jnp.concatenate([values[1024:], values], axis=0)
        return lax.dynamic_slice(longer, (1024 - own_start, 0), (2048, 256)).astype(F32)

    small = jnp.concatenate(
        [
            query_bias, value_bias, proj_bias, attn_gain, attn_shift,
            inner_bias, outer_bias, ffn_gain, ffn_shift,
        ]
    ).reshape(24, 128)
    wqkv, wproj, winner, wouter, smalls, start_low, grad_low = gather_all(
        query_weight, key_weight, value_weight, proj_weight, inner_weight, outer_weight,
        small, turned(hidden_in), turned(grad_out),
    )
    smalls = smalls.reshape(4, 3072)
    x, y = place()[4:]
    order = (y * 2 + x, y * 2 + 1 - x, (1 - y) * 2 + 1 - x, (1 - y) * 2 + x)
    placed = jnp.stack([lax.dynamic_index_in_dim(smalls, b, 0, keepdims=False) for b in order])
    weights = (wqkv, wproj, winner, wouter)
    vectors, offset = {}, 0
    for name, size in VECTORS:
        part = (smalls if name in SPLIT else placed)[:, offset : offset + size]
        offset += size
        if name in SPLIT:
            part = jnp.where(core == 0, part[:, : size // 2], part[:, size // 2 :])
        vectors[name] = part.reshape(1, -1)
    vectors["inner"] = (
        vectors["inner"].reshape(4, 2, 256).transpose(1, 0, 2).reshape(1, 2048)
    )
    vectors["qkv"] = jnp.concatenate(
        [vectors["q"], jnp.zeros_like(vectors["q"]), vectors["v"]], axis=1
    )

    middle, kept_one = fast_forward(
        start_low[:512].astype(F32), weights, vectors, ids, start_low
    )
    final_out, kept_two = fast_forward(middle, weights, vectors, ids)
    grad_flow = grad_low.astype(F32)
    parts = spread_out(rounded(final_out))
    grad_flow, terms_two, ffn_two, parts, small_two = fast_backward(
        grad_flow, kept_two, weights, vectors, ids, None, parts
    )
    hidden_out = join_parts(parts, own_start)
    grad_flow, terms_one, outer_full, inner_full, small_one = fast_backward(
        grad_flow, kept_one, weights, vectors, ids, ffn_two
    )
    terms = [rounded(a + b) for a, b in zip(terms_two, terms_one)]
    pieces = []
    for (name, size), a, b in zip(VECTORS, small_two, small_one):
        total = a + b
        if name not in SPLIT:
            blocks = total.reshape(4, 256)
            total = jnp.stack(
                [
                    lax.dynamic_index_in_dim(blocks, slot_of(n, x, y), 0, keepdims=False)
                    for n in range(4)
                ]
            )
        if name in SPLIT:
            half = total.reshape(4, 1, size // 2)
            if name == "inner":
                half = total.reshape(2, 4, 256).transpose(1, 0, 2).reshape(4, 1, 512)
            zero = jnp.zeros_like(half)
            total = jnp.where(
                core == 0,
                jnp.concatenate([half, zero], axis=1),
                jnp.concatenate([zero, half], axis=1),
            )
        pieces.append(total.reshape(-1))
    small_sum = jnp.concatenate(pieces).reshape(96, 128)
    results = scatter_all(*terms, inner_full, outer_full, small_sum, rounded(grad_flow))
    proj_g, q_g, k_g, v_g, inner_g, outer_g, small_all, grad_turned = results
    small_all = small_all.reshape(-1)
    sums, offset = {}, 0
    for name, size in VECTORS:
        sums[name] = lax.dynamic_slice(small_all, (offset + depth * size,), (size,))
        offset += 4 * size
    return (
        hidden_out,
        turned_back(grad_turned),
        q_g,
        k_g,
        v_g,
        sums["q"],
        sums["v"],
        proj_g,
        sums["proj"],
        sums["attn_gain"],
        sums["attn_shift"],
        inner_g,
        sums["inner"],
        outer_g,
        sums["outer"],
        sums["ffn_gain"],
        sums["ffn_shift"],
    )


def solution(mesh):
    in_specs = (
        P("row", "col"),
        P("row", "col"),
        P("row", "col"),
        P("row", "col"),
        P("col"),
        P("col"),
        P("col", "row"),
        P("col"),
        P("col"),
        P("col"),
        P("row", "col"),
        P("col"),
        P("col", "row"),
        P("col"),
        P("col"),
        P("col"),
        P("row", None),
        P("row", "col"),
    )
    out_specs = (
        P("row", "col"),
        P("row", "col"),
        P("row", "col"),
        P("row", "col"),
        P("row", "col"),
        P("col"),
        P("col"),
        P("col", "row"),
        P("col"),
        P("col"),
        P("col"),
        P("row", "col"),
        P("col"),
        P("col", "row"),
        P("col"),
        P("col"),
        P("col"),
    )
    same = dict(mesh.shape) == {"row": 8, "col": 4}
    return jax.shard_map(
        fast_device if same else general_device, mesh=mesh, in_specs=in_specs, out_specs=out_specs, check_vma=False
    )
```

```python
import functools

import jax
import jax.numpy as jnp
from jax import lax
from jax.experimental import pallas as pl
from jax.experimental.pallas import tpu as pltpu
from jax.sharding import PartitionSpec as P

NEG_FILL = -1e30
HEAD_DIM = 64
D = 1024
LEN = 2048
QBLOCK = 512
SEQS = 1


EPSILON = 1e-06


def rounded(values):
    return values.astype(jnp.bfloat16)


def matmul(left, right):
    return jnp.dot(left, right, preferred_element_type=jnp.float32)


def over_tokens(left, right):
    return lax.dot_general(
        left, right, (((0,), (0,)), ((), ())), preferred_element_type=jnp.float32
    )


def against(left, right):
    return lax.dot_general(
        left, right, (((1,), (1,)), ((), ())), preferred_element_type=jnp.float32
    )


def token_sum(values):
    return jnp.sum(values, axis=0, dtype=jnp.float32)


def exact_gelu(inputs):
    return jax.nn.gelu(inputs, approximate=False)


def gather_weights(shards):
    front_set = (
        lax.all_gather(shards[0], "row", axis=0, tiled=True),
        lax.all_gather(shards[1], "row", axis=0, tiled=True),
        lax.all_gather(shards[2], "row", axis=0, tiled=True),
        lax.all_gather(shards[3], "row", axis=0, tiled=True),
    )
    back_set = (
        lax.all_gather(shards[4], "row", axis=1, tiled=True),
        lax.all_gather(shards[5], "row", axis=1, tiled=True),
    )
    proj_cols = back_set[0]
    return (
        front_set[0],
        front_set[1],
        front_set[2],
        front_set[3],
        back_set[0],
        back_set[1],
        proj_cols,
    )


def spread_features(values):
    return lax.all_gather(rounded(values), "col", axis=1, tiled=True)


def sum_partials(partial_terms):
    return lax.psum_scatter(
        partial_terms.astype(jnp.bfloat16), "col", scatter_dimension=1, tiled=True
    ).astype(jnp.float32)


def spread_grads(values):
    return lax.all_gather(values, "col", axis=1, tiled=True)


def sum_grad_partials(partial_terms):
    return lax.psum_scatter(
        partial_terms.astype(jnp.bfloat16), "col", scatter_dimension=1, tiled=True
    ).astype(jnp.float32)


def norm_forward(summed, norm_gain, norm_shift):
    totals = lax.psum((jnp.sum(summed, axis=1), jnp.sum(summed * summed, axis=1)), "col")
    center = totals[0][:, None] / D
    spread = totals[1][:, None] / D - center * center
    inverse = lax.rsqrt(spread + EPSILON)
    normed = (summed - center) * inverse
    return (normed * norm_gain + norm_shift, normed, inverse)


def norm_backward(grad_output, normed, inverse, norm_gain):
    scaled = grad_output * norm_gain
    totals = lax.psum((jnp.sum(scaled, axis=1), jnp.sum(scaled * normed, axis=1)), "col")
    grad_input = inverse * (scaled - totals[0][:, None] / D - normed * (totals[1][:, None] / D))
    return (grad_input, jnp.sum(grad_output * normed, axis=0), jnp.sum(grad_output, axis=0))


def split_heads(values):
    return values.reshape(SEQS, LEN, values.shape[1] // HEAD_DIM, HEAD_DIM)


def attend_forward(queries, key_rows, value_rows, segments):
    score_scale = HEAD_DIM ** (-0.5)
    blocks = LEN // QBLOCK
    query_heads = split_heads(queries)
    key_heads = split_heads(key_rows)
    value_heads = split_heads(value_rows)

    def attend_one_block(block_index):
        sequence = block_index // blocks
        offset = block_index % blocks * QBLOCK
        seq_queries = lax.dynamic_index_in_dim(query_heads, sequence, 0, keepdims=False)
        seq_keys = lax.dynamic_index_in_dim(key_heads, sequence, 0, keepdims=False)
        seq_values = lax.dynamic_index_in_dim(value_heads, sequence, 0, keepdims=False)
        seq_segments = lax.dynamic_index_in_dim(segments, sequence, 0, keepdims=False)
        block_queries = lax.dynamic_slice_in_dim(seq_queries, offset, QBLOCK, 0)
        block_segments = lax.dynamic_slice_in_dim(seq_segments, offset, QBLOCK, 0)
        scores = (
            jnp.einsum("qhd,khd->hqk", block_queries, seq_keys, preferred_element_type=jnp.float32)
            * score_scale
        )
        same_doc = block_segments[:, None] == seq_segments[None, :]
        scores = jnp.where(same_doc[None], scores, NEG_FILL)
        highest = jnp.max(scores, axis=2, keepdims=True)
        weights = jnp.exp(scores - highest)
        totals = jnp.sum(weights, axis=2, keepdims=True)
        mixture = jnp.einsum(
            "hqk,khd->qhd",
            rounded(weights / totals),
            seq_values,
            preferred_element_type=jnp.float32,
        )
        return (mixture, (highest + jnp.log(totals))[:, :, 0])

    mixture, log_total = lax.map(attend_one_block, jnp.arange(SEQS * blocks))
    return (mixture.reshape(queries.shape), log_total)


def attend_backward(queries, key_rows, value_rows, segments, log_total, grad_mixed):
    score_scale = HEAD_DIM ** (-0.5)
    blocks = LEN // QBLOCK
    heads_here = queries.shape[1] // HEAD_DIM
    query_heads = split_heads(queries)
    key_heads = split_heads(key_rows)
    value_heads = split_heads(value_rows)
    grad_heads = split_heads(grad_mixed)
    lse_rows = log_total.reshape(SEQS, blocks, heads_here, QBLOCK)

    def one_sequence(sequence):
        seq_queries = lax.dynamic_index_in_dim(query_heads, sequence, 0, keepdims=False)
        seq_keys = lax.dynamic_index_in_dim(key_heads, sequence, 0, keepdims=False)
        seq_values = lax.dynamic_index_in_dim(value_heads, sequence, 0, keepdims=False)
        seq_grads = lax.dynamic_index_in_dim(grad_heads, sequence, 0, keepdims=False)
        seq_segments = lax.dynamic_index_in_dim(segments, sequence, 0, keepdims=False)
        seq_lse = lax.dynamic_index_in_dim(lse_rows, sequence, 0, keepdims=False)

        def one_one_block(carry, block_index):
            offset = block_index * QBLOCK
            block_queries = lax.dynamic_slice_in_dim(seq_queries, offset, QBLOCK, 0)
            block_grads = lax.dynamic_slice_in_dim(seq_grads, offset, QBLOCK, 0)
            block_segments = lax.dynamic_slice_in_dim(seq_segments, offset, QBLOCK, 0)
            block_lse = lax.dynamic_index_in_dim(seq_lse, block_index, 0, keepdims=False)
            scores = (
                jnp.einsum(
                    "qhd,khd->hqk", block_queries, seq_keys, preferred_element_type=jnp.float32
                )
                * score_scale
            )
            same_doc = block_segments[:, None] == seq_segments[None, :]
            scores = jnp.where(same_doc[None], scores, NEG_FILL)
            probs = jnp.exp(scores - block_lse[:, :, None])
            grad_probs = jnp.einsum(
                "qhd,khd->hqk", block_grads, seq_values, preferred_element_type=jnp.float32
            )
            grad_scores = rounded(
                probs * (grad_probs - jnp.sum(probs * grad_probs, axis=2, keepdims=True))
            )
            grad_query = (
                jnp.einsum(
                    "hqk,khd->qhd", grad_scores, seq_keys, preferred_element_type=jnp.float32
                )
                * score_scale
            )
            key_sum = (
                carry[0]
                + jnp.einsum(
                    "hqk,qhd->khd", grad_scores, block_queries, preferred_element_type=jnp.float32
                )
                * score_scale
            )
            value_sum = carry[1] + jnp.einsum(
                "hqk,qhd->khd", rounded(probs), block_grads, preferred_element_type=jnp.float32
            )
            return ((key_sum, value_sum), rounded(grad_query))

        zeros_init = jnp.zeros((LEN, heads_here, HEAD_DIM), jnp.float32)
        (key_sum, value_sum), grad_query = lax.scan(
            one_one_block, (zeros_init, zeros_init), jnp.arange(blocks)
        )
        return (grad_query.reshape(LEN, heads_here, HEAD_DIM), rounded(key_sum), rounded(value_sum))

    grad_query, grad_key, grad_value = lax.map(one_sequence, jnp.arange(SEQS))
    return (
        grad_query.reshape(queries.shape),
        grad_key.reshape(queries.shape),
        grad_value.reshape(queries.shape),
    )


def layer_forward(hidden, params, gathered, segments):
    query_w, key_w, value_w, inner_w, proj_w, outer_w, proj_cols = gathered
    whole_in = spread_features(hidden)
    queries = rounded(matmul(whole_in, query_w) + params[0])
    key_rows = rounded(matmul(whole_in, key_w))
    value_rows = rounded(matmul(whole_in, value_w) + params[1])
    mixture, log_total = attend_forward(queries, key_rows, value_rows, segments)
    attended = rounded(mixture)
    attn_branch = sum_partials(matmul(attended, proj_w)) + params[2]
    first_norm, normed_one, inverse_one = norm_forward(hidden + attn_branch, params[3], params[4])
    whole_mid = spread_features(first_norm)
    inner_act = matmul(whole_mid, inner_w) + params[5]
    active = rounded(exact_gelu(inner_act))
    ffn_branch = sum_partials(matmul(active, outer_w)) + params[6]
    output, normed_two, inverse_two = norm_forward(first_norm + ffn_branch, params[7], params[8])
    kept_values = (
        whole_in,
        queries,
        key_rows,
        value_rows,
        log_total,
        attended,
        normed_one,
        inverse_one,
        whole_mid,
        inner_act,
        active,
        normed_two,
        inverse_two,
    )
    return (output, kept_values)


def layer_backward(grad_output, kept_values, gathered, params, segments):
    (
        whole_in,
        queries,
        key_rows,
        value_rows,
        log_total,
        attended,
        normed_one,
        inverse_one,
        whole_mid,
        inner_act,
        active,
        normed_two,
        inverse_two,
    ) = kept_values
    query_w, key_w, value_w, inner_w, proj_w, outer_w, proj_cols = gathered
    grad_second, ffn_gain_sum, ffn_shift_sum = norm_backward(
        grad_output, normed_two, inverse_two, params[7]
    )
    ffn_low = rounded(grad_second)
    whole_second = spread_grads(ffn_low)
    outer_term = over_tokens(active, whole_second)
    active_grad = against(whole_second, outer_w)
    unused, pullback = jax.vjp(exact_gelu, inner_act)
    inner_low = rounded(pullback(active_grad)[0])
    inner_term = over_tokens(whole_mid, inner_low)
    grad_first = grad_second + sum_grad_partials(against(inner_low, inner_w))
    grad_attn, attn_gain_sum, attn_shift_sum = norm_backward(
        grad_first, normed_one, inverse_one, params[3]
    )
    attn_low = rounded(grad_attn)
    whole_attn = spread_grads(attn_low)
    proj_term = over_tokens(attended, whole_attn)
    mixed_grad = rounded(against(whole_attn, proj_w))
    query_low, key_low, value_low = attend_backward(
        queries, key_rows, value_rows, segments, log_total, mixed_grad
    )
    input_terms = (
        against(query_low, query_w) + against(key_low, key_w) + against(value_low, value_w)
    )
    grad_input = grad_attn + sum_grad_partials(input_terms)
    row_terms = (
        over_tokens(whole_in, query_low),
        over_tokens(whole_in, key_low),
        over_tokens(whole_in, value_low),
        inner_term,
    )
    col_terms = (proj_term, outer_term)
    small_terms = (
        token_sum(query_low),
        token_sum(value_low),
        token_sum(attn_low),
        attn_gain_sum,
        attn_shift_sum,
        token_sum(inner_low),
        token_sum(ffn_low),
        ffn_gain_sum,
        ffn_shift_sum,
    )
    return (grad_input, row_terms, col_terms, small_terms)


def general_device(
    hidden_in,
    query_weight,
    key_weight,
    value_weight,
    query_bias,
    value_bias,
    proj_weight,
    proj_bias,
    attn_gain,
    attn_shift,
    inner_weight,
    inner_bias,
    outer_weight,
    outer_bias,
    ffn_gain,
    ffn_shift,
    segment_ids,
    grad_out,
):
    shards = (query_weight, key_weight, value_weight, inner_weight, proj_weight, outer_weight)
    params = (
        query_bias,
        value_bias,
        proj_bias,
        attn_gain,
        attn_shift,
        inner_bias,
        outer_bias,
        ffn_gain,
        ffn_shift,
    )
    gathered = gather_weights(shards)
    start_in = hidden_in.astype(jnp.float32)
    middle, kept_one = layer_forward(start_in, params, gathered, segment_ids)
    final_out, kept_two = layer_forward(middle, params, gathered, segment_ids)
    kept = (kept_one, kept_two)
    grad_flow = grad_out.astype(jnp.float32)
    row_parts = []
    col_parts = []
    small_parts = []
    for layer_index in (1, 0):
        grad_flow, row_terms, col_terms, small_terms = layer_backward(
            grad_flow, kept[layer_index], gathered, params, segment_ids
        )
        row_parts.append(row_terms)
        col_parts.append(col_terms)
        small_parts.append(small_terms)
    row_sum = jax.tree.map(jnp.add, tuple(row_parts[0]), tuple(row_parts[1]))
    col_sum = jax.tree.map(jnp.add, tuple(col_parts[0]), tuple(col_parts[1]))
    small_sum = jax.tree.map(jnp.add, small_parts[0], small_parts[1])
    row_sum = (
        lax.psum_scatter(
            row_sum[0].astype(jnp.bfloat16), "row", scatter_dimension=0, tiled=True
        ).astype(jnp.float32),
        lax.psum_scatter(
            row_sum[1].astype(jnp.bfloat16), "row", scatter_dimension=0, tiled=True
        ).astype(jnp.float32),
        lax.psum_scatter(
            row_sum[2].astype(jnp.bfloat16), "row", scatter_dimension=0, tiled=True
        ).astype(jnp.float32),
        lax.psum_scatter(
            row_sum[3].astype(jnp.bfloat16), "row", scatter_dimension=0, tiled=True
        ).astype(jnp.float32),
    )
    col_sum = (
        lax.psum_scatter(
            col_sum[0].astype(jnp.bfloat16), "row", scatter_dimension=1, tiled=True
        ).astype(jnp.float32),
        lax.psum_scatter(
            col_sum[1].astype(jnp.bfloat16), "row", scatter_dimension=1, tiled=True
        ).astype(jnp.float32),
    )
    small_sum = lax.psum(
        (
            small_sum[0],
            small_sum[1],
            small_sum[2],
            small_sum[3],
            small_sum[4],
            small_sum[5],
            small_sum[6],
            small_sum[7],
            small_sum[8],
        ),
        "row",
    )
    return (
        final_out,
        grad_flow,
        row_sum[0],
        row_sum[1],
        row_sum[2],
        small_sum[0],
        small_sum[1],
        col_sum[0],
        small_sum[2],
        small_sum[3],
        small_sum[4],
        row_sum[3],
        small_sum[5],
        col_sum[1],
        small_sum[6],
        small_sum[7],
        small_sum[8],
    )


ANY = pl.BlockSpec(memory_space=pl.ANY)
VMEM = pl.BlockSpec(memory_space=pltpu.VMEM)
MESH = pl.DeviceIdType.MESH
DMA = pltpu.SemaphoreType.DMA
BF16 = jnp.bfloat16
F32 = jnp.float32


def place():
    row = lax.axis_index("row")
    depth = lax.axis_index("col")
    core = row % 2
    chip = row // 2
    x = chip % 2
    y = chip // 2
    return row, depth, core, chip, x, y


def remote(src, dst, send_sem, recv_sem, row, depth):
    return pltpu.make_async_remote_copy(
        src_ref=src,
        dst_ref=dst,
        send_sem=send_sem,
        recv_sem=recv_sem,
        device_id={"row": row, "col": depth},
        device_id_type=MESH,
    )


def slot_of(block, x, y):
    dx = (block % 2 - x) * (block % 2 - x)
    dy = (block // 2 - y) * (block // 2 - y)
    return 3 * dy + dx - 2 * dx * dy


def span(start, size):
    if isinstance(start, int):
        return pl.ds(start, size)
    return pl.ds(pl.multiple_of(start, 128), size)


def greet(row, depth, core, chip, x, y):
    barrier = pltpu.get_barrier_semaphore()
    mate = chip * 2 + (1 - core)
    friends = [(mate, depth)]
    for step in (1, 2, 3):
        friends.append((row, (depth + step) % 4))
        friends.append((mate, (depth + step) % 4))
    friends.append(((y * 2 + 1 - x) * 2 + core, depth))
    friends.append((((1 - y) * 2 + x) * 2 + core, depth))
    for r, d in friends:
        pl.semaphore_signal(
            barrier, inc=1, device_id={"row": r, "col": d}, device_id_type=MESH
        )
    pl.semaphore_wait(barrier, len(friends))


PIECES = 8
GROUPS = ((3,), (0,), (1,), (2,), (4,), (5,), (6,), (7,))


def gather_kernel(
    q_ref, k_ref, v_ref, proj_ref, inner_ref, outer_ref, small_ref, x_ref, g_ref,
    wqkv, wproj, winner, wouter, smalls, u_out, g_out,
    swap_s, swap_r, local_s, up_s, up_r, down_s, down_r, sm_s, sm_r,
    p1_s, p1_r, p2_s, p2_r, t_s, t_r, t_l, pair_s, pair_r,
):
    row, depth, core, chip, x, y = place()
    mate = chip * 2 + (1 - core)
    x_row = (y * 2 + 1 - x) * 2 + core
    y_row = ((1 - y) * 2 + x) * 2 + core
    greet(row, depth, core, chip, x, y)

    def swap_src(piece, half):
        if piece < 3:
            return (q_ref, k_ref, v_ref)[piece].at[:, span(half * 128, 128)]
        if piece == 3:
            return proj_ref.at[span(half * 128, 128), :]
        if piece < 6:
            return inner_ref.at[:, span(half * 512 + (piece - 4) * 256, 256)]
        return outer_ref.at[span(half * 512 + (piece - 6) * 256, 256), :]

    def cell(piece, start, size, origin):
        if piece < 3:
            return wqkv.at[span(start, size), span(piece * 512 + origin * 128, 128)]
        if piece == 3:
            return wproj.at[span(origin * 128, 128), span(start, size)]
        if piece < 6:
            return winner.at[
                span(start, size), span((piece - 4) * 1024 + origin * 256, 256)
            ]
        return wouter.at[span((piece - 6) * 1024 + origin * 256, 256), span(start, size)]

    def region(group, part, block):
        piece = GROUPS[group][0]
        if piece < 3:
            return wqkv.at[span(block * 256 + part * 128, 128), pl.ds(piece * 512, 512)]
        if piece == 3:
            return wproj.at[pl.ds(part * 256, 256), span(block * 256, 256)]
        if piece < 6:
            return winner.at[
                span(block * 256 + part * 128, 128), pl.ds((piece - 4) * 1024, 1024)
            ]
        return wouter.at[
            pl.ds((piece - 6) * 1024 + part * 512, 512), span(block * 256, 256)
        ]

    swaps, locals_ = [], []
    for piece in range(PIECES):
        target = cell(piece, core * 128, 128, depth)
        cp = remote(
            swap_src(piece, 1 - core), target, swap_s.at[piece], swap_r.at[piece], mate, depth
        )
        cp.start()
        swaps.append(cp)
        lc = pltpu.make_async_copy(swap_src(piece, core), target, local_s.at[piece])
        lc.start()
        locals_.append(lc)
    small_local = pltpu.make_async_copy(small_ref, smalls.at[depth], local_s.at[PIECES])
    small_local.start()

    def travel(piece, step, up):
        origin = depth - step if up else depth + step
        ref = cell(piece, 0, 256, origin)
        send, recv = (up_s, up_r) if up else (down_s, down_r)
        return remote(
            ref, ref, send.at[piece, step], recv.at[piece, step], row,
            depth + 1 if up else depth - 1,
        )

    def depth_step(group, step):
        for piece in GROUPS[group]:
            if step == 0:
                swaps[piece].wait_recv()
                locals_[piece].wait()
            for up in (True, False):
                inside = depth - step >= 0 if up else depth + step <= 3
                ready = inside & (depth < 3 if up else depth > 0)
                if step > 0:

                    @pl.when(inside)
                    def _():
                        origin = depth - step if up else depth + step
                        ref = cell(piece, 0, 256, origin)
                        recv = up_r if up else down_r
                        remote(
                            ref, ref, up_s.at[piece, step - 1], recv.at[piece, step - 1],
                            mate, depth,
                        ).wait_recv()

                if step < 3:

                    @pl.when(ready)
                    def _():
                        travel(piece, step, up).start()

    def depth_done():
        for piece in range(PIECES):
            for step in (0, 1, 2):
                for up in (True, False):
                    inside = depth - step >= 0 if up else depth + step <= 3

                    @pl.when(inside & (depth < 3 if up else depth > 0))
                    def _():
                        travel(piece, step, up).wait_send()

    def token_copies(index, src, dst):
        for j in range(4):
            to_core, to_depth = j % 2, core * 2 + j // 2
            mine = (to_core == core) & (to_depth == depth)
            source = src.at[pl.ds(j * 512, 512), :]
            target = dst.at[pl.ds(0, 512), span(slot_of(depth, x, y) * 256, 256)]

            @pl.when(mine)
            def _():
                pltpu.make_async_copy(source, target, t_l.at[index]).start()

            @pl.when(jnp.logical_not(mine))
            def _():
                remote(
                    source, target, t_s.at[index, j], t_r.at[index, depth],
                    chip * 2 + to_core, to_depth,
                ).start()

    def token_waits(index, src, dst):
        from_core = depth // 2
        for s in range(4):
            mine = (from_core == core) & (s == depth)
            target = dst.at[pl.ds(0, 512), span(slot_of(s, x, y) * 256, 256)]
            source = src.at[pl.ds(0, 512), :]

            @pl.when(mine)
            def _():
                pltpu.make_async_copy(source, target, t_l.at[index]).wait()

            @pl.when(jnp.logical_not(mine))
            def _():
                remote(
                    source, target, t_s.at[index, 0], t_r.at[index, s], mate, depth
                ).wait_recv()
        for j in range(4):
            to_core, to_depth = j % 2, core * 2 + j // 2
            mine = (to_core == core) & (to_depth == depth)

            @pl.when(jnp.logical_not(mine))
            def _():
                remote(
                    src.at[pl.ds(j * 512, 512), :], dst.at[pl.ds(0, 512), pl.ds(0, 256)],
                    t_s.at[index, j], t_r.at[index, 0], mate, depth,
                ).wait_send()

    first, second = {}, {}

    def start_first(group):
        for part, target, to in ((0, x_row, 1), (1, y_row, 3)):
            cp = remote(
                region(group, part, 0), region(group, part, to),
                p1_s.at[group, part], p1_r.at[group, part], target, depth,
            )
            cp.start()
            first[group, part] = cp

    def start_second(group):
        for part, target, moves in (
            (0, y_row, ((0, 3), (1, 2))), (1, x_row, ((0, 1), (3, 2))),
        ):
            first[group, part].wait_recv()
            for i, (origin, to) in enumerate(moves):
                cp = remote(
                    region(group, part, origin), region(group, part, to),
                    p2_s.at[group, part, i], p2_r.at[group, part, i], target, depth,
                )
                cp.start()
                second[group, part, i] = cp

    count = len(GROUPS)
    small_copies = []
    for tick in range(count + 4):
        for step in (0, 1, 2, 3):
            group = tick - step
            if 0 <= group < count:
                depth_step(group, step)
                if step == 3:
                    start_first(group)
        if 0 <= tick - 4 < count:
            start_second(tick - 4)
        if tick == TOKEN_TICK:
            token_copies(0, x_ref, u_out)
        if tick == count + 1:
            for k in (1, 2, 3):
                cp = remote(
                    small_ref, smalls.at[depth], sm_s.at[k - 1], sm_r.at[k - 1],
                    row, (depth + k) % 4,
                )
                cp.start()
                small_copies.append(cp)
            token_copies(1, g_ref, g_out)
    token_waits(0, x_ref, u_out)
    pair = remote(
        u_out.at[pl.ds(0, 512), :], u_out.at[pl.ds(512, 512), :], pair_s, pair_r, mate, depth
    )
    pair.start()
    token_waits(1, g_ref, g_out)
    pair.wait()
    for cp in small_copies:
        cp.wait()
    small_local.wait()
    depth_done()
    for cp in second.values():
        cp.wait()
    for cp in first.values():
        cp.wait_send()
    for cp in swaps:
        cp.wait_send()


TOKEN_TICK = 8


def gather_all(q, k, v, proj, inner, outer, small, x_rolled, g_rolled):
    sd = jax.ShapeDtypeStruct
    n = len(GROUPS)
    return pl.pallas_call(
        gather_kernel,
        out_shape=(
            sd((1024, 1536), BF16),
            sd((512, 1024), BF16),
            sd((1024, 2048), BF16),
            sd((2048, 1024), BF16),
            sd((4,) + small.shape, F32),
            sd((1024, 1024), BF16),
            sd((512, 1024), BF16),
        ),
        in_specs=[VMEM] * 7 + [ANY] * 2,
        out_specs=[ANY] * 7,
        scratch_shapes=[
            DMA((PIECES,)), DMA((PIECES,)), DMA((PIECES + 1,)),
            DMA((PIECES, 3)), DMA((PIECES, 3)), DMA((PIECES, 3)), DMA((PIECES, 3)),
            DMA((3,)), DMA((3,)),
            DMA((n, 2)), DMA((n, 2)), DMA((n, 2, 2)), DMA((n, 2, 2)),
            DMA((2, 4)), DMA((2, 4)), DMA((2,)), DMA, DMA,
        ],
        compiler_params=pltpu.CompilerParams(collective_id=1, has_side_effects=True),
    )(q, k, v, proj, inner, outer, small, x_rolled, g_rolled)


SHAPES = ((256, 256), (128, 512), (128, 512), (128, 512))
UNITS = ((128, 256), (256, 128), (256, 128), (256, 128))
FULLS = ((512, 256), (256, 512), (256, 512), (256, 512))
OUTS = ((256, 128), (128, 256), (128, 256), (128, 256), (128, 1024), (1024, 128))
HALVES = ((128, 128), (128, 128), (128, 128), (128, 128), (128, 512), (512, 128))
BY_COLS = (True, False, False, False)
INNER, OUTER = 4, 5


def add_rows(dst, terms):
    rows = dst.shape[0]
    step = 32

    def body(i, carry):
        sl = pl.ds(pl.multiple_of(i * step, step), step)
        total = terms[0][sl, :].astype(F32)
        for term in terms[1:]:
            total = total + term[sl, :].astype(F32)
        dst[sl, :] = total.astype(dst.dtype)
        return carry

    lax.fori_loop(0, rows // step, body, 0)


def scatter_kernel(*refs):
    grads = refs[0:4]
    inner_ref, outer_ref, small_ref, gi_ref = refs[4:8]
    outs = refs[8:14]
    small_out, gi_out = refs[14:16]
    rest = list(refs[16:])
    own = [[rest.pop(0) for _ in range(2)] for _ in range(4)]
    got1 = [[rest.pop(0) for _ in range(2)] for _ in range(4)]
    got2 = [[rest.pop(0) for _ in range(2)] for _ in range(4)]
    full = [rest.pop(0) for _ in range(4)]
    zgot = [rest.pop(0) for _ in range(4)]
    fin = [rest.pop(0) for _ in range(4)]
    cgot = [rest.pop(0) for _ in range(6)]
    sb = rest.pop(0)
    sg = rest.pop(0)
    (o_s, p1_s, p1_r, p2_s, p2_r, z_s, z_r, c_s, c_r, sm_s, sm_r, t_s, t_r, t_l) = rest

    row, depth, core, chip, x, y = place()
    mate = chip * 2 + (1 - core)
    x_row = (y * 2 + 1 - x) * 2 + core
    y_row = ((1 - y) * 2 + x) * 2 + core
    greet(row, depth, core, chip, x, y)

    def region(group, part, block):
        rows = SHAPES[group][0]
        if BY_COLS[group]:
            return grads[group].at[pl.ds(part * rows, rows), span(block * 256, 256)]
        return grads[group].at[span(block * 256 + part * 128, 128), :]

    def unit(group, z):
        if BY_COLS[group]:
            return full[group].at[span(z * UNITS[group][0], UNITS[group][0]), :]
        return full[group].at[:, span(z * UNITS[group][1], UNITS[group][1])]

    def side(group, half):
        if group == OUTER:
            return outer_ref.at[:, span(half * 128, 128)]
        if group == INNER:
            return inner_ref.at[span(half * 128, 128), :]
        if BY_COLS[group]:
            return fin[group].at[:, span(half * 128, 128)]
        return fin[group].at[span(half * 128, 128), :]

    def out_side(group, half):
        if group == OUTER:
            return outs[5].at[span(half * 512, 512), :]
        if group == INNER:
            return outs[4].at[:, span(half * 512, 512)]
        size = HALVES[group]
        if BY_COLS[group]:
            return outs[group].at[span(half * size[0], size[0]), :]
        return outs[group].at[:, span(half * size[1], size[1])]

    copies = {}

    def start_first(group):
        for part in (0, 1):
            target = y_row if part == 0 else x_row
            for i in (0, 1):
                kept = ((0, 1), (0, 3))[part][i]
                sent = ((3, 2), (1, 2))[part][i]
                lc = pltpu.make_async_copy(
                    region(group, part, kept), own[group][part].at[i], o_s.at[group, part, i]
                )
                lc.start()
                cp = remote(
                    region(group, part, sent), got1[group][part].at[i],
                    p1_s.at[group, part, i], p1_r.at[group, part, i], target, depth,
                )
                cp.start()
                copies["o", group, part, i] = lc
                copies["p1", group, part, i] = cp

    def start_second(group):
        for part in (0, 1):
            target = x_row if part == 0 else y_row
            for i in (0, 1):
                copies["o", group, part, i].wait()
                copies["p1", group, part, i].wait_recv()
            other = own[group][part].at[1]
            add_rows(other, (other, got1[group][part].at[1]))
            cp = remote(
                other, got2[group][part], p2_s.at[group, part], p2_r.at[group, part], target, depth
            )
            cp.start()
            copies["p2", group, part] = cp

    def send_depth(group):
        for k in (1, 2, 3):
            cp = remote(
                unit(group, (depth + k) % 4), zgot[group].at[k - 1],
                z_s.at[group, k - 1], z_r.at[group, k - 1], row, (depth + k) % 4,
            )
            cp.start()
            copies["z", group, k] = cp

    def start_depth(group):
        rows = SHAPES[group][0]
        for part in (0, 1):
            copies["p2", group, part].wait_recv()
            add_rows(
                full[group].at[pl.ds(part * rows, rows), :],
                (own[group][part].at[0], got1[group][part].at[0], got2[group][part]),
            )
        send_depth(group)

    def send_core(group):
        cp = remote(
            side(group, 1 - core), cgot[group], c_s.at[group], c_r.at[group], mate, depth
        )
        cp.start()
        copies["c", group] = cp

    def start_core(group):
        for k in (1, 2, 3):
            copies["z", group, k].wait_recv()
        add_rows(
            fin[group],
            (unit(group, depth), zgot[group].at[0], zgot[group].at[1], zgot[group].at[2]),
        )
        send_core(group)

    def finish(group):
        add_rows(out_side(group, core), (side(group, core),))
        copies["c", group].wait_recv()
        add_rows(out_side(group, 1 - core), (cgot[group],))

    def token_copies(index, src, dst):
        j = (depth % 2) * 2 + core
        to_core = depth // 2
        for z in range(4):
            mine = (to_core == core) & (z == depth)
            source = src.at[:, span(slot_of(z, x, y) * 256, 256)]
            target = dst.at[span(j * 512, 512), :]

            @pl.when(mine)
            def _():
                pltpu.make_async_copy(source, target, t_l.at[index]).start()

            @pl.when(jnp.logical_not(mine))
            def _():
                remote(
                    source, target, t_s.at[index, z], t_r.at[index, j], chip * 2 + to_core, z
                ).start()

    def token_waits(index, src, dst):
        to_core = depth // 2
        for j in range(4):
            from_core, from_depth = j % 2, core * 2 + j // 2
            mine = (from_core == core) & (from_depth == depth)
            target = dst.at[pl.ds(j * 512, 512), :]
            source = src.at[:, pl.ds(0, 256)]

            @pl.when(mine)
            def _():
                pltpu.make_async_copy(source, target, t_l.at[index]).wait()

            @pl.when(jnp.logical_not(mine))
            def _():
                remote(
                    source, target, t_s.at[index, 0], t_r.at[index, j], mate, depth
                ).wait_recv()
        for z in range(4):
            mine = (to_core == core) & (z == depth)

            @pl.when(jnp.logical_not(mine))
            def _():
                remote(
                    src.at[:, pl.ds(z * 256, 256)], dst.at[pl.ds(0, 512), :],
                    t_s.at[index, z], t_r.at[index, 0], mate, depth,
                ).wait_send()

    def small_send(step, slot, target_row, target_depth):
        cp = remote(
            sb.at[step], sg.at[slot], sm_s.at[slot], sm_r.at[slot], target_row, target_depth
        )
        cp.start()
        copies["s", slot] = cp

    def small_add(step, slot):
        copies["s", slot].wait_recv()
        sb[step + 1] = sb[step] + sg[slot]

    sb[0] = small_ref[...]
    token_copies(0, gi_ref, gi_out)
    for group in range(2):
        start_first(group)
    small_send(0, 0, mate, depth)
    send_core(OUTER)
    send_core(INNER)
    small_add(0, 0)
    small_send(1, 1, x_row, depth)
    finish(OUTER)
    finish(INNER)
    for group in range(4):
        start_second(group)
        if group + 2 < 4:
            start_first(group + 2)
        if group == 0:
            small_add(1, 1)
            small_send(2, 2, y_row, depth)
        if group > 0:
            start_depth(group - 1)
    small_add(2, 2)
    for k in (1, 2, 3):
        small_send(3, 2 + k, row, (depth + k) % 4)
    start_depth(3)
    for group in (0, 1, 2):
        start_core(group)
    for k in (1, 2, 3):
        copies["s", 2 + k].wait_recv()
    small_out[...] = ((sb[3] + sg[3]) + sg[4]) + sg[5]
    for group in (0, 1, 2):
        finish(group)
    start_core(3)
    token_waits(0, gi_ref, gi_out)
    finish(3)
    for key, cp in copies.items():
        if key[0] != "o":
            cp.wait_send()


def scatter_all(proj, q, k, v, inner, outer, small, gi):
    sd = jax.ShapeDtypeStruct
    scratch = []
    for size in SHAPES:
        scratch += [pltpu.VMEM((2,) + size, BF16)] * 2
    for size in SHAPES:
        scratch += [pltpu.VMEM((2,) + size, BF16)] * 2
    for size in SHAPES:
        scratch += [pltpu.VMEM(size, BF16)] * 2
    scratch += [pltpu.VMEM(size, BF16) for size in FULLS]
    scratch += [pltpu.VMEM((3,) + size, BF16) for size in UNITS]
    scratch += [pltpu.VMEM(size, BF16) for size in UNITS]
    scratch += [pltpu.VMEM(size, BF16) for size in HALVES]
    scratch += [pltpu.VMEM((4,) + small.shape, F32), pltpu.VMEM((6,) + small.shape, F32)]
    scratch += [
        DMA((4, 2, 2)), DMA((4, 2, 2)), DMA((4, 2, 2)), DMA((4, 2)), DMA((4, 2)),
        DMA((4, 3)), DMA((4, 3)), DMA((6,)), DMA((6,)), DMA((6,)), DMA((6,)),
        DMA((1, 4)), DMA((1, 4)), DMA((1,)),
    ]
    return pl.pallas_call(
        scatter_kernel,
        out_shape=tuple(sd(size, F32) for size in OUTS)
        + (sd(small.shape, F32), sd((2048, 256), BF16)),
        in_specs=[ANY] * 4 + [VMEM] * 3 + [ANY],
        out_specs=[VMEM] * 7 + [ANY],
        scratch_shapes=scratch,
        compiler_params=pltpu.CompilerParams(
            collective_id=2, has_side_effects=True, vmem_limit_bytes=48 * 1024 * 1024
        ),
    )(proj, q, k, v, inner, outer, small, gi)


def attend_kernel(flag_ref, q_ref, k_ref, v_ref, idq_ref, idk_ref, o_ref, lse_ref):
    rows = q_ref.shape[0]
    lane = lax.broadcasted_iota(jnp.int32, (1, 128), 1)
    low_half = lane < HEAD_DIM

    def compute(masked):
        keys = k_ref[...]
        values = v_ref[...]
        halves = (low_half, jnp.logical_not(low_half))
        sub = 256
        units = [(i, h) for i in range(rows // sub) for h in (0, 1)]

        def score(unit):
            i, h = unit
            scaled = q_ref[i * sub : (i + 1) * sub, :] * jnp.asarray(HEAD_DIM**-0.5, BF16)
            s = against(jnp.where(halves[h], scaled, jnp.zeros_like(scaled)), keys)
            if masked:
                s = jnp.where(idq_ref[i * sub : (i + 1) * sub, :] == idk_ref[...], s, NEG_FILL)
            return s

        def soft(s):
            top = jnp.max(s, axis=1, keepdims=True)
            weights = jnp.exp(s - top)
            return weights.astype(BF16), jnp.sum(weights, axis=1, keepdims=True), top

        skew = 1
        pending = [score(u) for u in units[:skew]]
        done = {}
        for n, unit in enumerate(units):
            if n + skew < len(units):
                pending.append(score(units[n + skew]))
            low, total, top = soft(pending.pop(0))
            mixed = matmul(low, values)
            done[unit] = (mixed / total, top + jnp.log(total))
            i, h = unit
            if h == 1:
                sl = slice(i * sub, (i + 1) * sub)
                a, b = done[i, 0], done[i, 1]
                o_ref[sl, :] = jnp.where(low_half, a[0], b[0]).astype(o_ref.dtype)
                lse_ref[sl, :] = jnp.where(low_half, a[1], b[1])

    @pl.when(flag_ref[0] == 1)
    def _():
        compute(False)

    @pl.when(flag_ref[0] != 1)
    def _():
        compute(True)


def attend(flag, qkv, id_col, id_row):
    tokens, width = qkv.shape[0], qkv.shape[1] // 3
    pairs = width // 128
    block = tokens
    return pl.pallas_call(
        attend_kernel,
        out_shape=(
            jax.ShapeDtypeStruct((tokens, width), BF16),
            jax.ShapeDtypeStruct((tokens, width), F32),
        ),
        grid_spec=pltpu.PrefetchScalarGridSpec(
            num_scalar_prefetch=1,
            grid=(width // 128, tokens // block),
            in_specs=[
                pl.BlockSpec((block, 128), lambda h, i, f: (i, h)),
                pl.BlockSpec((tokens, 128), lambda h, i, f: (0, h + pairs)),
                pl.BlockSpec((tokens, 128), lambda h, i, f: (0, h + 2 * pairs)),
                pl.BlockSpec((block, 1), lambda h, i, f: (i, 0)),
                pl.BlockSpec((1, tokens), lambda h, i, f: (0, 0)),
            ],
            out_specs=[
                pl.BlockSpec((block, 128), lambda h, i, f: (i, h)),
                pl.BlockSpec((block, 128), lambda h, i, f: (i, h)),
            ],
        ),
        compiler_params=pltpu.CompilerParams(
            dimension_semantics=("arbitrary", "arbitrary"), vmem_limit_bytes=48 * 1024 * 1024
        ),
        cost_estimate=pl.CostEstimate(
            flops=20_000_000_000, bytes_accessed=8_000_000, transcendentals=0
        ),
        name="attend",
    )(flag, qkv, qkv, qkv, id_col, id_row)


def attend_back_kernel(
    flag_ref, q_ref, k_ref, v_ref, do_ref, lse_ref, idk_ref, idq_ref,
    dq_ref, dk_ref, dv_ref,
):
    rows = q_ref.shape[0]
    scale = HEAD_DIM**-0.5
    lane = lax.broadcasted_iota(jnp.int32, (1, 128), 1)
    low_half = lane < HEAD_DIM

    def compute(masked):
        queries = q_ref[...]
        scaled = queries * jnp.asarray(scale, BF16)
        keys = k_ref[...]
        values = v_ref[...]
        grads = do_ref[...]
        lse_t = lse_ref[...].T
        q_t, k_t, do_t = queries.T, keys.T, grads.T
        dqs, dks, dvs = [], [], []
        for head in (0, 1):
            here = low_half if head == 0 else jnp.logical_not(low_half)
            part = slice(head * HEAD_DIM, (head + 1) * HEAD_DIM)
            zero = jnp.zeros_like(keys)
            scores = against(jnp.where(here, keys, zero), scaled)
            if masked:
                scores = jnp.where(idk_ref[...] == idq_ref[...], scores, NEG_FILL)
            log_row = lse_t[head * HEAD_DIM : head * HEAD_DIM + 1, :]
            probs = jnp.exp(scores - log_row)
            grad_probs = against(jnp.where(here, values, zero), grads)
            moved = probs * grad_probs
            delta = jnp.sum(moved, axis=0, keepdims=True)
            grad_scores = (moved - probs * delta).astype(BF16)
            low = probs.astype(BF16)
            dvs.append(against(do_t[part], low))
            dks.append(matmul(grad_scores, queries))
            dqs.append(matmul(k_t[part], grad_scores))
        dv_ref[...] = jnp.concatenate(dvs, axis=0).T.astype(BF16)
        dk_ref[...] = (jnp.where(low_half, dks[0], dks[1]) * scale).astype(BF16)
        dq_ref[...] = (jnp.concatenate(dqs, axis=0) * scale).T.astype(BF16)

    @pl.when(flag_ref[0] == 1)
    def _():
        compute(False)

    @pl.when(flag_ref[0] != 1)
    def _():
        compute(True)


def attend_back(flag, qkv, do, lse, id_col, id_row, first=0, count=4):
    tokens, width = qkv.shape[0], qkv.shape[1] // 3
    pairs = width // 128
    block = tokens
    shape = jax.ShapeDtypeStruct((tokens, count * 128), BF16)
    rows = pl.BlockSpec((block, 128), lambda h, i, f: (i, h + first))
    return pl.pallas_call(
        attend_back_kernel,
        out_shape=(shape, shape, shape),
        grid_spec=pltpu.PrefetchScalarGridSpec(
            num_scalar_prefetch=1,
            grid=(count, tokens // block),
            in_specs=[
                rows,
                pl.BlockSpec((tokens, 128), lambda h, i, f: (0, h + first + pairs)),
                pl.BlockSpec((tokens, 128), lambda h, i, f: (0, h + first + 2 * pairs)),
                rows, rows,
                pl.BlockSpec((tokens, 1), lambda h, i, f: (0, 0)),
                pl.BlockSpec((1, block), lambda h, i, f: (0, i)),
            ],
            out_specs=[
                pl.BlockSpec((block, 128), lambda h, i, f: (i, h)),
                pl.BlockSpec((tokens, 128), lambda h, i, f: (0, h)),
                pl.BlockSpec((tokens, 128), lambda h, i, f: (0, h)),
            ],
        ),
        compiler_params=pltpu.CompilerParams(
            dimension_semantics=("arbitrary", "arbitrary"), vmem_limit_bytes=48 * 1024 * 1024
        ),
        cost_estimate=pl.CostEstimate(
            flops=10_000_000_000 * count, bytes_accessed=2_500_000 * count, transcendentals=0
        ),
        name="attend_back",
    )(flag, qkv, qkv, qkv, do, lse, id_col, id_row)


def gelu_pair(inner):
    size = jnp.abs(inner)
    bell = jnp.exp(inner * (inner * -0.5))
    t = 1.0 / (1.0 + (0.3275911 * 0.5**0.5) * size)
    poly = (0.5 * 1.061405429) * t - 0.5 * 1.453152027
    poly = poly * t + 0.5 * 1.421413741
    poly = poly * t - 0.5 * 0.284496736
    poly = poly * t + 0.5 * 0.254829592
    tail = (poly * t) * bell
    below = jnp.where(inner >= 0.0, 1.0 - tail, tail)
    return (inner * below).astype(BF16), (below + inner * (bell * 0.3989422804014327)).astype(BF16)


def ffn_in_kernel(x_ref, w_ref, b_ref, active_ref, slope_ref):
    rows, cols = active_ref.shape
    sub = 128
    skew = 1

    def open_unit(i):
        return matmul(x_ref[i * sub : (i + 1) * sub, :], w_ref[...]) + b_ref[...]

    count = rows // sub
    pending = [open_unit(i) for i in range(skew)]
    for i in range(count):
        if i + skew < count:
            pending.append(open_unit(i + skew))
        active, slope = gelu_pair(pending.pop(0))
        active_ref[i * sub : (i + 1) * sub, :] = active
        slope_ref[i * sub : (i + 1) * sub, :] = slope


def ffn_in(x, w, bias):
    tokens, depth = x.shape
    hidden = w.shape[1]
    rows, cols = 1024, 512
    shape = jax.ShapeDtypeStruct((tokens, hidden), BF16)
    out = pl.BlockSpec((rows, cols), lambda n, m: (m, n))
    return pl.pallas_call(
        ffn_in_kernel,
        out_shape=(shape, shape),
        grid=(hidden // cols, tokens // rows),
        in_specs=[
            pl.BlockSpec((rows, depth), lambda n, m: (m, 0)),
            pl.BlockSpec((depth, cols), lambda n, m: (0, n)),
            pl.BlockSpec((1, cols), lambda n, m: (0, n)),
        ],
        out_specs=[out, out],
        compiler_params=pltpu.CompilerParams(
            dimension_semantics=("arbitrary", "arbitrary"), vmem_limit_bytes=48 * 1024 * 1024
        ),
        cost_estimate=pl.CostEstimate(
            flops=14_000_000_000, bytes_accessed=14_000_000, transcendentals=0
        ),
        name="ffn_in",
    )(x, w, bias)


def exchange(values):
    pairs = [(r, r + 1 - 2 * (r % 2)) for r in range(8)]
    return lax.ppermute(values, "row", pairs)


def both(own):
    return jnp.concatenate([own, exchange(own)], axis=0)


def share_sum(left, weight, product, apart=False):
    mate_part, left_own = lax.optimization_barrier(
        (rounded(product(left[512:], weight)), left[:512])
    )
    own_part, other = product(left_own, weight), exchange(mate_part)
    if apart:
        own_part, other = lax.optimization_barrier((own_part, other))
    return own_part + other.astype(F32)


def norm_rows(summed, gain, shift):
    center = jnp.mean(summed, axis=1, keepdims=True)
    spread = jnp.mean(summed * summed, axis=1, keepdims=True) - center * center
    inverse = lax.rsqrt(spread + EPSILON)
    normed = (summed - center) * inverse
    return normed * gain + shift, normed, inverse


def norm_rows_back(grad_output, normed, inverse, gain):
    scaled = grad_output * gain
    mean_one = jnp.mean(scaled, axis=1, keepdims=True)
    mean_two = jnp.mean(scaled * normed, axis=1, keepdims=True)
    grad_input = inverse * (scaled - mean_one - normed * mean_two)
    return grad_input, token_sum(grad_output * normed), token_sum(grad_output)


def fast_forward(hidden, weights, vectors, ids, whole_in=None):
    wqkv, wproj, winner, wouter = weights
    flag, id_col, id_row = ids
    if whole_in is None:
        whole_in = both(rounded(hidden))
    qkv = rounded(matmul(whole_in, wqkv) + vectors["qkv"])
    attended, lse = attend(flag, qkv, id_col, id_row)
    branch = share_sum(attended, wproj, matmul, True) + vectors["proj"]
    first, normed_one, inverse_one = norm_rows(
        hidden + branch, vectors["attn_gain"], vectors["attn_shift"]
    )
    whole_mid = both(rounded(first))
    active, slope = ffn_in(whole_mid, winner, vectors["inner"])
    ffn = share_sum(active, wouter, matmul, True) + vectors["outer"]
    output, normed_two, inverse_two = norm_rows(
        first + ffn, vectors["ffn_gain"], vectors["ffn_shift"]
    )
    kept = (
        whole_in, qkv, lse, attended, normed_one, inverse_one,
        whole_mid, active, slope, normed_two, inverse_two,
    )
    return output, kept


def fast_backward(grad_output, kept, weights, vectors, ids, later=None, beside=None):
    (
        whole_in, qkv, lse, attended, normed_one, inverse_one,
        whole_mid, active, slope, normed_two, inverse_two,
    ) = kept
    wqkv, wproj, winner, wouter = weights
    flag, id_col, id_row = ids
    grad_second, ffn_gain_sum, ffn_shift_sum = norm_rows_back(
        grad_output, normed_two, inverse_two, vectors["ffn_gain"]
    )
    ffn_low = rounded(grad_second)
    whole_second = both(ffn_low)
    inner_low = rounded(against(whole_second, wouter) * slope.astype(F32))
    if later is None:
        outer_terms = rounded(over_tokens(active, whole_second))
    else:
        outer_terms = add_trees(outer_pieces(active, whole_second), outer_cuts(later[0]))
        outer_planes = [Plane(outer_terms, h, 1) for h in (0, 1)]
        outer_got = [p.step_one() for p in outer_planes]
    grad_first = grad_second + share_sum(inner_low, winner, against)
    inner_terms = rounded(add_later(over_tokens(whole_mid, inner_low), later, 1))
    if later is not None:
        inner_planes = [Plane(inner_cuts(inner_terms), h, 0) for h in (0, 1)]
        inner_got = [p.step_one() for p in inner_planes]
    grad_attn, attn_gain_sum, attn_shift_sum = norm_rows_back(
        grad_first, normed_one, inverse_one, vectors["attn_gain"]
    )
    attn_low = rounded(grad_attn)
    whole_attn = both(attn_low)
    mixed_grad = rounded(against(whole_attn, wproj))
    proj_term = over_tokens(attended, whole_attn)
    if later is None:
        grads = attend_back(flag, qkv, mixed_grad, lse, id_col, id_row)
        if beside is not None:
            beside, grads = lax.optimization_barrier((beside, grads))
        outer_terms, inner_terms = (outer_terms, inner_terms), beside
    else:
        early = attend_back(flag, qkv, mixed_grad, lse, id_col, id_row, 0, 2)
        outer_got, early = lax.optimization_barrier((outer_got, early))
        outer_hand = [p.to_hand(g) for p, g in zip(outer_planes, outer_got)]
        outer_hand, mixed_grad = lax.optimization_barrier((outer_hand, mixed_grad))
        outer_more = [p.step_two(v) for p, v in zip(outer_planes, outer_hand)]
        late = attend_back(flag, qkv, mixed_grad, lse, id_col, id_row, 2, 2)
        inner_got, late = lax.optimization_barrier((inner_got, late))
        inner_hand = [p.to_hand(g) for p, g in zip(inner_planes, inner_got)]
        inner_hand, outer_more, late = lax.optimization_barrier((inner_hand, outer_more, late))
        inner_more = [p.step_two(v) for p, v in zip(inner_planes, inner_hand)]
        outer_terms = fold_depth([p.close(m) for p, m in zip(outer_planes, outer_more)], 0)
        inner_terms = fold_depth([p.close(m) for p, m in zip(inner_planes, inner_more)], 1)
        grads = tuple(jnp.concatenate(pair, axis=1) for pair in zip(early, late))
    grad_qkv = jnp.concatenate(grads, axis=1)
    grad_input = grad_attn + share_sum(grad_qkv, wqkv, against)
    terms = (proj_term,) + tuple(
        over_tokens(whole_in, part) for part in grads
    )
    small = (
        token_sum(grads[0]), token_sum(grads[2]), token_sum(attn_low),
        attn_gain_sum, attn_shift_sum, token_sum(inner_low), token_sum(ffn_low),
        ffn_gain_sum, ffn_shift_sum,
    )
    return grad_input, terms, outer_terms, inner_terms, small


def flip_row(bit):
    return [(r, r + bit - 2 * bit * ((r // bit) % 2)) for r in range(8)]


CUTS = (((512, 1024), (256, 512), (0, 256)), ((256, 768), (768, 1024), (0, 256)))


def outer_pieces(active, relative):
    return [
        [over_tokens(active[:, h * 1024 : (h + 1) * 1024], relative[:, a:b]) for a, b in CUTS[h]]
        for h in (0, 1)
    ]


def add_trees(left, right):
    return jax.tree.map(lambda p, q: p + q.astype(F32), left, right)


def outer_cuts(whole):
    return [
        [whole[h * 1024 : (h + 1) * 1024, a:b] for a, b in CUTS[h]] for h in (0, 1)
    ]


def inner_cuts(whole):
    return [
        [whole[a:b, h * 1024 : (h + 1) * 1024] for a, b in CUTS[h]] for h in (0, 1)
    ]


def add_later(term, later, index):
    return term if later is None else term + later[index].astype(F32)


class Plane:
    def __init__(self, pieces, half, axis):
        sent, handed, own = pieces[half]
        self.sent = rounded(sent)
        self.handed, self.own = handed.astype(F32), own.astype(F32)
        self.half, self.axis = half, axis
        self.first, self.second = (4, 2) if half == 0 else (2, 4)

    def step_one(self):
        return lax.ppermute(self.sent, "row", flip_row(self.first))

    def to_hand(self, got):
        low, high = jnp.split(got, 2, axis=self.axis)
        self.got, handed = (high, low) if self.half == 0 else (low, high)
        return rounded(self.handed + handed.astype(F32))

    def step_two(self, handed):
        return lax.ppermute(handed, "row", flip_row(self.second))

    def close(self, more):
        return rounded(self.own + self.got.astype(F32) + more.astype(F32))


def fold_depth(halves, axis):
    depth = lax.axis_index("col")

    def unit(z):
        picked = [lax.dynamic_slice_in_dim(half, z * 256, 256, axis) for half in halves]
        return jnp.concatenate(picked, axis=axis)

    total = unit(depth).astype(F32)
    for k in (1, 2, 3):
        pairs = [(z, (z + k) % 4) for z in range(4)]
        total = total + lax.ppermute(unit((depth + k) % 4), "col", pairs).astype(F32)
    return rounded(total)


def spread_out(values):
    core = lax.axis_index("row") % 2
    depth = lax.axis_index("col")
    j = (depth % 2) * 2 + core
    x, y = place()[4:]
    parts = []
    for k in range(4):
        pairs = []
        for r in range(8):
            for z in range(4):
                block = ((z % 2) * 2 + r % 2 + k) % 4
                pairs.append((r * 4 + z, (r // 2 * 2 + z // 2) * 4 + block))
        piece = lax.dynamic_slice_in_dim(values, slot_of((j + k) % 4, x, y) * 256, 256, 1)
        parts.append(lax.ppermute(piece, ("row", "col"), pairs))
    return parts


def join_parts(parts, own_start):
    depth = lax.axis_index("col")
    cycle = jnp.concatenate(parts[::-1] * 2, axis=0)
    start = ((3 - depth) * 512 - own_start + 2048) % 2048
    return lax.dynamic_slice(cycle, (start, 0), (2048, 256)).astype(F32)


VECTORS = (
    ("q", 256), ("v", 256), ("proj", 256), ("attn_gain", 256), ("attn_shift", 256),
    ("inner", 1024), ("outer", 256), ("ffn_gain", 256), ("ffn_shift", 256),
)
SPLIT = ("q", "v", "inner")


def fast_device(
    hidden_in,
    query_weight,
    key_weight,
    value_weight,
    query_bias,
    value_bias,
    proj_weight,
    proj_bias,
    attn_gain,
    attn_shift,
    inner_weight,
    inner_bias,
    outer_weight,
    outer_bias,
    ffn_gain,
    ffn_shift,
    segment_ids,
    grad_out,
):
    core = lax.axis_index("row") % 2
    depth = lax.axis_index("col")
    own_ids = segment_ids[0]
    mate_ids = exchange(own_ids)

    def big_start(ids):
        found = ids[:1025] == ids[1023:]
        return jnp.sum(jnp.where(found, jnp.arange(1025, dtype=jnp.int32), 0))

    own_start = big_start(own_ids)
    ids = jnp.where(depth // 2 == core, own_ids, mate_ids)
    ids = lax.dynamic_slice(
        jnp.concatenate([ids, ids[:1024]]), (big_start(ids),), (2048,)
    ).reshape(2, 2, 512)
    ids = lax.dynamic_index_in_dim(ids, depth % 2, 0, keepdims=False)
    ids = jnp.where(core == 0, ids, ids[::-1]).reshape(1024)
    flag = (1 - depth % 2).reshape(1).astype(jnp.int32)
    ids = (flag, ids[:, None], ids[None, :])

    def turned(values):
        longer = jnp.concatenate([values, values[:1024]], axis=0)
        return lax.dynamic_slice(longer, (own_start, 0), (2048, 256))

    def turned_back(values):
        longer = jnp.concatenate([values[1024:], values], axis=0)
        return lax.dynamic_slice(longer, (1024 - own_start, 0), (2048, 256)).astype(F32)

    small = jnp.concatenate(
        [
            query_bias, value_bias, proj_bias, attn_gain, attn_shift,
            inner_bias, outer_bias, ffn_gain, ffn_shift,
        ]
    ).reshape(24, 128)
    wqkv, wproj, winner, wouter, smalls, start_low, grad_low = gather_all(
        query_weight, key_weight, value_weight, proj_weight, inner_weight, outer_weight,
        small, turned(hidden_in), turned(grad_out),
    )
    smalls = smalls.reshape(4, 3072)
    x, y = place()[4:]
    order = (y * 2 + x, y * 2 + 1 - x, (1 - y) * 2 + 1 - x, (1 - y) * 2 + x)
    placed = jnp.stack([lax.dynamic_index_in_dim(smalls, b, 0, keepdims=False) for b in order])
    weights = (wqkv, wproj, winner, wouter)
    vectors, offset = {}, 0
    for name, size in VECTORS:
        part = (smalls if name in SPLIT else placed)[:, offset : offset + size]
        offset += size
        if name in SPLIT:
            part = jnp.where(core == 0, part[:, : size // 2], part[:, size // 2 :])
        vectors[name] = part.reshape(1, -1)
    vectors["inner"] = (
        vectors["inner"].reshape(4, 2, 256).transpose(1, 0, 2).reshape(1, 2048)
    )
    vectors["qkv"] = jnp.concatenate(
        [vectors["q"], jnp.zeros_like(vectors["q"]), vectors["v"]], axis=1
    )

    middle, kept_one = fast_forward(
        start_low[:512].astype(F32), weights, vectors, ids, start_low
    )
    final_out, kept_two = fast_forward(middle, weights, vectors, ids)
    grad_flow = grad_low.astype(F32)
    parts = spread_out(rounded(final_out))
    grad_flow, terms_two, ffn_two, parts, small_two = fast_backward(
        grad_flow, kept_two, weights, vectors, ids, None, parts
    )
    hidden_out = join_parts(parts, own_start)
    grad_flow, terms_one, outer_full, inner_full, small_one = fast_backward(
        grad_flow, kept_one, weights, vectors, ids, ffn_two
    )
    terms = [rounded(a + b) for a, b in zip(terms_two, terms_one)]
    pieces = []
    for (name, size), a, b in zip(VECTORS, small_two, small_one):
        total = a + b
        if name not in SPLIT:
            blocks = total.reshape(4, 256)
            total = jnp.stack(
                [
                    lax.dynamic_index_in_dim(blocks, slot_of(n, x, y), 0, keepdims=False)
                    for n in range(4)
                ]
            )
        if name in SPLIT:
            half = total.reshape(4, 1, size // 2)
            if name == "inner":
                half = total.reshape(2, 4, 256).transpose(1, 0, 2).reshape(4, 1, 512)
            zero = jnp.zeros_like(half)
            total = jnp.where(
                core == 0,
                jnp.concatenate([half, zero], axis=1),
                jnp.concatenate([zero, half], axis=1),
            )
        pieces.append(total.reshape(-1))
    small_sum = jnp.concatenate(pieces).reshape(96, 128)
    results = scatter_all(*terms, inner_full, outer_full, small_sum, rounded(grad_flow))
    proj_g, q_g, k_g, v_g, inner_g, outer_g, small_all, grad_turned = results
    small_all = small_all.reshape(-1)
    sums, offset = {}, 0
    for name, size in VECTORS:
        sums[name] = lax.dynamic_slice(small_all, (offset + depth * size,), (size,))
        offset += 4 * size
    return (
        hidden_out,
        turned_back(grad_turned),
        q_g,
        k_g,
        v_g,
        sums["q"],
        sums["v"],
        proj_g,
        sums["proj"],
        sums["attn_gain"],
        sums["attn_shift"],
        inner_g,
        sums["inner"],
        outer_g,
        sums["outer"],
        sums["ffn_gain"],
        sums["ffn_shift"],
    )


def solution(mesh):
    in_specs = (
        P("row", "col"),
        P("row", "col"),
        P("row", "col"),
        P("row", "col"),
        P("col"),
        P("col"),
        P("col", "row"),
        P("col"),
        P("col"),
        P("col"),
        P("row", "col"),
        P("col"),
        P("col", "row"),
        P("col"),
        P("col"),
        P("col"),
        P("row", None),
        P("row", "col"),
    )
    out_specs = (
        P("row", "col"),
        P("row", "col"),
        P("row", "col"),
        P("row", "col"),
        P("row", "col"),
        P("col"),
        P("col"),
        P("col", "row"),
        P("col"),
        P("col"),
        P("col"),
        P("row", "col"),
        P("col"),
        P("col", "row"),
        P("col"),
        P("col"),
        P("col"),
    )
    same = dict(mesh.shape) == {"row": 8, "col": 4}
    return jax.shard_map(
        fast_device if same else general_device, mesh=mesh, in_specs=in_specs, out_specs=out_specs, check_vma=False
    )
```
